32 devices in a mesh: groups: 2 (over x), seq: 16 (over z, y, core).
Axes of the slice: x: 2, y: 2, z: 4, core: 2. Of those that a mesh axis runs over, the one named last changes fastest.
Arguments:
- prompt_query: bfloat16 [4096, 4096], P(('groups', 'seq')), parts along dimension 0, may hold values from -16 to 16
- prompt_key: bfloat16 [4096, 4096], P(('groups', 'seq')), parts along dimension 0, may hold values from -16 to 16
- prompt_value: bfloat16 [4096, 4096], P(('groups', 'seq')), parts along dimension 0, may hold values from -6 to 6
- response_embed: bfloat16 [1024, 4096], P('groups'), parts along dimension 0, may hold values from -32 to 32
- mask_embed: bfloat16 [4096], replicated, may hold values from -6 to 6
- commit_step: int32 [1024], P('groups'), parts along dimension 0, may hold values from 1 to 4
- block_index: int32 [2], P('groups'), parts along dimension 0, may hold values from 0 to 7
- attention_gain: bfloat16 [4096], replicated, may hold values from 0.099609375 to 1.8984375
- residual_gain: bfloat16 [4096], replicated, may hold values from 0.099609375 to 1.8984375
- query_weight: bfloat16 [4096, 4096], P(None, 'seq'), may hold values from -0.125 to 0.125
- key_weight: bfloat16 [4096, 4096], P(None, 'seq'), may hold values from -0.09375 to 0.09375
- value_weight: bfloat16 [4096, 4096], P(None, 'seq'), may hold values from -1.5 to 1.5
- output_weight: bfloat16 [4096, 4096], P('seq'), may hold values from -0.09375 to 0.09375
Outputs:
- prompt_context: bfloat16 [4096, 4096], P(('groups', 'seq')), parts along dimension 0
- response_residual: bfloat16 [4, 1024, 4096], P(None, ('groups', 'seq')), parts along dimension 1
- response_normed: bfloat16 [4, 1024, 4096], P(None, ('groups', 'seq')), parts along dimension 1
The draws below stay inside these ranges and needn't reach their ends.
There are 2 independent parts, one for each index of `groups`. The reference program is written for one: setup_inputs(seed, part) draws one part's arguments, and reference() takes and returns one part's arrays. A program takes and returns all parts, laid end to end along the dimension named above; an argument that names none is the same for every part. Nothing has to cross between parts.
All inputs are finite; a program needn't handle non-finite values.
Results may differ from the reference program's by a relative error of at most 0.018.
Values may be sent and summed in bfloat16 or wider, within the bound.
No kernel may reach another device: no remote copies, remote signals or barrier semaphores. Data moves between devices by JAX's collectives and lax.ppermute only.
A program may use at most 128 MiB of HBM per device.

```python
import math
import jax
import jax.numpy as jnp
from jax import lax

D = 4096
HEADS = 32
HD = 128
RESP = 512
STEPS = 4
BLOCKS = 8
PROMPT = 2048


def draw_prompt_query(key, part):
    values = jnp.clip(jax.random.normal(jax.random.fold_in(key, 11), (PROMPT, HEADS * HD), jnp.float32), -4.0, 4.0) * 1.6
    return values.astype(jnp.bfloat16)


def draw_prompt_key(key, part):
    values = jnp.clip(jax.random.normal(jax.random.fold_in(key, 13), (PROMPT, HEADS * HD), jnp.float32), -4.0, 4.0) * 1.6
    return values.astype(jnp.bfloat16)


def draw_response_embed(key, part):
    row_scale = jnp.exp(jax.random.uniform(jax.random.fold_in(key, 21), (RESP, 1), jnp.float32, minval=-1.15, maxval=1.15))
    col_scale = jnp.exp(jax.random.uniform(jax.random.fold_in(key, 22), (1, D), jnp.float32, minval=-0.8, maxval=0.8))
    core = jnp.clip(jax.random.normal(jax.random.fold_in(key, 23), (RESP, D), jnp.float32), -4.0, 4.0)
    return (core * row_scale * col_scale).astype(jnp.bfloat16)


def place_ends(values, own_key, low, top_value):
    dims = values.shape
    spot = [jax.random.randint(jax.random.fold_in(own_key, axis), (), 0, dims[axis]) for axis in range(len(dims))]
    values = values.at[tuple(spot)].set(low)
    longest = dims.index(max(dims))
    spot[longest] = (spot[longest] + 1) % dims[longest]
    return values.at[tuple(spot)].set(top_value)


def level_of(own_key, extent, pieces, smallest, top_value):
    factor_of = 1.0
    for position, shards_of in pieces:
        heights = jax.random.uniform(jax.random.fold_in(jax.random.fold_in(own_key, 6), position), (shards_of,), jnp.float32, smallest / len(pieces), top_value / len(pieces))
        factor_of = factor_of * jnp.repeat(jnp.exp(heights), extent[position] // shards_of).reshape((-1,) + (1,) * (len(extent) - 1 - position))
    return factor_of


def bell_draw(own_key, dims, scale, bound, pieces=(), kind=jnp.bfloat16):
    values = scale * jax.random.normal(own_key, dims, jnp.float32)
    if pieces:
        values = values * level_of(own_key, dims, pieces, -0.22, 0.18)
    return jnp.clip(values, -bound, bound).astype(kind)


def setup_inputs(seed: int = 0, part: int = 0) -> dict:
    arg_keys = jax.random.split(jax.random.key(seed), 14)
    part_keys = jax.random.split(jax.random.fold_in(arg_keys[13], part), 14)
    return {
        "prompt_query": draw_prompt_query(jax.random.fold_in(jax.random.fold_in(arg_keys[13], part), 71), part),
        "prompt_key": draw_prompt_key(jax.random.fold_in(jax.random.fold_in(arg_keys[13], part), 71), part),
        "prompt_value": bell_draw(part_keys[2], (PROMPT, HEADS * HD), 1.0, 6.0, ((0, 16),)),
        "response_embed": draw_response_embed(jax.random.fold_in(jax.random.fold_in(arg_keys[13], part), 71), part),
        "mask_embed": bell_draw(arg_keys[4], (D,), 1.0, 6.0),
        "commit_step": place_ends(jax.random.randint(part_keys[5], (RESP,), 1, STEPS + 1), jax.random.fold_in(part_keys[5], 1), 1, STEPS).astype(jnp.int32),
        "block_index": jax.random.randint(part_keys[6], (1,), 0, BLOCKS).astype(jnp.int32),
        "attention_gain": jnp.clip(1.0 + 0.18 * jax.random.normal(arg_keys[7], (D,), jnp.float32), 0.099609375, 1.8984375).astype(jnp.bfloat16),
        "residual_gain": jnp.clip(1.0 + 0.18 * jax.random.normal(arg_keys[8], (D,), jnp.float32), 0.099609375, 1.8984375).astype(jnp.bfloat16),
        "query_weight": bell_draw(arg_keys[9], (D, HEADS * HD), (D // 2) ** -0.5, 0.125, ((1, 16),)),
        "key_weight": bell_draw(arg_keys[10], (D, HEADS * HD), D ** -0.5, 0.09375, ((1, 16),)),
        "value_weight": bell_draw(arg_keys[11], (D, HEADS * HD), (max(1, D // 256)) ** -0.5, 1.5, ((1, 16),)),
        "output_weight": bell_draw(arg_keys[12], (HEADS * HD, D), (HEADS * HD) ** -0.5, 0.09375, ((0, 16),)),
    }


rope_base = 500000.0
norm_eps = 1e-05

def rotary(vectors, positions):
    half_size = vectors.shape[-1] // 2
    exponent = jnp.arange(half_size, dtype=jnp.float32) * (2.0 / vectors.shape[-1])
    inv_freq = rope_base ** (-exponent)
    angles = positions.astype(jnp.float32)[:, None] * inv_freq[None, :]
    cosine = jnp.cos(angles)[:, None, :]
    sine_part = jnp.sin(angles)[:, None, :]
    first_half = vectors[..., :half_size]
    second = vectors[..., half_size:]
    return jnp.concatenate([first_half * cosine - second * sine_part, second * cosine + first_half * sine_part], axis=-1)

def rms_scale(row_values, gain_row):
    return row_values * lax.rsqrt(lax.optimization_barrier(jnp.mean(row_values * row_values, axis=-1, keepdims=True)) + norm_eps) * gain_row.astype(jnp.float32)

def attend_one(queries, all_keys, all_values):
    score_scale = 1.0 / math.sqrt(queries.shape[-1])
    scores = jnp.dot(queries, all_keys.T, preferred_element_type=jnp.float32) * score_scale
    row_max = lax.optimization_barrier(jnp.max(scores, axis=-1, keepdims=True))
    weights = jnp.exp(scores - row_max)
    row_total = lax.optimization_barrier(jnp.sum(weights, axis=-1))
    weighted = jnp.dot(weights.astype(jnp.bfloat16), all_values, preferred_element_type=jnp.float32)
    return (weighted / row_total[:, None]).astype(jnp.bfloat16)

def attend_heads(queries, all_keys, all_values):
    head_q = jnp.transpose(queries, (1, 0, 2))
    head_k = jnp.transpose(all_keys, (1, 0, 2))
    head_v = jnp.transpose(all_values, (1, 0, 2))
    result = lax.map(lambda trio: attend_one(trio[0], trio[1], trio[2]), (head_q, head_k, head_v))
    return jnp.transpose(result, (1, 0, 2))

def reference(prompt_query, prompt_key, prompt_value, response_embed, mask_embed, commit_step, block_index, attention_gain, residual_gain, query_weight, key_weight, value_weight, output_weight):
    prompt_len = prompt_query.shape[0]
    resp_len = response_embed.shape[0]
    prompt_pos = jnp.arange(prompt_len, dtype=jnp.int32)
    resp_pos = (prompt_len + block_index[0] * resp_len + jnp.arange(resp_len, dtype=jnp.int32)).astype(jnp.int32)
    rot_query = rotary(prompt_query.astype(jnp.float32).reshape(prompt_len, HEADS, HD), prompt_pos).astype(jnp.bfloat16)
    rot_key = rotary(prompt_key.astype(jnp.float32).reshape(prompt_len, HEADS, HD), prompt_pos).astype(jnp.bfloat16)
    plain_value = prompt_value.reshape(prompt_len, HEADS, HD)
    residuals = []
    normed_rows = []
    prompt_out = None
    for step_index in range(STEPS):
        shown = (commit_step <= step_index)[:, None]
        step_input = jnp.where(shown, response_embed, mask_embed[None, :])
        input_f32 = step_input.astype(jnp.float32)
        normed_in = rms_scale(input_f32, attention_gain).astype(jnp.bfloat16)
        resp_query = rotary(jnp.dot(normed_in, query_weight, preferred_element_type=jnp.float32).reshape(resp_len, HEADS, HD), resp_pos).astype(jnp.bfloat16)
        resp_key = rotary(jnp.dot(normed_in, key_weight, preferred_element_type=jnp.float32).reshape(resp_len, HEADS, HD), resp_pos).astype(jnp.bfloat16)
        resp_value = jnp.dot(normed_in, value_weight, preferred_element_type=jnp.float32).astype(jnp.bfloat16).reshape(resp_len, HEADS, HD)
        all_keys = jnp.concatenate([rot_key, resp_key], axis=0)
        all_values = jnp.concatenate([plain_value, resp_value], axis=0)
        if step_index == 0:
            prompt_out = attend_heads(rot_query, all_keys, all_values).reshape(prompt_len, HEADS * HD)
        context = attend_heads(resp_query, all_keys, all_values).reshape(resp_len, HEADS * HD)
        attn_out = jnp.dot(context, output_weight, preferred_element_type=jnp.float32)
        hidden = input_f32 + attn_out
        residuals.append(hidden.astype(jnp.bfloat16))
        normed_rows.append(rms_scale(hidden, residual_gain).astype(jnp.bfloat16))
    return (prompt_out, jnp.stack(residuals), jnp.stack(normed_rows))
```

```python
import functools
import math

import jax
import jax.numpy as jnp
from jax import lax
from jax.experimental import pallas as pl
from jax.experimental.pallas import tpu as pltpu
from jax.sharding import PartitionSpec as P

HD = 128
STEPS = 4
ROPE_BASE = 500000.0
NORM_EPS = 1e-05
SCORE_SCALE = math.log2(math.e) / math.sqrt(HD)

F32 = jnp.float32
BF16 = jnp.bfloat16


def call(body, grid, in_specs, out_specs, out_shape, name, scratch=(), flops=0, moved=0, exps=0):
    return pl.pallas_call(
        body,
        grid=grid,
        in_specs=in_specs,
        out_specs=out_specs,
        out_shape=out_shape,
        scratch_shapes=list(scratch),
        name=name,
        cost_estimate=pl.CostEstimate(flops=flops, bytes_accessed=moved, transcendentals=exps),
    )


def whole(shape):
    return pl.BlockSpec(shape, lambda *_: (0,) * len(shape))


def tables(positions):
    half = HD // 2
    exponent = jnp.arange(half, dtype=F32) * (2.0 / HD)
    inv_freq = ROPE_BASE ** (-exponent)
    angles = positions.astype(F32)[:, None] * inv_freq[None, :]
    cosine, sine = jnp.cos(angles), jnp.sin(angles)
    return jnp.concatenate([cosine, cosine], 1), jnp.concatenate([-sine, sine], 1)


def rope(u, cosine, sine):
    return u * cosine + pltpu.roll(u, HD // 2, 1) * sine


def pack_kv_body(k_ref, v_ref, cos_ref, sin_ref, out_ref):
    cosine, sine = cos_ref[...], sin_ref[...]
    width = out_ref.shape[3]
    for dest in range(out_ref.shape[0]):
        for lane in range(0, width, HD):
            column = dest * width + lane
            out_ref[dest, 0, :, lane : lane + HD] = rope(
                k_ref[:, column : column + HD].astype(F32), cosine, sine
            ).astype(BF16)
        out_ref[dest, 1] = v_ref[:, dest * width : (dest + 1) * width]


def pack_q_body(q_ref, cos_ref, sin_ref, out_ref):
    cosine, sine = cos_ref[...] * SCORE_SCALE, sin_ref[...] * SCORE_SCALE
    width = out_ref.shape[2]
    for dest in range(out_ref.shape[0]):
        for lane in range(0, width, HD):
            column = dest * width + lane
            out_ref[dest, :, lane : lane + HD] = rope(
                q_ref[:, column : column + HD].astype(F32), cosine, sine
            ).astype(BF16)


def normed(rows, gain):
    rows = rows.astype(F32)
    return (
        rows * lax.rsqrt(jnp.mean(rows * rows, axis=-1, keepdims=True) + NORM_EPS) * gain.astype(F32)
    ).astype(BF16)


def project_body(
    embed_ref, mask_ref, gain_ref, wq_ref, wk_ref, wv_ref, cos_ref, sin_ref,
    qe_ref, qm_ref, ke_ref, km_ref, ve_ref, vm_ref, mq, mk,
):
    gain = gain_ref[...]

    @pl.when(pl.program_id(0) == 0)
    def _():
        mask_row = normed(jnp.broadcast_to(mask_ref[...], (16, mask_ref.shape[1])), gain)
        mq[...] = jnp.dot(mask_row, wq_ref[...], preferred_element_type=F32)
        mk[...] = jnp.dot(mask_row, wk_ref[...], preferred_element_type=F32)
        vm_ref[...] = jnp.dot(mask_row, wv_ref[...], preferred_element_type=F32).astype(BF16)

    rows = normed(embed_ref[...], gain)
    count = rows.shape[0]
    q = jnp.dot(rows, wq_ref[...], preferred_element_type=F32)
    k = jnp.dot(rows, wk_ref[...], preferred_element_type=F32)
    ve_ref[...] = jnp.dot(rows, wv_ref[...], preferred_element_type=F32).astype(BF16)
    cosine, sine = cos_ref[...], sin_ref[...]
    for lane in range(0, q.shape[1], HD):
        at = slice(lane, lane + HD)
        qe_ref[:, at] = (rope(q[:, at], cosine, sine) * SCORE_SCALE).astype(BF16)
        ke_ref[:, at] = rope(k[:, at], cosine, sine).astype(BF16)
        one_q = jnp.broadcast_to(mq[0:1, at], (count, HD))
        one_k = jnp.broadcast_to(mk[0:1, at], (count, HD))
        qm_ref[:, at] = (rope(one_q, cosine, sine) * SCORE_SCALE).astype(BF16)
        km_ref[:, at] = rope(one_k, cosine, sine).astype(BF16)


def scores(q, k):
    return lax.dot_general(q, k, (((1,), (1,)), ((), ())), preferred_element_type=F32)


def start_softmax(s):
    top = jnp.max(s, axis=-1, keepdims=True)
    w = jnp.exp2(s - top)
    return top, jnp.sum(w, axis=-1, keepdims=True), w.astype(BF16)


def merge(state, s, v):
    top = jnp.max(s, axis=-1, keepdims=True)
    if state is None:
        w = jnp.exp2(s - top)
        return (
            top,
            jnp.sum(w, axis=-1, keepdims=True),
            jnp.dot(w.astype(BF16), v, preferred_element_type=F32),
        )
    old, total, acc = state
    top = jnp.maximum(old, top)
    keep = jnp.exp2(old - top)
    w = jnp.exp2(s - top)
    total = total * keep + jnp.sum(w, axis=-1, keepdims=True)
    acc = acc * keep + jnp.dot(w.astype(BF16), v, preferred_element_type=F32)
    return top, total, acc


def over_prompt(q, kv_ref, chunk):
    state = None
    sources, _, rows, width = kv_ref.shape
    for first in range(0, sources, chunk):
        k = kv_ref[first : first + chunk, 0].reshape(chunk * rows, width)
        v = kv_ref[first : first + chunk, 1].reshape(chunk * rows, width)
        state = merge(state, scores(q, k), v)
    return state


def response_body(chunk, kv_ref, qe_ref, qm_ref, ke_ref, km_ref, ve_ref, vm_ref, rows_ref, keys_ref, out_ref):
    lows, steps, highs, per, _ = out_ref.shape
    by_mask = over_prompt(qm_ref[...], kv_ref, chunk)
    by_embed = over_prompt(qe_ref[...], kv_ref, chunk)
    mask_value = jnp.broadcast_to(vm_ref[0:1], ve_ref.shape)
    for step in range(steps):
        shown = rows_ref[...] <= step
        shown_key = keys_ref[...] <= step
        one = rows_ref[:, 0:1] <= step
        q = jnp.where(shown, qe_ref[...], qm_ref[...])
        k = jnp.where(shown_key, ke_ref[...], km_ref[...])
        v = jnp.where(shown_key, ve_ref[...], mask_value)
        state = (
            jnp.where(one, by_embed[0], by_mask[0]),
            jnp.where(one, by_embed[1], by_mask[1]),
            jnp.where(shown, by_embed[2], by_mask[2]),
        )
        _, total, acc = merge(state, scores(q, k), v)
        context = (acc / total).astype(BF16)
        for high in range(highs):
            for low in range(lows):
                at = (high * lows + low) * per
                out_ref[low, step, high] = context[at : at + per]


def prompt_body(chunk, q_ref, kv_ref, km_ref, vm_ref, out_ref):
    sources, rows, width = q_ref.shape
    q = q_ref[...].reshape(sources * rows, width)
    s = scores(q, km_ref[...])
    top = jnp.max(s, axis=-1, keepdims=True)
    total = jnp.sum(jnp.exp2(s - top), axis=-1, keepdims=True)
    state = (top, total, total * vm_ref[0:1].astype(F32))
    count, _, per, _ = kv_ref.shape
    for first in range(0, count, chunk):
        k = kv_ref[first : first + chunk, 0].reshape(chunk * per, width)
        v = kv_ref[first : first + chunk, 1].reshape(chunk * per, width)
        state = merge(state, scores(q, k), v)
    out_ref[...] = (state[2] / state[1]).astype(BF16).reshape(sources, rows, width)


def output_body(place_ref, x_ref, *refs):
    w_refs, (send_ref, keep_ref) = refs[:-2], refs[-2:]
    low, bit = place_ref[0], place_ref[1]
    _, steps, highs, per, width = x_ref.shape
    total = None
    for k, w_ref in enumerate(w_refs):
        x = x_ref[low ^ k].reshape(steps * highs * per, width)
        term = jnp.dot(x, w_ref[...], preferred_element_type=F32)
        total = term if total is None else total + term
    for step in range(steps):
        for high in range(0, highs, 2):
            at = (step * highs + high) * per
            first, second = total[at : at + per], total[at + per : at + 2 * per]
            keep_ref[step, high // 2] = jnp.where(bit == 0, first, second)
            send_ref[step, high // 2] = jnp.where(bit == 0, second, first).astype(BF16)


def per_device(
    prompt_query,
    prompt_key,
    prompt_value,
    response_embed,
    mask_embed,
    commit_step,
    block_index,
    attention_gain,
    residual_gain,
    query_weight,
    key_weight,
    value_weight,
    output_weight,
):
    rows, head_cols = prompt_query.shape
    resp, model = response_embed.shape
    n = lax.axis_size("seq")
    me = lax.axis_index("seq")
    width = query_weight.shape[1]
    heads = width // HD
    prompt_len = rows * n
    lows = min(4, n)
    highs = n // lows
    per = resp // n

    def swap(x, bit):
        return lax.ppermute(x, "seq", [(i, i ^ bit) for i in range(n)])

    cos_p, sin_p = tables(me * rows + jnp.arange(rows, dtype=jnp.int32))
    cos_r, sin_r = tables(prompt_len + block_index[0] * resp + jnp.arange(resp, dtype=jnp.int32))

    dests = max(1, n // 4)
    kv_send = call(
        pack_kv_body,
        (n // dests,),
        [
            pl.BlockSpec((rows, dests * width), lambda j: (0, j)),
            pl.BlockSpec((rows, dests * width), lambda j: (0, j)),
            whole((rows, HD)),
            whole((rows, HD)),
        ],
        pl.BlockSpec((dests, 2, rows, width), lambda j: (j, 0, 0, 0)),
        jax.ShapeDtypeStruct((n, 2, rows, width), BF16),
        "pack_kv",
        flops=6 * rows * head_cols,
        moved=8 * rows * head_cols,
    )(prompt_key, prompt_value, cos_p, sin_p)
    kv = lax.all_to_all(kv_send, "seq", 0, 0, tiled=True)
    q_send = call(
        pack_q_body,
        (n // dests,),
        [
            pl.BlockSpec((rows, dests * width), lambda j: (0, j)),
            whole((rows, HD)),
            whole((rows, HD)),
        ],
        pl.BlockSpec((dests, rows, width), lambda j: (j, 0, 0)),
        jax.ShapeDtypeStruct((n, rows, width), BF16),
        "pack_q",
        flops=6 * rows * head_cols,
        moved=4 * rows * head_cols,
    )(prompt_query, cos_p, sin_p)
    q_heads = lax.all_to_all(q_send, "seq", 0, 0, tiled=True)

    weights = [output_weight]
    for bit in (2, 1) if lows == 4 else (1,):
        weights += [swap(w, bit) for w in weights]
    order = [0, 2, 1, 3] if lows == 4 else [0, 1]
    weights = [weights[order.index(k)] for k in range(lows)]

    block = min(resp, 128)
    row_block = pl.BlockSpec((block, width), lambda i: (i, 0))
    wide = jax.ShapeDtypeStruct((resp, width), BF16)
    qe, qm, ke, km, ve, vm = call(
        project_body,
        (resp // block,),
        [
            pl.BlockSpec((block, model), lambda i: (i, 0)),
            whole((1, model)),
            whole((1, model)),
            whole((model, width)),
            whole((model, width)),
            whole((model, width)),
            pl.BlockSpec((block, HD), lambda i: (i, 0)),
            pl.BlockSpec((block, HD), lambda i: (i, 0)),
        ],
        [row_block] * 5 + [whole((16, width))],
        [wide] * 5 + [jax.ShapeDtypeStruct((16, width), BF16)],
        "project",
        scratch=[pltpu.VMEM((16, width), F32)] * 2,
        flops=6 * resp * model * width,
        moved=2 * resp * model + 6 * model * width,
    )(
        response_embed, mask_embed[None, :], attention_gain[None, :],
        query_weight, key_weight, value_weight, cos_r, sin_r,
    )

    commit = jnp.broadcast_to(commit_step[:, None], (resp, HD))
    chunk = max(1, min(n, 512 // rows))
    q_rows = min(resp, 256)
    part = q_rows // (lows * per)
    kv_block = pl.BlockSpec((n, 2, rows, HD), lambda h, i: (0, 0, 0, h))
    q_block = pl.BlockSpec((q_rows, HD), lambda h, i: (i, h))
    key_block = pl.BlockSpec((resp, HD), lambda h, i: (0, h))
    vm_block = pl.BlockSpec((16, HD), lambda h, i: (0, h))
    context = call(
        functools.partial(response_body, chunk),
        (heads, resp // q_rows),
        [
            kv_block, q_block, q_block, key_block, key_block, key_block, vm_block,
            pl.BlockSpec((q_rows, HD), lambda h, i: (i, 0)),
            pl.BlockSpec((resp, HD), lambda h, i: (0, 0)),
        ],
        pl.BlockSpec((lows, STEPS, part, per, HD), lambda h, i: (0, 0, i, 0, h)),
        jax.ShapeDtypeStruct((lows, STEPS, highs, per, width), BF16),
        "response_attention",
        flops=4 * resp * width * (2 * prompt_len + STEPS * resp),
        moved=4 * prompt_len * width,
        exps=heads * resp * (2 * prompt_len + STEPS * resp),
    )(kv, qe, qm, ke, km, ve, vm, commit, commit)
    planes = [[h * lows + l for l in range(lows)] for h in range(highs)]
    plane_context = lax.all_to_all(context, "seq", 0, 0, axis_index_groups=planes, tiled=True)

    low = me % lows
    high = me // lows
    place = jnp.stack([low, high % 2]).astype(jnp.int32)
    columns = min(model, 512)
    out_block = pl.BlockSpec((STEPS, highs // 2, per, columns), lambda j, *_: (0, 0, 0, j))
    half = (STEPS, highs // 2, per, model)
    send, keep = pl.pallas_call(
        output_body,
        grid_spec=pltpu.PrefetchScalarGridSpec(
            num_scalar_prefetch=1,
            grid=(model // columns,),
            in_specs=[pl.BlockSpec((lows, STEPS, highs, per, width), lambda j, *_: (0, 0, 0, 0, 0))]
            + [pl.BlockSpec((width, columns), lambda j, *_: (0, j))] * lows,
            out_specs=[out_block, out_block],
        ),
        out_shape=[jax.ShapeDtypeStruct(half, BF16), jax.ShapeDtypeStruct(half, F32)],
        name="output_projection",
        cost_estimate=pl.CostEstimate(
            flops=2 * STEPS * resp * model * width, bytes_accessed=2 * lows * width * model, transcendentals=0
        ),
    )(place, plane_context, *weights)

    my_embed = lax.dynamic_slice_in_dim(response_embed, me * per, per, 0)
    my_commit = lax.dynamic_slice_in_dim(commit_step, me * per, per, 0)
    residuals, normeds = [], []
    for step in range(STEPS):
        sent, kept = send[step], keep[step]
        stride, level = lows, 0
        while True:
            kept = kept + swap(sent, stride).astype(F32)
            level += 1
            if kept.shape[0] == 1:
                break
            bit = (high >> level) & 1
            pairs = kept.reshape(kept.shape[0] // 2, 2, per, model)
            sent = lax.dynamic_index_in_dim(pairs, 1 - bit, 1, keepdims=False).astype(BF16)
            kept = lax.dynamic_index_in_dim(pairs, bit, 1, keepdims=False)
            stride *= 2
        shown = (my_commit <= step)[:, None]
        hidden = jnp.where(shown, my_embed, mask_embed[None, :]).astype(F32) + kept[0]
        residuals.append(hidden.astype(BF16))
        scale = lax.rsqrt(jnp.mean(hidden * hidden, axis=-1, keepdims=True) + NORM_EPS)
        normeds.append((hidden * scale * residual_gain.astype(F32)).astype(BF16))

    q_sources = max(1, 256 // rows)
    prompt_context = call(
        functools.partial(prompt_body, chunk),
        (heads, n // q_sources),
        [
            pl.BlockSpec((q_sources, rows, HD), lambda h, i: (i, 0, h)),
            kv_block,
            key_block,
            vm_block,
        ],
        pl.BlockSpec((q_sources, rows, HD), lambda h, i: (i, 0, h)),
        jax.ShapeDtypeStruct((n, rows, width), BF16),
        "prompt_attention",
        flops=4 * prompt_len * width * (prompt_len + resp),
        moved=8 * prompt_len * width,
        exps=heads * prompt_len * (prompt_len + resp),
    )(q_heads, kv, km, vm)
    back = lax.all_to_all(prompt_context, "seq", 0, 0, tiled=True)
    prompt_out = jnp.transpose(back, (1, 0, 2)).reshape(rows, head_cols)
    return prompt_out, jnp.stack(residuals), jnp.stack(normeds)


def solution(mesh):
    return jax.shard_map(
        per_device,
        mesh=mesh,
        in_specs=(
            P(("groups", "seq"), None),
            P(("groups", "seq"), None),
            P(("groups", "seq"), None),
            P("groups", None),
            P(),
            P("groups"),
            P("groups"),
            P(),
            P(),
            P(None, "seq"),
            P(None, "seq"),
            P(None, "seq"),
            P("seq", None),
        ),
        out_specs=(
            P(("groups", "seq"), None),
            P(None, ("groups", "seq"), None),
            P(None, ("groups", "seq"), None),
        ),
        check_vma=False,
    )
```

```python
import functools
import math

import jax
import jax.numpy as jnp
from jax import lax
from jax.experimental import pallas as pl
from jax.experimental.pallas import tpu as pltpu
from jax.sharding import PartitionSpec as P


HD = 128
STEPS = 4
ROPE_BASE = 500000.0
NORM_EPS = 1e-05
SCORE_SCALE = math.log2(math.e) / math.sqrt(HD)

F32 = jnp.float32
BF16 = jnp.bfloat16


def call(body, grid, in_specs, out_specs, out_shape, scratch=(), flops=0, moved=0, exps=0):
    return pl.pallas_call(
        body,
        grid=grid,
        in_specs=in_specs,
        out_specs=out_specs,
        out_shape=out_shape,
        scratch_shapes=list(scratch),
        cost_estimate=pl.CostEstimate(flops=flops, bytes_accessed=moved, transcendentals=exps),
    )


def whole(shape):
    return pl.BlockSpec(shape, lambda *_: (0,) * len(shape))


def tables(positions):
    half = HD // 2
    exponent = jnp.arange(half, dtype=F32) * (2.0 / HD)
    inv_freq = ROPE_BASE ** (-exponent)
    angles = positions.astype(F32)[:, None] * inv_freq[None, :]
    cosine, sine = jnp.cos(angles), jnp.sin(angles)
    return jnp.concatenate([cosine, cosine], 1), jnp.concatenate([-sine, sine], 1)


def rope(u, cosine, sine):
    return u * cosine + pltpu.roll(u, HD // 2, 1) * sine


def pack_kv_body(k_ref, v_ref, cos_ref, sin_ref, out_ref):
    cosine, sine = cos_ref[...], sin_ref[...]
    width = out_ref.shape[3]
    for dest in range(out_ref.shape[0]):
        for lane in range(0, width, HD):
            column = dest * width + lane
            out_ref[dest, 0, :, lane : lane + HD] = rope(
                k_ref[:, column : column + HD].astype(F32), cosine, sine
            ).astype(BF16)
        out_ref[dest, 1] = v_ref[:, dest * width : (dest + 1) * width]


def pack_q_body(me_ref, q_ref, cos_ref, sin_ref, *out_refs):
    cosine, sine = cos_ref[...] * SCORE_SCALE, sin_ref[...] * SCORE_SCALE
    width = out_refs[0].shape[1]
    for k, out_ref in enumerate(out_refs):
        start = (me_ref[0] ^ k) * width
        for lane in range(0, width, HD):
            u = q_ref[:, pl.ds(pl.multiple_of(start + lane, HD), HD)].astype(F32)
            out_ref[:, lane : lane + HD] = rope(u, cosine, sine).astype(BF16)


def normed(rows, gain):
    rows = rows.astype(F32)
    return (
        rows * lax.rsqrt(jnp.mean(rows * rows, axis=-1, keepdims=True) + NORM_EPS) * gain.astype(F32)
    ).astype(BF16)


def project_body(
    embed_ref, mask_ref, gain_ref, wq_ref, wk_ref, wv_ref, cos_ref, sin_ref,
    qe_ref, qm_ref, ke_ref, km_ref, ve_ref, vm_ref, mq, mk,
):
    gain = gain_ref[...]

    @pl.when(pl.program_id(0) == 0)
    def _():
        mask_row = normed(jnp.broadcast_to(mask_ref[...], (16, mask_ref.shape[1])), gain)
        mq[...] = jnp.dot(mask_row, wq_ref[...], preferred_element_type=F32)
        mk[...] = jnp.dot(mask_row, wk_ref[...], preferred_element_type=F32)
        vm_ref[...] = jnp.dot(mask_row, wv_ref[...], preferred_element_type=F32).astype(BF16)

    rows = normed(embed_ref[...], gain)
    count = rows.shape[0]
    q = jnp.dot(rows, wq_ref[...], preferred_element_type=F32)
    k = jnp.dot(rows, wk_ref[...], preferred_element_type=F32)
    ve_ref[...] = jnp.dot(rows, wv_ref[...], preferred_element_type=F32).astype(BF16)
    cosine, sine = cos_ref[...], sin_ref[...]
    for lane in range(0, q.shape[1], HD):
        at = slice(lane, lane + HD)
        qe_ref[:, at] = (rope(q[:, at], cosine, sine) * SCORE_SCALE).astype(BF16)
        ke_ref[:, at] = rope(k[:, at], cosine, sine).astype(BF16)
        one_q = jnp.broadcast_to(mq[0:1, at], (count, HD))
        one_k = jnp.broadcast_to(mk[0:1, at], (count, HD))
        qm_ref[:, at] = (rope(one_q, cosine, sine) * SCORE_SCALE).astype(BF16)
        km_ref[:, at] = rope(one_k, cosine, sine).astype(BF16)


def scores(q, k):
    return lax.dot_general(q, k, (((1,), (1,)), ((), ())), preferred_element_type=F32)


def merge(state, s, v):
    top = jnp.max(s, axis=-1, keepdims=True)
    if state is None:
        w = jnp.exp2(s - top)
        return (
            top,
            jnp.sum(w, axis=-1, keepdims=True),
            jnp.dot(w.astype(BF16), v, preferred_element_type=F32),
        )
    old, total, acc = state
    top = jnp.maximum(old, top)
    keep = jnp.exp2(old - top)
    w = jnp.exp2(s - top)
    total = total * keep + jnp.sum(w, axis=-1, keepdims=True)
    acc = acc * keep + jnp.dot(w.astype(BF16), v, preferred_element_type=F32)
    return top, total, acc


def over_prompt(state, q, kv_ref, chunk):
    sources, _, rows, width = kv_ref.shape
    for first in range(0, sources, chunk):
        k = kv_ref[first : first + chunk, 0].reshape(chunk * rows, width)
        v = kv_ref[first : first + chunk, 1].reshape(chunk * rows, width)
        state = merge(state, scores(q, k), v)
    return state


def response_body(chunk, low_ref, kv_ref, qe_ref, qm_ref, ke_ref, km_ref, ve_ref, vm_ref, commit_ref, *refs):
    out_refs, scratch_ref = refs[:-1], refs[-1]
    lows = len(out_refs)
    steps, highs, per, _ = out_refs[0].shape
    resp = qe_ref.shape[0]
    both = over_prompt(None, jnp.concatenate([qm_ref[...], qe_ref[...]], 0), kv_ref, chunk)
    mask_value = jnp.broadcast_to(vm_ref[0:1], ve_ref.shape)
    span = min(resp, chunk * kv_ref.shape[2])
    for step in range(steps):
        shown = commit_ref[...] <= step
        one = commit_ref[:, 0:1] <= step
        q = jnp.where(shown, qe_ref[...], qm_ref[...])
        k = jnp.where(shown, ke_ref[...], km_ref[...])
        v = jnp.where(shown, ve_ref[...], mask_value)
        state = (
            jnp.where(one, both[0][resp:], both[0][:resp]),
            jnp.where(one, both[1][resp:], both[1][:resp]),
            jnp.where(shown, both[2][resp:], both[2][:resp]),
        )
        for first in range(0, resp, span):
            state = merge(state, scores(q, k[first : first + span]), v[first : first + span])
        _, total, acc = state
        scratch_ref[...] = acc / total
        for high in range(highs):
            for k in range(lows):
                at = (high * lows + (low_ref[0] ^ k)) * per
                out_refs[k][step, high] = scratch_ref[pl.ds(pl.multiple_of(at, per), per), :].astype(BF16)


def prompt_body(chunk, group, me_ref, kv_ref, km_ref, vm_ref, *refs):
    q_refs, out_ref, queries = refs[: kv_ref.shape[0]], refs[-2], refs[-1]
    rows = out_ref.shape[1]
    for k, ref in enumerate(q_refs):
        queries[k * rows : (k + 1) * rows] = ref[...]

    @pl.loop(0, len(q_refs) // group)
    def _(turn):
        q = queries[pl.ds(pl.multiple_of(turn * (group * rows), group * rows), group * rows), :]
        s = scores(q, km_ref[...])
        top = jnp.max(s, axis=-1, keepdims=True)
        total = jnp.sum(jnp.exp2(s - top), axis=-1, keepdims=True)
        state = over_prompt((top, total, total * vm_ref[0:1].astype(F32)), q, kv_ref, chunk)
        context = (state[2] / state[1]).astype(BF16)
        for k in range(group):
            out_ref[me_ref[0] ^ (turn * group + k)] = context[k * rows : (k + 1) * rows]


def output_body(lows, place_ref, *refs):
    x_refs, w_refs, outs = refs[:lows], refs[lows : 2 * lows], refs[2 * lows :]
    steps, highs, per, width = x_refs[0].shape
    sends, keeps = outs[:steps], outs[steps:]
    bit = place_ref[1]
    total = None
    for x_ref, w_ref in zip(x_refs, w_refs):
        x = x_ref[...].reshape(steps * highs * per, width)
        term = jnp.dot(x, w_ref[...], preferred_element_type=F32)
        total = term if total is None else total + term
    for step in range(steps):
        for high in range(0, highs, 2):
            at = (step * highs + high) * per
            first, second = total[at : at + per], total[at + per : at + 2 * per]
            keeps[step][high // 2] = jnp.where(bit == 0, first, second)
            sends[step][high // 2] = jnp.where(bit == 0, second, first).astype(BF16)


def halve_body(place_ref, keep_ref, got_ref, send_ref, kept_ref):
    bit = place_ref[0]
    for pair in range(send_ref.shape[0]):
        first = keep_ref[2 * pair] + got_ref[2 * pair].astype(F32)
        second = keep_ref[2 * pair + 1] + got_ref[2 * pair + 1].astype(F32)
        kept_ref[pair] = jnp.where(bit == 0, first, second)
        send_ref[pair] = jnp.where(bit == 0, second, first).astype(BF16)


def finish_body(steps, place_ref, embed_ref, mask_ref, gain_ref, commit_ref, *refs):
    keeps, gots, (residual_ref, normed_ref) = refs[:steps], refs[steps : 2 * steps], refs[2 * steps :]
    gain = gain_ref[...].astype(F32)
    for step in range(steps):
        shown = commit_ref[:, 0:1] <= step
        rows = jnp.where(shown, embed_ref[...].astype(F32), mask_ref[...].astype(F32))
        hidden = rows + (keeps[step][0] + gots[step][0].astype(F32))
        residual_ref[step] = hidden.astype(BF16)
        scale = lax.rsqrt(jnp.mean(hidden * hidden, axis=-1, keepdims=True) + NORM_EPS)
        normed_ref[step] = (hidden * scale * gain).astype(BF16)


def unpack_body(in_ref, out_ref):
    width = in_ref.shape[2]
    for source in range(in_ref.shape[0]):
        out_ref[:, source * width : (source + 1) * width] = in_ref[source]


def per_device(
    prompt_query,
    prompt_key,
    prompt_value,
    response_embed,
    mask_embed,
    commit_step,
    block_index,
    attention_gain,
    residual_gain,
    query_weight,
    key_weight,
    value_weight,
    output_weight,
):
    rows, head_cols = prompt_query.shape
    resp, model = response_embed.shape
    n = lax.axis_size("seq")
    me = lax.axis_index("seq")
    width = query_weight.shape[1]
    heads = width // HD
    prompt_len = rows * n
    lows = min(4, n)
    highs = n // lows
    per = resp // n

    def swap(x, bit):
        return lax.ppermute(x, "seq", [(i, i ^ bit) for i in range(n)])

    dests = max(1, n // 4)
    cos_p, sin_p = tables(me * rows + jnp.arange(rows, dtype=jnp.int32))
    kv_send = call(
        pack_kv_body,
        (n // dests,),
        [
            pl.BlockSpec((rows, dests * width), lambda j: (0, j)),
            pl.BlockSpec((rows, dests * width), lambda j: (0, j)),
            whole((rows, HD)),
            whole((rows, HD)),
        ],
        pl.BlockSpec((dests, 2, rows, width), lambda j: (j, 0, 0, 0)),
        jax.ShapeDtypeStruct((n, 2, rows, width), BF16),
        flops=6 * rows * head_cols,
        moved=8 * rows * head_cols,
    )(prompt_key, prompt_value, cos_p, sin_p)
    kv = lax.all_to_all(kv_send, "seq", 0, 0, tiled=True)
    where = me.astype(jnp.int32).reshape(1)
    q_parts = pl.pallas_call(
        pack_q_body,
        grid_spec=pltpu.PrefetchScalarGridSpec(
            num_scalar_prefetch=1,
            grid=(1,),
            in_specs=[whole((rows, head_cols)), whole((rows, HD)), whole((rows, HD))],
            out_specs=[whole((rows, width))] * n,
        ),
        out_shape=[jax.ShapeDtypeStruct((rows, width), BF16)] * n,
        name="pack_q",
        cost_estimate=pl.CostEstimate(
            flops=6 * rows * head_cols, bytes_accessed=4 * rows * head_cols, transcendentals=0
        ),
    )(where, prompt_query, cos_p, sin_p)
    q_heads = [q_parts[0]]
    for k in range(1, n):
        q_heads.append(swap(q_parts[k], k))

    weights = [output_weight]
    if lows == 4:
        weights.append(swap(output_weight, 2))
    near = swap(output_weight, 1)
    if lows == 4:
        last = swap(weights[1], 1)
        weights = [output_weight, near, weights[1], last]
    else:
        weights = [output_weight, near]

    cos_r, sin_r = tables(prompt_len + block_index[0] * resp + jnp.arange(resp, dtype=jnp.int32))
    commit = jnp.broadcast_to(commit_step[:, None], (resp, HD))
    block = min(resp, 128)
    row_block = pl.BlockSpec((block, width), lambda i: (i, 0))
    wide = jax.ShapeDtypeStruct((resp, width), BF16)
    qe, qm, ke, km, ve, vm = call(
        project_body,
        (resp // block,),
        [
            pl.BlockSpec((block, model), lambda i: (i, 0)),
            whole((1, model)),
            whole((1, model)),
            whole((model, width)),
            whole((model, width)),
            whole((model, width)),
            pl.BlockSpec((block, HD), lambda i: (i, 0)),
            pl.BlockSpec((block, HD), lambda i: (i, 0)),
        ],
        [row_block] * 5 + [whole((16, width))],
        [wide] * 5 + [jax.ShapeDtypeStruct((16, width), BF16)],
        scratch=[pltpu.VMEM((16, width), F32)] * 2,
        flops=6 * resp * model * width,
        moved=2 * resp * model + 6 * model * width,
    )(
        response_embed, mask_embed[None, :], attention_gain[None, :],
        query_weight, key_weight, value_weight, cos_r, sin_r,
    )

    chunk = max(1, min(n, 256 // rows))
    kv_block = pl.BlockSpec((n, 2, rows, HD), lambda h, *_: (0, 0, 0, h))
    key_block = pl.BlockSpec((resp, HD), lambda h, *_: (0, h))
    vm_block = pl.BlockSpec((16, HD), lambda h, *_: (0, h))
    low = me & (lows - 1)
    high = me >> (lows.bit_length() - 1)
    place = jnp.stack([low, high & 1]).astype(jnp.int32)
    context = pl.pallas_call(
        functools.partial(response_body, chunk),
        grid_spec=pltpu.PrefetchScalarGridSpec(
            num_scalar_prefetch=1,
            grid=(heads,),
            in_specs=[kv_block] + [key_block] * 5 + [vm_block, whole((resp, HD))],
            out_specs=[pl.BlockSpec((STEPS, highs, per, HD), lambda h, *_: (0, 0, 0, h))] * lows,
            scratch_shapes=[pltpu.VMEM((resp, HD), F32)],
        ),
        out_shape=[jax.ShapeDtypeStruct((STEPS, highs, per, width), BF16)] * lows,
        name="response_attention",
        cost_estimate=pl.CostEstimate(
            flops=4 * resp * width * (2 * prompt_len + STEPS * resp),
            bytes_accessed=4 * prompt_len * width,
            transcendentals=heads * resp * (2 * prompt_len + STEPS * resp),
        ),
    )(place, kv, qe, qm, ke, km, ve, vm, commit)
    plane_context = [context[0]]
    for k in range(1, lows):
        plane_context.append(swap(context[k], k))

    columns = min(model, 512)
    out_block = pl.BlockSpec((highs // 2, per, columns), lambda j, *_: (0, 0, j))
    half = (highs // 2, per, model)
    parts = pl.pallas_call(
        functools.partial(output_body, lows),
        grid_spec=pltpu.PrefetchScalarGridSpec(
            num_scalar_prefetch=1,
            grid=(model // columns,),
            in_specs=[whole((STEPS, highs, per, width))] * lows
            + [pl.BlockSpec((width, columns), lambda j, *_: (0, j))] * lows,
            out_specs=[out_block] * (2 * STEPS),
        ),
        out_shape=[jax.ShapeDtypeStruct(half, BF16)] * STEPS + [jax.ShapeDtypeStruct(half, F32)] * STEPS,
        name="output_projection",
        cost_estimate=pl.CostEstimate(
            flops=2 * STEPS * resp * model * width, bytes_accessed=2 * lows * width * model, transcendentals=0
        ),
    )(place, *plane_context, *weights)
    sends, keeps = parts[:STEPS], parts[STEPS:]

    level = 0
    while True:
        gots = []
        for step in range(STEPS):
            gots.append(swap(sends[step], lows << level))
        count = keeps[0].shape[0]
        if count == 1:
            break
        level += 1
        bit = ((high >> level) & 1).astype(jnp.int32).reshape(1)
        sends, kept = [], []
        for step in range(STEPS):
            columns = min(model, 2048)
            get = pl.BlockSpec((count, per, columns), lambda j, *_: (0, 0, j))
            put = pl.BlockSpec((count // 2, per, columns), lambda j, *_: (0, 0, j))
            one, two = pl.pallas_call(
                halve_body,
                grid_spec=pltpu.PrefetchScalarGridSpec(
                    num_scalar_prefetch=1,
                    grid=(model // columns,),
                    in_specs=[get, get],
                    out_specs=[put, put],
                ),
                out_shape=[
                    jax.ShapeDtypeStruct((count // 2, per, model), BF16),
                    jax.ShapeDtypeStruct((count // 2, per, model), F32),
                ],
                name="halve",
                cost_estimate=pl.CostEstimate(
                    flops=count * per * model, bytes_accessed=9 * count * per * model, transcendentals=0
                ),
            )(bit, keeps[step], gots[step])
            sends.append(one)
            kept.append(two)
        keeps = kept

    group = max(1, min(n, 1024 // rows))
    prompt_context = None
    for head in range(heads):
        of_head = functools.partial(lambda head, *_: (0, head), head)
        of_kv = functools.partial(lambda head, *_: (0, 0, 0, head), head)
        earlier = [] if prompt_context is None else [prompt_context]
        prompt_context = pl.pallas_call(
            functools.partial(prompt_body, chunk, group),
            grid_spec=pltpu.PrefetchScalarGridSpec(
                num_scalar_prefetch=1,
                grid=(1,),
                in_specs=[
                    pl.BlockSpec((n, 2, rows, HD), of_kv),
                    pl.BlockSpec((resp, HD), of_head),
                    pl.BlockSpec((16, HD), of_head),
                ]
                + [pl.BlockSpec((rows, HD), of_head)] * n
                + [pl.BlockSpec(memory_space=pl.ANY)] * len(earlier),
                out_specs=pl.BlockSpec((n, rows, HD), functools.partial(lambda head, *_: (0, 0, head), head)),
                scratch_shapes=[pltpu.VMEM((n * rows, HD), BF16)],
            ),
            out_shape=jax.ShapeDtypeStruct((n, rows, width), BF16),
            name="prompt_attention",
            input_output_aliases={n + 4: 0} if earlier else {},
            cost_estimate=pl.CostEstimate(
                flops=4 * prompt_len * HD * (prompt_len + resp),
                bytes_accessed=8 * prompt_len * HD,
                transcendentals=prompt_len * (prompt_len + resp),
            ),
        )(where, kv, km, vm, *q_heads, *earlier)
    back = lax.all_to_all(prompt_context, "seq", 0, 0, tiled=True)

    row_block = pl.BlockSpec((per, model), lambda i, at: (at[0], 0))
    sums = pl.BlockSpec((1, per, model), lambda i, at: (0, 0, 0))
    result = pl.BlockSpec((STEPS, per, model), lambda i, at: (0, 0, 0))
    residual, normed_rows = pl.pallas_call(
        functools.partial(finish_body, STEPS),
        grid_spec=pltpu.PrefetchScalarGridSpec(
            num_scalar_prefetch=1,
            grid=(1,),
            in_specs=[
                row_block,
                pl.BlockSpec((1, model), lambda i, at: (0, 0)),
                pl.BlockSpec((1, model), lambda i, at: (0, 0)),
                pl.BlockSpec((per, HD), lambda i, at: (at[0], 0)),
            ]
            + [sums] * (2 * STEPS),
            out_specs=[result, result],
        ),
        out_shape=[jax.ShapeDtypeStruct((STEPS, per, model), BF16)] * 2,
        name="finish",
    )(
        where, response_embed, mask_embed[None, :], residual_gain[None, :],
        commit, *keeps, *gots,
    )
    columns = max(1, n // 4)
    prompt_out = call(
        unpack_body,
        (n // columns,),
        [pl.BlockSpec((columns, rows, width), lambda j: (j, 0, 0))],
        pl.BlockSpec((rows, columns * width), lambda j: (0, j)),
        jax.ShapeDtypeStruct((rows, head_cols), BF16),
        moved=4 * rows * head_cols,
    )(back)
    return prompt_out, residual, normed_rows


def solution(mesh):
    return jax.shard_map(
        per_device,
        mesh=mesh,
        in_specs=(
            P(("groups", "seq"), None),
            P(("groups", "seq"), None),
            P(("groups", "seq"), None),
            P("groups", None),
            P(),
            P("groups"),
            P("groups"),
            P(),
            P(),
            P(None, "seq"),
            P(None, "seq"),
            P(None, "seq"),
            P("seq", None),
        ),
        out_specs=(
            P(("groups", "seq"), None),
            P(None, ("groups", "seq"), None),
            P(None, ("groups", "seq"), None),
        ),
        check_vma=False,
    )
```

```python
import functools
import math

import jax
import jax.numpy as jnp
from jax import lax
from jax.experimental import pallas as pl
from jax.experimental.pallas import tpu as pltpu
from jax.sharding import PartitionSpec as P


HD = 128
STEPS = 4
ROPE_BASE = 500000.0
NORM_EPS = 1e-05
SCORE_SCALE = math.log2(math.e) / math.sqrt(HD)

F32 = jnp.float32
BF16 = jnp.bfloat16


def call(body, grid, in_specs, out_specs, out_shape, scratch=(), flops=0, moved=0, exps=0):
    return pl.pallas_call(
        body,
        grid=grid,
        in_specs=in_specs,
        out_specs=out_specs,
        out_shape=out_shape,
        scratch_shapes=list(scratch),
        cost_estimate=pl.CostEstimate(flops=flops, bytes_accessed=moved, transcendentals=exps),
    )


def whole(shape):
    return pl.BlockSpec(shape, lambda *_: (0,) * len(shape))


def tables(positions):
    half = HD // 2
    exponent = jnp.arange(half, dtype=F32) * (2.0 / HD)
    inv_freq = ROPE_BASE ** (-exponent)
    angles = positions.astype(F32)[:, None] * inv_freq[None, :]
    cosine, sine = jnp.cos(angles), jnp.sin(angles)
    return jnp.concatenate([cosine, cosine], 1), jnp.concatenate([-sine, sine], 1)


def rope(u, cosine, sine):
    return u * cosine + pltpu.roll(u, HD // 2, 1) * sine


def pack_kv_body(k_ref, v_ref, cos_ref, sin_ref, out_ref):
    cosine, sine = cos_ref[...], sin_ref[...]
    width = out_ref.shape[3]
    for dest in range(out_ref.shape[0]):
        for lane in range(0, width, HD):
            column = dest * width + lane
            out_ref[dest, 0, :, lane : lane + HD] = rope(
                k_ref[:, column : column + HD].astype(F32), cosine, sine
            ).astype(BF16)
        out_ref[dest, 1] = v_ref[:, dest * width : (dest + 1) * width]


def pack_q_body(me_ref, q_ref, cos_ref, sin_ref, *out_refs):
    cosine, sine = cos_ref[...] * SCORE_SCALE, sin_ref[...] * SCORE_SCALE
    width = out_refs[0].shape[1]
    for k, out_ref in enumerate(out_refs):
        start = (me_ref[0] ^ k) * width
        for lane in range(0, width, HD):
            u = q_ref[:, pl.ds(pl.multiple_of(start + lane, HD), HD)].astype(F32)
            out_ref[:, lane : lane + HD] = rope(u, cosine, sine).astype(BF16)


def normed(rows, gain):
    rows = rows.astype(F32)
    return (
        rows * lax.rsqrt(jnp.mean(rows * rows, axis=-1, keepdims=True) + NORM_EPS) * gain.astype(F32)
    ).astype(BF16)


def project_body(
    embed_ref, mask_ref, gain_ref, wq_ref, wk_ref, wv_ref, cos_ref, sin_ref,
    qe_ref, qm_ref, ke_ref, km_ref, ve_ref, vm_ref, mq, mk,
):
    gain = gain_ref[...]

    @pl.when(pl.program_id(0) == 0)
    def _():
        mask_row = normed(jnp.broadcast_to(mask_ref[...], (16, mask_ref.shape[1])), gain)
        mq[...] = jnp.dot(mask_row, wq_ref[...], preferred_element_type=F32)
        mk[...] = jnp.dot(mask_row, wk_ref[...], preferred_element_type=F32)
        vm_ref[...] = jnp.dot(mask_row, wv_ref[...], preferred_element_type=F32).astype(BF16)

    rows = normed(embed_ref[...], gain)
    count = rows.shape[0]
    q = jnp.dot(rows, wq_ref[...], preferred_element_type=F32)
    k = jnp.dot(rows, wk_ref[...], preferred_element_type=F32)
    ve_ref[...] = jnp.dot(rows, wv_ref[...], preferred_element_type=F32).astype(BF16)
    cosine, sine = cos_ref[...], sin_ref[...]
    for lane in range(0, q.shape[1], HD):
        at = slice(lane, lane + HD)
        qe_ref[:, at] = (rope(q[:, at], cosine, sine) * SCORE_SCALE).astype(BF16)
        ke_ref[:, at] = rope(k[:, at], cosine, sine).astype(BF16)
        one_q = jnp.broadcast_to(mq[0:1, at], (count, HD))
        one_k = jnp.broadcast_to(mk[0:1, at], (count, HD))
        qm_ref[:, at] = (rope(one_q, cosine, sine) * SCORE_SCALE).astype(BF16)
        km_ref[:, at] = rope(one_k, cosine, sine).astype(BF16)


def scores(q, k):
    return lax.dot_general(q, k, (((1,), (1,)), ((), ())), preferred_element_type=F32)


def merge(state, s, v):
    top = jnp.max(s, axis=-1, keepdims=True)
    if state is None:
        w = jnp.exp2(s - top)
        return (
            top,
            jnp.sum(w, axis=-1, keepdims=True),
            jnp.dot(w.astype(BF16), v, preferred_element_type=F32),
        )
    old, total, acc = state
    top = jnp.maximum(old, top)
    keep = jnp.exp2(old - top)
    w = jnp.exp2(s - top)
    total = total * keep + jnp.sum(w, axis=-1, keepdims=True)
    acc = acc * keep + jnp.dot(w.astype(BF16), v, preferred_element_type=F32)
    return top, total, acc


def over_prompt(state, q, kv_ref, chunk):
    sources, _, rows, width = kv_ref.shape
    for first in range(0, sources, chunk):
        k = kv_ref[first : first + chunk, 0].reshape(chunk * rows, width)
        v = kv_ref[first : first + chunk, 1].reshape(chunk * rows, width)
        state = merge(state, scores(q, k), v)
    return state


def response_body(chunk, kept, place_ref, kv_ref, qe_ref, qm_ref, ke_ref, km_ref, ve_ref, vm_ref, commit_ref, *refs):
    out_refs, scratch_ref = refs[:-1], refs[-1]
    lows = len(out_refs)
    steps, blocks, per, _ = out_refs[0].shape
    low, bit = place_ref[0], place_ref[1]
    span_rows = lows * per
    count = blocks * span_rows
    side = bit if kept else 1 - bit

    def mine(ref):
        parts = [
            ref[pl.ds(pl.multiple_of((2 * block + side) * span_rows, span_rows), span_rows), :]
            for block in range(blocks)
        ]
        return jnp.concatenate(parts, 0) if blocks > 1 else parts[0]

    by_mask, by_embed, revealed = mine(qm_ref), mine(qe_ref), mine(commit_ref)
    both = over_prompt(None, jnp.concatenate([by_mask, by_embed], 0), kv_ref, chunk)
    mask_value = jnp.broadcast_to(vm_ref[0:1], ve_ref.shape)
    for step in range(steps):
        shown = revealed <= step
        one = revealed[:, 0:1] <= step
        shown_key = commit_ref[...] <= step
        q = jnp.where(shown, by_embed, by_mask)
        k = jnp.where(shown_key, ke_ref[...], km_ref[...])
        v = jnp.where(shown_key, ve_ref[...], mask_value)
        state = (
            jnp.where(one, both[0][count:], both[0][:count]),
            jnp.where(one, both[1][count:], both[1][:count]),
            jnp.where(shown, both[2][count:], both[2][:count]),
        )
        _, total, acc = merge(state, scores(q, k), v)
        scratch_ref[step] = acc * (1.0 / total)
    for step in range(steps):
        for block in range(blocks):
            for k in range(lows):
                at = block * span_rows + (low ^ k) * per
                out_refs[k][step, block] = scratch_ref[step, pl.ds(pl.multiple_of(at, per), per), :].astype(BF16)


def prompt_body(chunk, group, me_ref, kv_ref, km_ref, vm_ref, *refs):
    q_refs, out_ref, queries = refs[: kv_ref.shape[0]], refs[-2], refs[-1]
    rows = out_ref.shape[1]
    for k, ref in enumerate(q_refs):
        queries[k * rows : (k + 1) * rows] = ref[...]

    @pl.loop(0, len(q_refs) // group)
    def _(turn):
        q = queries[pl.ds(pl.multiple_of(turn * (group * rows), group * rows), group * rows), :]
        s = scores(q, km_ref[...])
        top = jnp.max(s, axis=-1, keepdims=True)
        total = jnp.sum(jnp.exp2(s - top), axis=-1, keepdims=True)
        state = over_prompt((top, total, total * vm_ref[0:1].astype(F32)), q, kv_ref, chunk)
        context = (state[2] / state[1]).astype(BF16)
        for k in range(group):
            out_ref[me_ref[0] ^ (turn * group + k)] = context[k * rows : (k + 1) * rows]


def output_body(lows, split, place_ref, *refs):
    x_refs, refs = refs[:lows], refs[lows:]
    outs = refs[-STEPS:]
    steps, blocks, per, width = x_refs[0].shape
    far = lows // 2 if split else lows
    w = jnp.concatenate([ref[...] for ref in refs[:-STEPS]], 0)
    xs = []
    for k, x_ref in enumerate(x_refs):
        x = x_ref[...].reshape(steps * blocks * per, width)
        if k >= far:
            swapped = jnp.concatenate([x[:, width // 2 :], x[:, : width // 2]], 1)
            x = jnp.where(place_ref[2] == 0, x, swapped)
        xs.append(x)
    total = jnp.dot(jnp.concatenate(xs, 1), w, preferred_element_type=F32)
    for step, out_ref in enumerate(outs):
        for block in range(blocks):
            at = (step * blocks + block) * per
            out_ref[block] = total[at : at + per].astype(out_ref.dtype)


def halve_body(place_ref, keep_ref, got_ref, send_ref, kept_ref):
    bit = place_ref[0]
    for pair in range(send_ref.shape[0]):
        first = keep_ref[2 * pair] + got_ref[2 * pair].astype(F32)
        second = keep_ref[2 * pair + 1] + got_ref[2 * pair + 1].astype(F32)
        kept_ref[pair] = jnp.where(bit == 0, first, second)
        send_ref[pair] = jnp.where(bit == 0, second, first).astype(BF16)


def finish_body(steps, place_ref, embed_ref, mask_ref, gain_ref, commit_ref, *refs):
    keeps, gots, (residual_ref, normed_ref) = refs[:steps], refs[steps : 2 * steps], refs[2 * steps :]
    gain = gain_ref[...].astype(F32)
    for step in range(steps):
        shown = commit_ref[:, 0:1] <= step
        rows = jnp.where(shown, embed_ref[...].astype(F32), mask_ref[...].astype(F32))
        hidden = rows + (keeps[step][0] + gots[step][0].astype(F32))
        residual_ref[step] = hidden.astype(BF16)
        scale = lax.rsqrt(jnp.mean(hidden * hidden, axis=-1, keepdims=True) + NORM_EPS)
        normed_ref[step] = (hidden * scale * gain).astype(BF16)


def unpack_body(in_ref, out_ref):
    width = in_ref.shape[2]
    for source in range(in_ref.shape[0]):
        out_ref[:, source * width : (source + 1) * width] = in_ref[source]


def per_device(
    prompt_query,
    prompt_key,
    prompt_value,
    response_embed,
    mask_embed,
    commit_step,
    block_index,
    attention_gain,
    residual_gain,
    query_weight,
    key_weight,
    value_weight,
    output_weight,
):
    rows, head_cols = prompt_query.shape
    resp, model = response_embed.shape
    n = lax.axis_size("seq")
    me = lax.axis_index("seq")
    width = query_weight.shape[1]
    heads = width // HD
    prompt_len = rows * n
    lows = min(4, n)
    highs = n // lows
    per = resp // n

    def swap(x, bit):
        return lax.ppermute(x, "seq", [(i, i ^ bit) for i in range(n)])

    dests = max(1, n // 4)
    cos_p, sin_p = tables(me * rows + jnp.arange(rows, dtype=jnp.int32))
    kv_send = call(
        pack_kv_body,
        (n // dests,),
        [
            pl.BlockSpec((rows, dests * width), lambda j: (0, j)),
            pl.BlockSpec((rows, dests * width), lambda j: (0, j)),
            whole((rows, HD)),
            whole((rows, HD)),
        ],
        pl.BlockSpec((dests, 2, rows, width), lambda j: (j, 0, 0, 0)),
        jax.ShapeDtypeStruct((n, 2, rows, width), BF16),
        flops=6 * rows * head_cols,
        moved=8 * rows * head_cols,
    )(prompt_key, prompt_value, cos_p, sin_p)
    kv = lax.all_to_all(kv_send, "seq", 0, 0, tiled=True)
    where = me.astype(jnp.int32).reshape(1)
    q_parts = pl.pallas_call(
        pack_q_body,
        grid_spec=pltpu.PrefetchScalarGridSpec(
            num_scalar_prefetch=1,
            grid=(1,),
            in_specs=[whole((rows, head_cols)), whole((rows, HD)), whole((rows, HD))],
            out_specs=[whole((rows, width))] * n,
        ),
        out_shape=[jax.ShapeDtypeStruct((rows, width), BF16)] * n,
        name="pack_q",
        cost_estimate=pl.CostEstimate(
            flops=6 * rows * head_cols, bytes_accessed=4 * rows * head_cols, transcendentals=0
        ),
    )(where, prompt_query, cos_p, sin_p)
    q_heads = [q_parts[0]]
    for k in range(1, n):
        q_heads.append(swap(q_parts[k], k))

    groups = lax.axis_size("groups")
    group = lax.axis_index("groups")
    split = lows == 4 and groups % 2 == 0
    weights = [output_weight, swap(output_weight, 1)]
    if split:
        half_rows = lax.dynamic_slice_in_dim(output_weight, (group & 1) * (width // 2), width // 2, 0)
        fetched = swap(half_rows, 2)
        given = lax.ppermute(fetched, "groups", [(i, i ^ 1) for i in range(groups)])
        last = swap(fetched, 1)
        weights += [fetched, given, last, swap(given, 1)]
    elif lows == 4:
        far = swap(output_weight, 2)
        weights += [far, swap(far, 1)]

    cos_r, sin_r = tables(prompt_len + block_index[0] * resp + jnp.arange(resp, dtype=jnp.int32))
    commit = jnp.broadcast_to(commit_step[:, None], (resp, HD))
    block = min(resp, 128)
    row_block = pl.BlockSpec((block, width), lambda i: (i, 0))
    wide = jax.ShapeDtypeStruct((resp, width), BF16)
    qe, qm, ke, km, ve, vm = call(
        project_body,
        (resp // block,),
        [
            pl.BlockSpec((block, model), lambda i: (i, 0)),
            whole((1, model)),
            whole((1, model)),
            whole((model, width)),
            whole((model, width)),
            whole((model, width)),
            pl.BlockSpec((block, HD), lambda i: (i, 0)),
            pl.BlockSpec((block, HD), lambda i: (i, 0)),
        ],
        [row_block] * 5 + [whole((16, width))],
        [wide] * 5 + [jax.ShapeDtypeStruct((16, width), BF16)],
        scratch=[pltpu.VMEM((16, width), F32)] * 2,
        flops=6 * resp * model * width,
        moved=2 * resp * model + 6 * model * width,
    )(
        response_embed, mask_embed[None, :], attention_gain[None, :],
        query_weight, key_weight, value_weight, cos_r, sin_r,
    )

    chunk = max(1, min(n, 256 // rows))
    kv_block = pl.BlockSpec((n, 2, rows, HD), lambda h, *_: (0, 0, 0, h))
    key_block = pl.BlockSpec((resp, HD), lambda h, *_: (0, h))
    vm_block = pl.BlockSpec((16, HD), lambda h, *_: (0, h))
    low = me & (lows - 1)
    high = me >> (lows.bit_length() - 1)
    blocks = highs // 2
    place = jnp.stack([low, high & 1, group & 1]).astype(jnp.int32)
    columns = min(model, 1024)
    projected = {}
    for kept in (False, True):
        context = pl.pallas_call(
            functools.partial(response_body, chunk, kept),
            grid_spec=pltpu.PrefetchScalarGridSpec(
                num_scalar_prefetch=1,
                grid=(heads,),
                in_specs=[kv_block] + [key_block] * 5 + [vm_block, whole((resp, HD))],
                out_specs=[pl.BlockSpec((STEPS, blocks, per, HD), lambda h, *_: (0, 0, 0, h))] * lows,
                scratch_shapes=[pltpu.VMEM((STEPS, resp // 2, HD), F32)],
            ),
            out_shape=[jax.ShapeDtypeStruct((STEPS, blocks, per, width), BF16)] * lows,
            name="response_attention",
            cost_estimate=pl.CostEstimate(
                flops=2 * resp * width * (2 * prompt_len + STEPS * resp),
                bytes_accessed=4 * prompt_len * width,
                transcendentals=heads * resp * (2 * prompt_len + STEPS * resp) // 2,
            ),
        )(place, kv, qe, qm, ke, km, ve, vm, commit)
        plane_context = [context[0]]
        for k in range(1, lows):
            plane_context.append(swap(context[k], k))
        projected[kept] = pl.pallas_call(
            functools.partial(output_body, lows, split),
            grid_spec=pltpu.PrefetchScalarGridSpec(
                num_scalar_prefetch=1,
                grid=(model // columns,),
                in_specs=[whole((STEPS, blocks, per, width))] * lows
                + [pl.BlockSpec((w.shape[0], columns), lambda j, *_: (0, j)) for w in weights],
                out_specs=[pl.BlockSpec((blocks, per, columns), lambda j, *_: (0, 0, j))] * STEPS,
            ),
            out_shape=[jax.ShapeDtypeStruct((blocks, per, model), F32 if kept else BF16)] * STEPS,
            name="output_projection",
            cost_estimate=pl.CostEstimate(
                flops=STEPS * resp * model * width, bytes_accessed=2 * lows * width * model, transcendentals=0
            ),
        )(place, *plane_context, *weights)
    sends, keeps = projected[False], projected[True]

    level = 0
    while True:
        gots = []
        for step in range(STEPS):
            gots.append(swap(sends[step], lows << level))
        count = keeps[0].shape[0]
        if count == 1:
            break
        level += 1
        bit = ((high >> level) & 1).astype(jnp.int32).reshape(1)
        sends, kept = [], []
        for step in range(STEPS):
            columns = min(model, 2048)
            get = pl.BlockSpec((count, per, columns), lambda j, *_: (0, 0, j))
            put = pl.BlockSpec((count // 2, per, columns), lambda j, *_: (0, 0, j))
            one, two = pl.pallas_call(
                halve_body,
                grid_spec=pltpu.PrefetchScalarGridSpec(
                    num_scalar_prefetch=1,
                    grid=(model // columns,),
                    in_specs=[get, get],
                    out_specs=[put, put],
                ),
                out_shape=[
                    jax.ShapeDtypeStruct((count // 2, per, model), BF16),
                    jax.ShapeDtypeStruct((count // 2, per, model), F32),
                ],
                name="halve",
                cost_estimate=pl.CostEstimate(
                    flops=count * per * model, bytes_accessed=9 * count * per * model, transcendentals=0
                ),
            )(bit, keeps[step], gots[step])
            sends.append(one)
            kept.append(two)
        keeps = kept

    blocks_of_q = max(1, min(n, 1024 // rows))
    prompt_context = None
    for head in range(heads):
        of_head = functools.partial(lambda head, *_: (0, head), head)
        of_kv = functools.partial(lambda head, *_: (0, 0, 0, head), head)
        earlier = [] if prompt_context is None else [prompt_context]
        prompt_context = pl.pallas_call(
            functools.partial(prompt_body, chunk, blocks_of_q),
            grid_spec=pltpu.PrefetchScalarGridSpec(
                num_scalar_prefetch=1,
                grid=(1,),
                in_specs=[
                    pl.BlockSpec((n, 2, rows, HD), of_kv),
                    pl.BlockSpec((resp, HD), of_head),
                    pl.BlockSpec((16, HD), of_head),
                ]
                + [pl.BlockSpec((rows, HD), of_head)] * n
                + [pl.BlockSpec(memory_space=pl.ANY)] * len(earlier),
                out_specs=pl.BlockSpec((n, rows, HD), functools.partial(lambda head, *_: (0, 0, head), head)),
                scratch_shapes=[pltpu.VMEM((n * rows, HD), BF16)],
            ),
            out_shape=jax.ShapeDtypeStruct((n, rows, width), BF16),
            name="prompt_attention",
            input_output_aliases={n + 4: 0} if earlier else {},
            cost_estimate=pl.CostEstimate(
                flops=4 * prompt_len * HD * (prompt_len + resp),
                bytes_accessed=8 * prompt_len * HD,
                transcendentals=prompt_len * (prompt_len + resp),
            ),
        )(where, kv, km, vm, *q_heads, *earlier)
    back = lax.all_to_all(prompt_context, "seq", 0, 0, tiled=True)

    row_block = pl.BlockSpec((per, model), lambda i, at: (at[0], 0))
    sums = pl.BlockSpec((1, per, model), lambda i, at: (0, 0, 0))
    result = pl.BlockSpec((STEPS, per, model), lambda i, at: (0, 0, 0))
    residual, normed_rows = pl.pallas_call(
        functools.partial(finish_body, STEPS),
        grid_spec=pltpu.PrefetchScalarGridSpec(
            num_scalar_prefetch=1,
            grid=(1,),
            in_specs=[
                row_block,
                pl.BlockSpec((1, model), lambda i, at: (0, 0)),
                pl.BlockSpec((1, model), lambda i, at: (0, 0)),
                pl.BlockSpec((per, HD), lambda i, at: (at[0], 0)),
            ]
            + [sums] * (2 * STEPS),
            out_specs=[result, result],
        ),
        out_shape=[jax.ShapeDtypeStruct((STEPS, per, model), BF16)] * 2,
        name="finish",
    )(
        where, response_embed, mask_embed[None, :], residual_gain[None, :],
        commit, *keeps, *gots,
    )
    columns = max(1, n // 4)
    prompt_out = call(
        unpack_body,
        (n // columns,),
        [pl.BlockSpec((columns, rows, width), lambda j: (j, 0, 0))],
        pl.BlockSpec((rows, columns * width), lambda j: (0, j)),
        jax.ShapeDtypeStruct((rows, head_cols), BF16),
        moved=4 * rows * head_cols,
    )(back)
    return prompt_out, residual, normed_rows


def solution(mesh):
    return jax.shard_map(
        per_device,
        mesh=mesh,
        in_specs=(
            P(("groups", "seq"), None),
            P(("groups", "seq"), None),
            P(("groups", "seq"), None),
            P("groups", None),
            P(),
            P("groups"),
            P("groups"),
            P(),
            P(),
            P(None, "seq"),
            P(None, "seq"),
            P(None, "seq"),
            P("seq", None),
        ),
        out_specs=(
            P(("groups", "seq"), None),
            P(None, ("groups", "seq"), None),
            P(None, ("groups", "seq"), None),
        ),
        check_vma=False,
    )
```

```python
import functools
import math

import jax
import jax.numpy as jnp
from jax import lax
from jax.experimental import pallas as pl
from jax.experimental.pallas import tpu as pltpu
from jax.sharding import PartitionSpec as P


HD = 128
STEPS = 4
ROPE_BASE = 500000.0
NORM_EPS = 1e-05
SCORE_SCALE = math.log2(math.e) / math.sqrt(HD)

F32 = jnp.float32
BF16 = jnp.bfloat16


def call(body, grid, in_specs, out_specs, out_shape, scratch=(), flops=0, moved=0, exps=0):
    return pl.pallas_call(
        body,
        grid=grid,
        in_specs=in_specs,
        out_specs=out_specs,
        out_shape=out_shape,
        scratch_shapes=list(scratch),
        cost_estimate=pl.CostEstimate(flops=flops, bytes_accessed=moved, transcendentals=exps),
    )


def whole(shape):
    return pl.BlockSpec(shape, lambda *_: (0,) * len(shape))


def tables(positions):
    half = HD // 2
    exponent = jnp.arange(half, dtype=F32) * (2.0 / HD)
    inv_freq = ROPE_BASE ** (-exponent)
    angles = positions.astype(F32)[:, None] * inv_freq[None, :]
    cosine, sine = jnp.cos(angles), jnp.sin(angles)
    return jnp.concatenate([cosine, cosine], 1), jnp.concatenate([-sine, sine], 1)


def rope(u, cosine, sine):
    return u * cosine + pltpu.roll(u, HD // 2, 1) * sine


def pack_kv_body(k_ref, v_ref, cos_ref, sin_ref, out_ref):
    cosine, sine = cos_ref[...], sin_ref[...]
    width = out_ref.shape[3]
    for dest in range(out_ref.shape[0]):
        for lane in range(0, width, HD):
            column = dest * width + lane
            out_ref[dest, 0, :, lane : lane + HD] = rope(
                k_ref[:, column : column + HD].astype(F32), cosine, sine
            ).astype(BF16)
        out_ref[dest, 1] = v_ref[:, dest * width : (dest + 1) * width]


def pack_q_body(q_ref, cos_ref, sin_ref, out_ref):
    cosine, sine = cos_ref[...] * SCORE_SCALE, sin_ref[...] * SCORE_SCALE
    width = out_ref.shape[2]
    for dest in range(out_ref.shape[0]):
        for lane in range(0, width, HD):
            column = dest * width + lane
            out_ref[dest, :, lane : lane + HD] = rope(
                q_ref[:, column : column + HD].astype(F32), cosine, sine
            ).astype(BF16)


def normed(rows, gain):
    rows = rows.astype(F32)
    return (
        rows * lax.rsqrt(jnp.mean(rows * rows, axis=-1, keepdims=True) + NORM_EPS) * gain.astype(F32)
    ).astype(BF16)


def project_body(
    embed_ref, mask_ref, gain_ref, wq_ref, wk_ref, wv_ref, cos_ref, sin_ref,
    qe_ref, qm_ref, ke_ref, km_ref, ve_ref, vm_ref, mq, mk,
):
    gain = gain_ref[...]

    @pl.when(pl.program_id(0) == 0)
    def _():
        mask_row = normed(jnp.broadcast_to(mask_ref[...], (16, mask_ref.shape[1])), gain)
        mq[...] = jnp.dot(mask_row, wq_ref[...], preferred_element_type=F32)
        mk[...] = jnp.dot(mask_row, wk_ref[...], preferred_element_type=F32)
        vm_ref[...] = jnp.dot(mask_row, wv_ref[...], preferred_element_type=F32).astype(BF16)

    rows = normed(embed_ref[...], gain)
    count = rows.shape[0]
    q = jnp.dot(rows, wq_ref[...], preferred_element_type=F32)
    k = jnp.dot(rows, wk_ref[...], preferred_element_type=F32)
    ve_ref[...] = jnp.dot(rows, wv_ref[...], preferred_element_type=F32).astype(BF16)
    cosine, sine = cos_ref[...], sin_ref[...]
    for lane in range(0, q.shape[1], HD):
        at = slice(lane, lane + HD)
        qe_ref[:, at] = (rope(q[:, at], cosine, sine) * SCORE_SCALE).astype(BF16)
        ke_ref[:, at] = rope(k[:, at], cosine, sine).astype(BF16)
        one_q = jnp.broadcast_to(mq[0:1, at], (count, HD))
        one_k = jnp.broadcast_to(mk[0:1, at], (count, HD))
        qm_ref[:, at] = (rope(one_q, cosine, sine) * SCORE_SCALE).astype(BF16)
        km_ref[:, at] = rope(one_k, cosine, sine).astype(BF16)


def scores(q, k):
    return lax.dot_general(q, k, (((1,), (1,)), ((), ())), preferred_element_type=F32)


def merge(state, s, v):
    top = jnp.max(s, axis=-1, keepdims=True)
    if state is None:
        w = jnp.exp2(s - top)
        return (
            top,
            jnp.sum(w, axis=-1, keepdims=True),
            jnp.dot(w.astype(BF16), v, preferred_element_type=F32),
        )
    old, total, acc = state
    top = jnp.maximum(old, top)
    keep = jnp.exp2(old - top)
    w = jnp.exp2(s - top)
    total = total * keep + jnp.sum(w, axis=-1, keepdims=True)
    acc = acc * keep + jnp.dot(w.astype(BF16), v, preferred_element_type=F32)
    return top, total, acc


def over_prompt(state, q, kv_ref, chunk):
    sources, _, rows, width = kv_ref.shape
    for first in range(0, sources, chunk):
        k = kv_ref[first : first + chunk, 0].reshape(chunk * rows, width)
        v = kv_ref[first : first + chunk, 1].reshape(chunk * rows, width)
        state = merge(state, scores(q, k), v)
    return state


def response_body(chunk, kept, place_ref, kv_ref, qe_ref, qm_ref, ke_ref, km_ref, ve_ref, vm_ref, commit_ref, *refs):
    out_refs, scratch_ref = refs[:-1], refs[-1]
    lows = len(out_refs)
    steps, blocks, per, _ = out_refs[0].shape
    low, bit = place_ref[0], place_ref[1]
    span_rows = lows * per
    count = blocks * span_rows
    side = bit if kept else 1 - bit

    def mine(ref):
        parts = [
            ref[pl.ds(pl.multiple_of((2 * block + side) * span_rows, span_rows), span_rows), :]
            for block in range(blocks)
        ]
        return jnp.concatenate(parts, 0) if blocks > 1 else parts[0]

    by_mask, by_embed, revealed = mine(qm_ref), mine(qe_ref), mine(commit_ref)
    both = over_prompt(None, jnp.concatenate([by_mask, by_embed], 0), kv_ref, chunk)
    mask_value = jnp.broadcast_to(vm_ref[0:1], ve_ref.shape)
    for step in range(steps):
        shown = revealed <= step
        one = revealed[:, 0:1] <= step
        shown_key = commit_ref[...] <= step
        q = jnp.where(shown, by_embed, by_mask)
        k = jnp.where(shown_key, ke_ref[...], km_ref[...])
        v = jnp.where(shown_key, ve_ref[...], mask_value)
        state = (
            jnp.where(one, both[0][count:], both[0][:count]),
            jnp.where(one, both[1][count:], both[1][:count]),
            jnp.where(shown, both[2][count:], both[2][:count]),
        )
        _, total, acc = merge(state, scores(q, k), v)
        scratch_ref[step] = acc * (1.0 / total)
    for step in range(steps):
        for block in range(blocks):
            for k in range(lows):
                at = block * span_rows + (low ^ k) * per
                out_refs[k][step, block] = scratch_ref[step, pl.ds(pl.multiple_of(at, per), per), :].astype(BF16)


def prompt_body(chunk, group, q_ref, kv_ref, km_ref, vm_ref, *refs):
    out_ref = refs[-1]
    sources, rows, width = q_ref.shape

    @pl.loop(0, sources // group)
    def _(turn):
        at = pl.ds(turn * group, group)
        q = q_ref[at].reshape(group * rows, width)
        s = scores(q, km_ref[...])
        top = jnp.max(s, axis=-1, keepdims=True)
        total = jnp.sum(jnp.exp2(s - top), axis=-1, keepdims=True)
        state = over_prompt((top, total, total * vm_ref[0:1].astype(F32)), q, kv_ref, chunk)
        out_ref[at] = (state[2] / state[1]).astype(BF16).reshape(group, rows, width)


def output_body(lows, split, place_ref, *refs):
    x_refs, refs = refs[:lows], refs[lows:]
    outs = refs[-STEPS:]
    steps, blocks, per, width = x_refs[0].shape
    far = lows // 2 if split else lows
    w = jnp.concatenate([ref[...] for ref in refs[:-STEPS]], 0)
    xs = []
    for k, x_ref in enumerate(x_refs):
        x = x_ref[...].reshape(steps * blocks * per, width)
        if k >= far:
            swapped = jnp.concatenate([x[:, width // 2 :], x[:, : width // 2]], 1)
            x = jnp.where(place_ref[2] == 0, x, swapped)
        xs.append(x)
    total = jnp.dot(jnp.concatenate(xs, 1), w, preferred_element_type=F32)
    for step, out_ref in enumerate(outs):
        for block in range(blocks):
            at = (step * blocks + block) * per
            out_ref[block] = total[at : at + per].astype(out_ref.dtype)


def halve_body(place_ref, keep_ref, got_ref, send_ref, kept_ref):
    bit = place_ref[0]
    for pair in range(send_ref.shape[0]):
        first = keep_ref[2 * pair] + got_ref[2 * pair].astype(F32)
        second = keep_ref[2 * pair + 1] + got_ref[2 * pair + 1].astype(F32)
        kept_ref[pair] = jnp.where(bit == 0, first, second)
        send_ref[pair] = jnp.where(bit == 0, second, first).astype(BF16)


def finish_body(step, place_ref, embed_ref, mask_ref, gain_ref, commit_ref, keep_ref, got_ref, *refs):
    residual_ref, normed_ref = refs[-2:]
    shown = commit_ref[:, 0:1] <= step
    rows = jnp.where(shown, embed_ref[...].astype(F32), mask_ref[...].astype(F32))
    hidden = rows + (keep_ref[0] + got_ref[0].astype(F32))
    residual_ref[0] = hidden.astype(BF16)
    scale = lax.rsqrt(jnp.mean(hidden * hidden, axis=-1, keepdims=True) + NORM_EPS)
    normed_ref[0] = (hidden * scale * gain_ref[...].astype(F32)).astype(BF16)


def unpack_body(in_ref, out_ref):
    width = in_ref.shape[2]
    for source in range(in_ref.shape[0]):
        out_ref[:, source * width : (source + 1) * width] = in_ref[source]


def per_device(
    prompt_query,
    prompt_key,
    prompt_value,
    response_embed,
    mask_embed,
    commit_step,
    block_index,
    attention_gain,
    residual_gain,
    query_weight,
    key_weight,
    value_weight,
    output_weight,
):
    rows, head_cols = prompt_query.shape
    resp, model = response_embed.shape
    n = lax.axis_size("seq")
    me = lax.axis_index("seq")
    width = query_weight.shape[1]
    heads = width // HD
    prompt_len = rows * n
    lows = min(4, n)
    highs = n // lows
    per = resp // n

    def swap(x, bit):
        return lax.ppermute(x, "seq", [(i, i ^ bit) for i in range(n)])

    dests = max(1, n // 4)
    cos_p, sin_p = tables(me * rows + jnp.arange(rows, dtype=jnp.int32))
    kv_send = call(
        pack_kv_body,
        (n // dests,),
        [
            pl.BlockSpec((rows, dests * width), lambda j: (0, j)),
            pl.BlockSpec((rows, dests * width), lambda j: (0, j)),
            whole((rows, HD)),
            whole((rows, HD)),
        ],
        pl.BlockSpec((dests, 2, rows, width), lambda j: (j, 0, 0, 0)),
        jax.ShapeDtypeStruct((n, 2, rows, width), BF16),
        flops=6 * rows * head_cols,
        moved=8 * rows * head_cols,
    )(prompt_key, prompt_value, cos_p, sin_p)
    kv = lax.all_to_all(kv_send, "seq", 0, 0, tiled=True)
    q_send = call(
        pack_q_body,
        (n // dests,),
        [
            pl.BlockSpec((rows, dests * width), lambda j: (0, j)),
            whole((rows, HD)),
            whole((rows, HD)),
        ],
        pl.BlockSpec((dests, rows, width), lambda j: (j, 0, 0)),
        jax.ShapeDtypeStruct((n, rows, width), BF16),
        flops=6 * rows * head_cols,
        moved=4 * rows * head_cols,
    )(prompt_query, cos_p, sin_p)
    q_heads = lax.all_to_all(q_send, "seq", 0, 0, tiled=True)

    groups = lax.axis_size("groups")
    group = lax.axis_index("groups")
    split = lows == 4 and groups % 2 == 0
    weights = [output_weight, swap(output_weight, 1)]
    if split:
        half_rows = lax.dynamic_slice_in_dim(output_weight, (group & 1) * (width // 2), width // 2, 0)
        fetched = swap(half_rows, 2)
        given = lax.ppermute(fetched, "groups", [(i, i ^ 1) for i in range(groups)])
        last = swap(fetched, 1)
        weights += [fetched, given, last, swap(given, 1)]
    elif lows == 4:
        far = swap(output_weight, 2)
        weights += [far, swap(far, 1)]

    cos_r, sin_r = tables(prompt_len + block_index[0] * resp + jnp.arange(resp, dtype=jnp.int32))
    commit = jnp.broadcast_to(commit_step[:, None], (resp, HD))
    block = min(resp, 128)
    row_block = pl.BlockSpec((block, width), lambda i: (i, 0))
    wide = jax.ShapeDtypeStruct((resp, width), BF16)
    qe, qm, ke, km, ve, vm = call(
        project_body,
        (resp // block,),
        [
            pl.BlockSpec((block, model), lambda i: (i, 0)),
            whole((1, model)),
            whole((1, model)),
            whole((model, width)),
            whole((model, width)),
            whole((model, width)),
            pl.BlockSpec((block, HD), lambda i: (i, 0)),
            pl.BlockSpec((block, HD), lambda i: (i, 0)),
        ],
        [row_block] * 5 + [whole((16, width))],
        [wide] * 5 + [jax.ShapeDtypeStruct((16, width), BF16)],
        scratch=[pltpu.VMEM((16, width), F32)] * 2,
        flops=6 * resp * model * width,
        moved=2 * resp * model + 6 * model * width,
    )(
        response_embed, mask_embed[None, :], attention_gain[None, :],
        query_weight, key_weight, value_weight, cos_r, sin_r,
    )

    chunk = max(1, min(n, 256 // rows))
    kv_block = pl.BlockSpec((n, 2, rows, HD), lambda h, *_: (0, 0, 0, h))
    key_block = pl.BlockSpec((resp, HD), lambda h, *_: (0, h))
    vm_block = pl.BlockSpec((16, HD), lambda h, *_: (0, h))
    low = me & (lows - 1)
    high = me >> (lows.bit_length() - 1)
    blocks = highs // 2
    place = jnp.stack([low, high & 1, group & 1]).astype(jnp.int32)
    columns = min(model, 1024)
    projected = {}
    for kept in (False, True):
        context = pl.pallas_call(
            functools.partial(response_body, chunk, kept),
            grid_spec=pltpu.PrefetchScalarGridSpec(
                num_scalar_prefetch=1,
                grid=(heads,),
                in_specs=[kv_block] + [key_block] * 5 + [vm_block, whole((resp, HD))],
                out_specs=[pl.BlockSpec((STEPS, blocks, per, HD), lambda h, *_: (0, 0, 0, h))] * lows,
                scratch_shapes=[pltpu.VMEM((STEPS, resp // 2, HD), F32)],
            ),
            out_shape=[jax.ShapeDtypeStruct((STEPS, blocks, per, width), BF16)] * lows,
            name="response_attention",
            cost_estimate=pl.CostEstimate(
                flops=2 * resp * width * (2 * prompt_len + STEPS * resp),
                bytes_accessed=4 * prompt_len * width,
                transcendentals=heads * resp * (2 * prompt_len + STEPS * resp) // 2,
            ),
        )(place, kv, qe, qm, ke, km, ve, vm, commit)
        plane_context = [context[0]]
        for k in range(1, lows):
            plane_context.append(swap(context[k], k))
        projected[kept] = pl.pallas_call(
            functools.partial(output_body, lows, split),
            grid_spec=pltpu.PrefetchScalarGridSpec(
                num_scalar_prefetch=1,
                grid=(model // columns,),
                in_specs=[whole((STEPS, blocks, per, width))] * lows
                + [pl.BlockSpec((w.shape[0], columns), lambda j, *_: (0, j)) for w in weights],
                out_specs=[pl.BlockSpec((blocks, per, columns), lambda j, *_: (0, 0, j))] * STEPS,
            ),
            out_shape=[jax.ShapeDtypeStruct((blocks, per, model), F32 if kept else BF16)] * STEPS,
            name="output_projection",
            cost_estimate=pl.CostEstimate(
                flops=STEPS * resp * model * width, bytes_accessed=2 * lows * width * model, transcendentals=0
            ),
        )(place, *plane_context, *weights)
    sends, keeps = projected[False], projected[True]

    level = 0
    while True:
        gots = []
        for step in range(STEPS):
            gots.append(swap(sends[step], lows << level))
        count = keeps[0].shape[0]
        if count == 1:
            break
        level += 1
        bit = ((high >> level) & 1).astype(jnp.int32).reshape(1)
        sends, kept = [], []
        for step in range(STEPS):
            columns = min(model, 2048)
            get = pl.BlockSpec((count, per, columns), lambda j, *_: (0, 0, j))
            put = pl.BlockSpec((count // 2, per, columns), lambda j, *_: (0, 0, j))
            one, two = pl.pallas_call(
                halve_body,
                grid_spec=pltpu.PrefetchScalarGridSpec(
                    num_scalar_prefetch=1,
                    grid=(model // columns,),
                    in_specs=[get, get],
                    out_specs=[put, put],
                ),
                out_shape=[
                    jax.ShapeDtypeStruct((count // 2, per, model), BF16),
                    jax.ShapeDtypeStruct((count // 2, per, model), F32),
                ],
                name="halve",
                cost_estimate=pl.CostEstimate(
                    flops=count * per * model, bytes_accessed=9 * count * per * model, transcendentals=0
                ),
            )(bit, keeps[step], gots[step])
            sends.append(one)
            kept.append(two)
        keeps = kept

    blocks_of_q = max(1, min(n, 1024 // rows))
    prompt_context = None
    for head in range(heads):
        of_head = functools.partial(lambda head, *_: (0, head), head)
        of_block = functools.partial(lambda head, *_: (0, 0, head), head)
        of_kv = functools.partial(lambda head, *_: (0, 0, 0, head), head)
        earlier = [] if prompt_context is None else [prompt_context]
        prompt_context = pl.pallas_call(
            functools.partial(prompt_body, chunk, blocks_of_q),
            grid=(1,),
            in_specs=[
                pl.BlockSpec((n, rows, HD), of_block),
                pl.BlockSpec((n, 2, rows, HD), of_kv),
                pl.BlockSpec((resp, HD), of_head),
                pl.BlockSpec((16, HD), of_head),
            ]
            + [pl.BlockSpec(memory_space=pl.ANY)] * len(earlier),
            out_specs=pl.BlockSpec((n, rows, HD), of_block),
            out_shape=jax.ShapeDtypeStruct((n, rows, width), BF16),
            name="prompt_attention",
            input_output_aliases={4: 0} if earlier else {},
            cost_estimate=pl.CostEstimate(
                flops=4 * prompt_len * HD * (prompt_len + resp),
                bytes_accessed=8 * prompt_len * HD,
                transcendentals=prompt_len * (prompt_len + resp),
            ),
        )(q_heads, kv, km, vm, *earlier)
    back = lax.all_to_all(prompt_context, "seq", 0, 0, tiled=True)

    results = []
    for step in range(STEPS):
        at_row = lambda i, at: (at[0], 0)
        at_step = functools.partial(lambda step, i, at: (step, 0, 0), step)
        one_row = pl.BlockSpec((1, model), lambda i, at: (0, 0))
        one_sum = pl.BlockSpec((1, per, model), lambda i, at: (0, 0, 0))
        results = pl.pallas_call(
            functools.partial(finish_body, step),
            grid_spec=pltpu.PrefetchScalarGridSpec(
                num_scalar_prefetch=1,
                grid=(1,),
                in_specs=[
                    pl.BlockSpec((per, model), at_row), one_row, one_row,
                    pl.BlockSpec((per, HD), at_row), one_sum, one_sum,
                ]
                + [pl.BlockSpec(memory_space=pl.ANY)] * len(results),
                out_specs=[pl.BlockSpec((1, per, model), at_step)] * 2,
            ),
            out_shape=[jax.ShapeDtypeStruct((STEPS, per, model), BF16)] * 2,
            name="finish",
            input_output_aliases={7: 0, 8: 1} if results else {},
            cost_estimate=pl.CostEstimate(flops=8 * per * model, bytes_accessed=12 * per * model, transcendentals=0),
        )(
            me.astype(jnp.int32).reshape(1), response_embed, mask_embed[None, :], residual_gain[None, :],
            commit, keeps[step], gots[step], *results,
        )
    residual, normed_rows = results
    columns = max(1, n // 4)
    prompt_out = call(
        unpack_body,
        (n // columns,),
        [pl.BlockSpec((columns, rows, width), lambda j: (j, 0, 0))],
        pl.BlockSpec((rows, columns * width), lambda j: (0, j)),
        jax.ShapeDtypeStruct((rows, head_cols), BF16),
        moved=4 * rows * head_cols,
    )(back)
    return prompt_out, residual, normed_rows


def solution(mesh):
    return jax.shard_map(
        per_device,
        mesh=mesh,
        in_specs=(
            P(("groups", "seq"), None),
            P(("groups", "seq"), None),
            P(("groups", "seq"), None),
            P("groups", None),
            P(),
            P("groups"),
            P("groups"),
            P(),
            P(),
            P(None, "seq"),
            P(None, "seq"),
            P(None, "seq"),
            P("seq", None),
        ),
        out_specs=(
            P(("groups", "seq"), None),
            P(None, ("groups", "seq"), None),
            P(None, ("groups", "seq"), None),
        ),
        check_vma=False,
    )
```

```python
import functools
import math

import jax
import jax.numpy as jnp
from jax import lax
from jax.experimental import pallas as pl
from jax.experimental.pallas import tpu as pltpu
from jax.sharding import PartitionSpec as P


HD = 128
STEPS = 4
ROPE_BASE = 500000.0
NORM_EPS = 1e-05
SCORE_SCALE = math.log2(math.e) / math.sqrt(HD)

F32 = jnp.float32
BF16 = jnp.bfloat16


def call(body, grid, in_specs, out_specs, out_shape, scratch=(), flops=0, moved=0, exps=0):
    return pl.pallas_call(
        body,
        grid=grid,
        in_specs=in_specs,
        out_specs=out_specs,
        out_shape=out_shape,
        scratch_shapes=list(scratch),
        cost_estimate=pl.CostEstimate(flops=flops, bytes_accessed=moved, transcendentals=exps),
    )


def whole(shape):
    return pl.BlockSpec(shape, lambda *_: (0,) * len(shape))


def tables(positions):
    half = HD // 2
    exponent = jnp.arange(half, dtype=F32) * (2.0 / HD)
    inv_freq = ROPE_BASE ** (-exponent)
    angles = positions.astype(F32)[:, None] * inv_freq[None, :]
    cosine, sine = jnp.cos(angles), jnp.sin(angles)
    return jnp.concatenate([cosine, cosine], 1), jnp.concatenate([-sine, sine], 1)


def rope(u, cosine, sine):
    return u * cosine + pltpu.roll(u, HD // 2, 1) * sine


def pack_kv_body(k_ref, v_ref, cos_ref, sin_ref, out_ref):
    cosine, sine = cos_ref[...], sin_ref[...]
    width = out_ref.shape[3]
    for dest in range(out_ref.shape[0]):
        for lane in range(0, width, HD):
            column = dest * width + lane
            out_ref[dest, 0, :, lane : lane + HD] = rope(
                k_ref[:, column : column + HD].astype(F32), cosine, sine
            ).astype(BF16)
        out_ref[dest, 1] = v_ref[:, dest * width : (dest + 1) * width]


def pack_q_body(q_ref, cos_ref, sin_ref, out_ref):
    cosine, sine = cos_ref[...] * SCORE_SCALE, sin_ref[...] * SCORE_SCALE
    width = out_ref.shape[2]
    for dest in range(out_ref.shape[0]):
        for lane in range(0, width, HD):
            column = dest * width + lane
            out_ref[dest, :, lane : lane + HD] = rope(
                q_ref[:, column : column + HD].astype(F32), cosine, sine
            ).astype(BF16)


def normed(rows, gain):
    rows = rows.astype(F32)
    return (
        rows * lax.rsqrt(jnp.mean(rows * rows, axis=-1, keepdims=True) + NORM_EPS) * gain.astype(F32)
    ).astype(BF16)


def project_body(
    embed_ref, mask_ref, gain_ref, wq_ref, wk_ref, wv_ref, cos_ref, sin_ref,
    qe_ref, qm_ref, ke_ref, km_ref, ve_ref, vm_ref, mq, mk,
):
    gain = gain_ref[...]

    @pl.when(pl.program_id(0) == 0)
    def _():
        mask_row = normed(jnp.broadcast_to(mask_ref[...], (16, mask_ref.shape[1])), gain)
        mq[...] = jnp.dot(mask_row, wq_ref[...], preferred_element_type=F32)
        mk[...] = jnp.dot(mask_row, wk_ref[...], preferred_element_type=F32)
        vm_ref[...] = jnp.dot(mask_row, wv_ref[...], preferred_element_type=F32).astype(BF16)

    rows = normed(embed_ref[...], gain)
    count = rows.shape[0]
    q = jnp.dot(rows, wq_ref[...], preferred_element_type=F32)
    k = jnp.dot(rows, wk_ref[...], preferred_element_type=F32)
    ve_ref[...] = jnp.dot(rows, wv_ref[...], preferred_element_type=F32).astype(BF16)
    cosine, sine = cos_ref[...], sin_ref[...]
    for lane in range(0, q.shape[1], HD):
        at = slice(lane, lane + HD)
        qe_ref[:, at] = (rope(q[:, at], cosine, sine) * SCORE_SCALE).astype(BF16)
        ke_ref[:, at] = rope(k[:, at], cosine, sine).astype(BF16)
        one_q = jnp.broadcast_to(mq[0:1, at], (count, HD))
        one_k = jnp.broadcast_to(mk[0:1, at], (count, HD))
        qm_ref[:, at] = (rope(one_q, cosine, sine) * SCORE_SCALE).astype(BF16)
        km_ref[:, at] = rope(one_k, cosine, sine).astype(BF16)


def scores(q, k):
    return lax.dot_general(q, k, (((1,), (1,)), ((), ())), preferred_element_type=F32)


def merge(state, s, v):
    top = jnp.max(s, axis=-1, keepdims=True)
    if state is None:
        w = jnp.exp2(s - top)
        return (
            top,
            jnp.sum(w, axis=-1, keepdims=True),
            jnp.dot(w.astype(BF16), v, preferred_element_type=F32),
        )
    old, total, acc = state
    top = jnp.maximum(old, top)
    keep = jnp.exp2(old - top)
    w = jnp.exp2(s - top)
    total = total * keep + jnp.sum(w, axis=-1, keepdims=True)
    acc = acc * keep + jnp.dot(w.astype(BF16), v, preferred_element_type=F32)
    return top, total, acc


def over_prompt(state, q, kv_ref, chunk):
    sources, _, rows, width = kv_ref.shape
    for first in range(0, sources, chunk):
        k = kv_ref[first : first + chunk, 0].reshape(chunk * rows, width)
        v = kv_ref[first : first + chunk, 1].reshape(chunk * rows, width)
        state = merge(state, scores(q, k), v)
    return state


def response_body(chunk, kept, place_ref, kv_ref, qe_ref, qm_ref, ke_ref, km_ref, ve_ref, vm_ref, commit_ref, *refs):
    out_refs, scratch_ref = refs[:-1], refs[-1]
    lows = len(out_refs)
    steps, blocks, per, _ = out_refs[0].shape
    low, bit = place_ref[0], place_ref[1]
    span_rows = lows * per
    count = blocks * span_rows
    side = bit if kept else 1 - bit

    def mine(ref):
        parts = [
            ref[pl.ds(pl.multiple_of((2 * block + side) * span_rows, span_rows), span_rows), :]
            for block in range(blocks)
        ]
        return jnp.concatenate(parts, 0) if blocks > 1 else parts[0]

    by_mask, by_embed, revealed = mine(qm_ref), mine(qe_ref), mine(commit_ref)
    both = over_prompt(None, jnp.concatenate([by_mask, by_embed], 0), kv_ref, chunk)
    mask_value = jnp.broadcast_to(vm_ref[0:1], ve_ref.shape)
    for step in range(steps):
        shown = revealed <= step
        one = revealed[:, 0:1] <= step
        shown_key = commit_ref[...] <= step
        q = jnp.where(shown, by_embed, by_mask)
        k = jnp.where(shown_key, ke_ref[...], km_ref[...])
        v = jnp.where(shown_key, ve_ref[...], mask_value)
        state = (
            jnp.where(one, both[0][count:], both[0][:count]),
            jnp.where(one, both[1][count:], both[1][:count]),
            jnp.where(shown, both[2][count:], both[2][:count]),
        )
        _, total, acc = merge(state, scores(q, k), v)
        scratch_ref[step] = acc * (1.0 / total)
    for step in range(steps):
        for block in range(blocks):
            for k in range(lows):
                at = block * span_rows + (low ^ k) * per
                out_refs[k][step, block] = scratch_ref[step, pl.ds(pl.multiple_of(at, per), per), :].astype(BF16)


def prompt_body(chunk, q_ref, kv_ref, km_ref, vm_ref, *refs):
    sources, rows, width = q_ref.shape
    q = q_ref[...].reshape(sources * rows, width)
    s = scores(q, km_ref[...])
    top = jnp.max(s, axis=-1, keepdims=True)
    total = jnp.sum(jnp.exp2(s - top), axis=-1, keepdims=True)
    state = over_prompt((top, total, total * vm_ref[0:1].astype(F32)), q, kv_ref, chunk)
    refs[-1][...] = (state[2] / state[1]).astype(BF16).reshape(sources, rows, width)


def output_body(lows, split, place_ref, *refs):
    x_refs, refs = refs[:lows], refs[lows:]
    outs = refs[-STEPS:]
    steps, blocks, per, width = x_refs[0].shape
    far = lows // 2 if split else lows
    w = jnp.concatenate([ref[...] for ref in refs[:-STEPS]], 0)
    xs = []
    for k, x_ref in enumerate(x_refs):
        x = x_ref[...].reshape(steps * blocks * per, width)
        if k >= far:
            swapped = jnp.concatenate([x[:, width // 2 :], x[:, : width // 2]], 1)
            x = jnp.where(place_ref[2] == 0, x, swapped)
        xs.append(x)
    total = jnp.dot(jnp.concatenate(xs, 1), w, preferred_element_type=F32)
    for step, out_ref in enumerate(outs):
        for block in range(blocks):
            at = (step * blocks + block) * per
            out_ref[block] = total[at : at + per].astype(out_ref.dtype)


def halve_body(place_ref, keep_ref, got_ref, send_ref, kept_ref):
    bit = place_ref[0]
    for pair in range(send_ref.shape[0]):
        first = keep_ref[2 * pair] + got_ref[2 * pair].astype(F32)
        second = keep_ref[2 * pair + 1] + got_ref[2 * pair + 1].astype(F32)
        kept_ref[pair] = jnp.where(bit == 0, first, second)
        send_ref[pair] = jnp.where(bit == 0, second, first).astype(BF16)


def finish_body(step, place_ref, embed_ref, mask_ref, gain_ref, commit_ref, keep_ref, got_ref, *refs):
    residual_ref, normed_ref = refs[-2:]
    shown = commit_ref[:, 0:1] <= step
    rows = jnp.where(shown, embed_ref[...].astype(F32), mask_ref[...].astype(F32))
    hidden = rows + (keep_ref[0] + got_ref[0].astype(F32))
    residual_ref[0] = hidden.astype(BF16)
    scale = lax.rsqrt(jnp.mean(hidden * hidden, axis=-1, keepdims=True) + NORM_EPS)
    normed_ref[0] = (hidden * scale * gain_ref[...].astype(F32)).astype(BF16)


def unpack_body(in_ref, out_ref):
    width = in_ref.shape[2]
    for source in range(in_ref.shape[0]):
        out_ref[:, source * width : (source + 1) * width] = in_ref[source]


def per_device(
    prompt_query,
    prompt_key,
    prompt_value,
    response_embed,
    mask_embed,
    commit_step,
    block_index,
    attention_gain,
    residual_gain,
    query_weight,
    key_weight,
    value_weight,
    output_weight,
):
    rows, head_cols = prompt_query.shape
    resp, model = response_embed.shape
    n = lax.axis_size("seq")
    me = lax.axis_index("seq")
    width = query_weight.shape[1]
    heads = width // HD
    prompt_len = rows * n
    lows = min(4, n)
    highs = n // lows
    per = resp // n

    def swap(x, bit):
        return lax.ppermute(x, "seq", [(i, i ^ bit) for i in range(n)])

    dests = max(1, n // 4)
    cos_p, sin_p = tables(me * rows + jnp.arange(rows, dtype=jnp.int32))
    kv_send = call(
        pack_kv_body,
        (n // dests,),
        [
            pl.BlockSpec((rows, dests * width), lambda j: (0, j)),
            pl.BlockSpec((rows, dests * width), lambda j: (0, j)),
            whole((rows, HD)),
            whole((rows, HD)),
        ],
        pl.BlockSpec((dests, 2, rows, width), lambda j: (j, 0, 0, 0)),
        jax.ShapeDtypeStruct((n, 2, rows, width), BF16),
        flops=6 * rows * head_cols,
        moved=8 * rows * head_cols,
    )(prompt_key, prompt_value, cos_p, sin_p)
    kv = lax.all_to_all(kv_send, "seq", 0, 0, tiled=True)
    q_send = call(
        pack_q_body,
        (n // dests,),
        [
            pl.BlockSpec((rows, dests * width), lambda j: (0, j)),
            whole((rows, HD)),
            whole((rows, HD)),
        ],
        pl.BlockSpec((dests, rows, width), lambda j: (j, 0, 0)),
        jax.ShapeDtypeStruct((n, rows, width), BF16),
        flops=6 * rows * head_cols,
        moved=4 * rows * head_cols,
    )(prompt_query, cos_p, sin_p)
    q_heads = lax.all_to_all(q_send, "seq", 0, 0, tiled=True)

    groups = lax.axis_size("groups")
    group = lax.axis_index("groups")
    split = lows == 4 and groups % 2 == 0
    weights = [output_weight, swap(output_weight, 1)]
    if split:
        half_rows = lax.dynamic_slice_in_dim(output_weight, (group & 1) * (width // 2), width // 2, 0)
        fetched = swap(half_rows, 2)
        given = lax.ppermute(fetched, "groups", [(i, i ^ 1) for i in range(groups)])
        last = swap(fetched, 1)
        weights += [fetched, given, last, swap(given, 1)]
    elif lows == 4:
        far = swap(output_weight, 2)
        weights += [far, swap(far, 1)]

    cos_r, sin_r = tables(prompt_len + block_index[0] * resp + jnp.arange(resp, dtype=jnp.int32))
    commit = jnp.broadcast_to(commit_step[:, None], (resp, HD))
    block = min(resp, 128)
    row_block = pl.BlockSpec((block, width), lambda i: (i, 0))
    wide = jax.ShapeDtypeStruct((resp, width), BF16)
    qe, qm, ke, km, ve, vm = call(
        project_body,
        (resp // block,),
        [
            pl.BlockSpec((block, model), lambda i: (i, 0)),
            whole((1, model)),
            whole((1, model)),
            whole((model, width)),
            whole((model, width)),
            whole((model, width)),
            pl.BlockSpec((block, HD), lambda i: (i, 0)),
            pl.BlockSpec((block, HD), lambda i: (i, 0)),
        ],
        [row_block] * 5 + [whole((16, width))],
        [wide] * 5 + [jax.ShapeDtypeStruct((16, width), BF16)],
        scratch=[pltpu.VMEM((16, width), F32)] * 2,
        flops=6 * resp * model * width,
        moved=2 * resp * model + 6 * model * width,
    )(
        response_embed, mask_embed[None, :], attention_gain[None, :],
        query_weight, key_weight, value_weight, cos_r, sin_r,
    )

    chunk = max(1, min(n, 256 // rows))
    kv_block = pl.BlockSpec((n, 2, rows, HD), lambda h, *_: (0, 0, 0, h))
    key_block = pl.BlockSpec((resp, HD), lambda h, *_: (0, h))
    vm_block = pl.BlockSpec((16, HD), lambda h, *_: (0, h))
    low = me & (lows - 1)
    high = me >> (lows.bit_length() - 1)
    blocks = highs // 2
    place = jnp.stack([low, high & 1, group & 1]).astype(jnp.int32)
    columns = min(model, 1024)
    projected = {}
    for kept in (False, True):
        context = pl.pallas_call(
            functools.partial(response_body, chunk, kept),
            grid_spec=pltpu.PrefetchScalarGridSpec(
                num_scalar_prefetch=1,
                grid=(heads,),
                in_specs=[kv_block] + [key_block] * 5 + [vm_block, whole((resp, HD))],
                out_specs=[pl.BlockSpec((STEPS, blocks, per, HD), lambda h, *_: (0, 0, 0, h))] * lows,
                scratch_shapes=[pltpu.VMEM((STEPS, resp // 2, HD), F32)],
            ),
            out_shape=[jax.ShapeDtypeStruct((STEPS, blocks, per, width), BF16)] * lows,
            name="response_attention",
            cost_estimate=pl.CostEstimate(
                flops=2 * resp * width * (2 * prompt_len + STEPS * resp),
                bytes_accessed=4 * prompt_len * width,
                transcendentals=heads * resp * (2 * prompt_len + STEPS * resp) // 2,
            ),
        )(place, kv, qe, qm, ke, km, ve, vm, commit)
        plane_context = [context[0]]
        for k in range(1, lows):
            plane_context.append(swap(context[k], k))
        projected[kept] = pl.pallas_call(
            functools.partial(output_body, lows, split),
            grid_spec=pltpu.PrefetchScalarGridSpec(
                num_scalar_prefetch=1,
                grid=(model // columns,),
                in_specs=[whole((STEPS, blocks, per, width))] * lows
                + [pl.BlockSpec((w.shape[0], columns), lambda j, *_: (0, j)) for w in weights],
                out_specs=[pl.BlockSpec((blocks, per, columns), lambda j, *_: (0, 0, j))] * STEPS,
            ),
            out_shape=[jax.ShapeDtypeStruct((blocks, per, model), F32 if kept else BF16)] * STEPS,
            name="output_projection",
            cost_estimate=pl.CostEstimate(
                flops=STEPS * resp * model * width, bytes_accessed=2 * lows * width * model, transcendentals=0
            ),
        )(place, *plane_context, *weights)
    sends, keeps = projected[False], projected[True]

    level = 0
    while True:
        gots = []
        for step in range(STEPS):
            gots.append(swap(sends[step], lows << level))
        count = keeps[0].shape[0]
        if count == 1:
            break
        level += 1
        bit = ((high >> level) & 1).astype(jnp.int32).reshape(1)
        sends, kept = [], []
        for step in range(STEPS):
            columns = min(model, 2048)
            get = pl.BlockSpec((count, per, columns), lambda j, *_: (0, 0, j))
            put = pl.BlockSpec((count // 2, per, columns), lambda j, *_: (0, 0, j))
            one, two = pl.pallas_call(
                halve_body,
                grid_spec=pltpu.PrefetchScalarGridSpec(
                    num_scalar_prefetch=1,
                    grid=(model // columns,),
                    in_specs=[get, get],
                    out_specs=[put, put],
                ),
                out_shape=[
                    jax.ShapeDtypeStruct((count // 2, per, model), BF16),
                    jax.ShapeDtypeStruct((count // 2, per, model), F32),
                ],
                name="halve",
                cost_estimate=pl.CostEstimate(
                    flops=count * per * model, bytes_accessed=9 * count * per * model, transcendentals=0
                ),
            )(bit, keeps[step], gots[step])
            sends.append(one)
            kept.append(two)
        keeps = kept

    blocks_of_q = max(1, min(n, 1024 // rows))
    prompt_context = None
    for head in range(heads):
        of_head = functools.partial(lambda head, *_: (0, head), head)
        of_kv = functools.partial(lambda head, *_: (0, 0, 0, head), head)
        for turn in range(n // blocks_of_q):
            of_block = functools.partial(lambda head, turn, *_: (turn, 0, head), head, turn)
            earlier = [] if prompt_context is None else [prompt_context]
            prompt_context = pl.pallas_call(
                functools.partial(prompt_body, chunk),
                grid=(1,),
                in_specs=[
                    pl.BlockSpec((blocks_of_q, rows, HD), of_block),
                    pl.BlockSpec((n, 2, rows, HD), of_kv),
                    pl.BlockSpec((resp, HD), of_head),
                    pl.BlockSpec((16, HD), of_head),
                ]
                + [pl.BlockSpec(memory_space=pl.ANY)] * len(earlier),
                out_specs=pl.BlockSpec((blocks_of_q, rows, HD), of_block),
                out_shape=jax.ShapeDtypeStruct((n, rows, width), BF16),
                name="prompt_attention",
                input_output_aliases={4: 0} if earlier else {},
                cost_estimate=pl.CostEstimate(
                    flops=4 * blocks_of_q * rows * HD * (prompt_len + resp),
                    bytes_accessed=4 * prompt_len * HD + 4 * blocks_of_q * rows * HD,
                    transcendentals=blocks_of_q * rows * (prompt_len + resp),
                ),
            )(q_heads, kv, km, vm, *earlier)
    back = lax.all_to_all(prompt_context, "seq", 0, 0, tiled=True)

    results = []
    for step in range(STEPS):
        at_row = lambda i, at: (at[0], 0)
        at_step = functools.partial(lambda step, i, at: (step, 0, 0), step)
        one_row = pl.BlockSpec((1, model), lambda i, at: (0, 0))
        one_sum = pl.BlockSpec((1, per, model), lambda i, at: (0, 0, 0))
        results = pl.pallas_call(
            functools.partial(finish_body, step),
            grid_spec=pltpu.PrefetchScalarGridSpec(
                num_scalar_prefetch=1,
                grid=(1,),
                in_specs=[
                    pl.BlockSpec((per, model), at_row), one_row, one_row,
                    pl.BlockSpec((per, HD), at_row), one_sum, one_sum,
                ]
                + [pl.BlockSpec(memory_space=pl.ANY)] * len(results),
                out_specs=[pl.BlockSpec((1, per, model), at_step)] * 2,
            ),
            out_shape=[jax.ShapeDtypeStruct((STEPS, per, model), BF16)] * 2,
            name="finish",
            input_output_aliases={7: 0, 8: 1} if results else {},
            cost_estimate=pl.CostEstimate(flops=8 * per * model, bytes_accessed=12 * per * model, transcendentals=0),
        )(
            me.astype(jnp.int32).reshape(1), response_embed, mask_embed[None, :], residual_gain[None, :],
            commit, keeps[step], gots[step], *results,
        )
    residual, normed_rows = results
    columns = max(1, n // 4)
    prompt_out = call(
        unpack_body,
        (n // columns,),
        [pl.BlockSpec((columns, rows, width), lambda j: (j, 0, 0))],
        pl.BlockSpec((rows, columns * width), lambda j: (0, j)),
        jax.ShapeDtypeStruct((rows, head_cols), BF16),
        moved=4 * rows * head_cols,
    )(back)
    return prompt_out, residual, normed_rows


def solution(mesh):
    return jax.shard_map(
        per_device,
        mesh=mesh,
        in_specs=(
            P(("groups", "seq"), None),
            P(("groups", "seq"), None),
            P(("groups", "seq"), None),
            P("groups", None),
            P(),
            P("groups"),
            P("groups"),
            P(),
            P(),
            P(None, "seq"),
            P(None, "seq"),
            P(None, "seq"),
            P("seq", None),
        ),
        out_specs=(
            P(("groups", "seq"), None),
            P(None, ("groups", "seq"), None),
            P(None, ("groups", "seq"), None),
        ),
        check_vma=False,
    )
```

```python
import functools
import math

import jax
import jax.numpy as jnp
from jax import lax
from jax.experimental import pallas as pl
from jax.experimental.pallas import tpu as pltpu
from jax.sharding import PartitionSpec as P


HD = 128
STEPS = 4
ROPE_BASE = 500000.0
NORM_EPS = 1e-05
SCORE_SCALE = math.log2(math.e) / math.sqrt(HD)

F32 = jnp.float32
BF16 = jnp.bfloat16


GRANT = pltpu.CompilerParams(vmem_limit_bytes=28 << 20)


def call(body, grid, in_specs, out_specs, out_shape, scratch=(), flops=0, moved=0, exps=0):
    return pl.pallas_call(
        body,
        grid=grid,
        in_specs=in_specs,
        out_specs=out_specs,
        out_shape=out_shape,
        scratch_shapes=list(scratch),
        compiler_params=GRANT,
        cost_estimate=pl.CostEstimate(flops=flops, bytes_accessed=moved, transcendentals=exps),
    )


def whole(shape):
    return pl.BlockSpec(shape, lambda *_: (0,) * len(shape))


def tables(positions):
    half = HD // 2
    exponent = jnp.arange(half, dtype=F32) * (2.0 / HD)
    inv_freq = ROPE_BASE ** (-exponent)
    angles = positions.astype(F32)[:, None] * inv_freq[None, :]
    cosine, sine = jnp.cos(angles), jnp.sin(angles)
    return jnp.concatenate([cosine, cosine], 1), jnp.concatenate([-sine, sine], 1)


def rope(u, cosine, sine):
    return u * cosine + pltpu.roll(u, HD // 2, 1) * sine


def pack_kv_body(k_ref, v_ref, cos_ref, sin_ref, out_ref):
    cosine, sine = cos_ref[...], sin_ref[...]
    width = out_ref.shape[3]
    for dest in range(out_ref.shape[0]):
        for lane in range(0, width, HD):
            column = dest * width + lane
            out_ref[dest, 0, :, lane : lane + HD] = rope(
                k_ref[:, column : column + HD].astype(F32), cosine, sine
            ).astype(BF16)
        out_ref[dest, 1] = v_ref[:, dest * width : (dest + 1) * width]


def pack_q_body(q_ref, cos_ref, sin_ref, out_ref):
    cosine, sine = cos_ref[...] * SCORE_SCALE, sin_ref[...] * SCORE_SCALE
    width = out_ref.shape[2]
    for dest in range(out_ref.shape[0]):
        for lane in range(0, width, HD):
            column = dest * width + lane
            out_ref[dest, :, lane : lane + HD] = rope(
                q_ref[:, column : column + HD].astype(F32), cosine, sine
            ).astype(BF16)


def normed(rows, gain):
    rows = rows.astype(F32)
    return (
        rows * lax.rsqrt(jnp.mean(rows * rows, axis=-1, keepdims=True) + NORM_EPS) * gain.astype(F32)
    ).astype(BF16)


def project_body(
    embed_ref, mask_ref, gain_ref, wq_ref, wk_ref, wv_ref, cos_ref, sin_ref,
    qe_ref, qm_ref, ke_ref, km_ref, ve_ref, vm_ref, mq, mk,
):
    gain = gain_ref[...]

    @pl.when(pl.program_id(0) == 0)
    def _():
        mask_row = normed(jnp.broadcast_to(mask_ref[...], (16, mask_ref.shape[1])), gain)
        mq[...] = jnp.dot(mask_row, wq_ref[...], preferred_element_type=F32)
        mk[...] = jnp.dot(mask_row, wk_ref[...], preferred_element_type=F32)
        vm_ref[...] = jnp.dot(mask_row, wv_ref[...], preferred_element_type=F32).astype(BF16)

    rows = normed(embed_ref[...], gain)
    count = rows.shape[0]
    q = jnp.dot(rows, wq_ref[...], preferred_element_type=F32)
    k = jnp.dot(rows, wk_ref[...], preferred_element_type=F32)
    ve_ref[...] = jnp.dot(rows, wv_ref[...], preferred_element_type=F32).astype(BF16)
    cosine, sine = cos_ref[...], sin_ref[...]
    for lane in range(0, q.shape[1], HD):
        at = slice(lane, lane + HD)
        qe_ref[:, at] = (rope(q[:, at], cosine, sine) * SCORE_SCALE).astype(BF16)
        ke_ref[:, at] = rope(k[:, at], cosine, sine).astype(BF16)
        one_q = jnp.broadcast_to(mq[0:1, at], (count, HD))
        one_k = jnp.broadcast_to(mk[0:1, at], (count, HD))
        qm_ref[:, at] = (rope(one_q, cosine, sine) * SCORE_SCALE).astype(BF16)
        km_ref[:, at] = rope(one_k, cosine, sine).astype(BF16)


def scores(q, k):
    return lax.dot_general(q, k, (((1,), (1,)), ((), ())), preferred_element_type=F32)


def merge(state, s, v):
    top = jnp.max(s, axis=-1, keepdims=True)
    if state is None:
        w = jnp.exp2(s - top)
        return (
            top,
            jnp.sum(w, axis=-1, keepdims=True),
            jnp.dot(w.astype(BF16), v, preferred_element_type=F32),
        )
    old, total, acc = state
    top = jnp.maximum(old, top)
    keep = jnp.exp2(old - top)
    w = jnp.exp2(s - top)
    total = total * keep + jnp.sum(w, axis=-1, keepdims=True)
    acc = acc * keep + jnp.dot(w.astype(BF16), v, preferred_element_type=F32)
    return top, total, acc


def over_prompt(state, q, kv_ref, chunk):
    sources, _, rows, width = kv_ref.shape
    for first in range(0, sources, chunk):
        k = kv_ref[first : first + chunk, 0].reshape(chunk * rows, width)
        v = kv_ref[first : first + chunk, 1].reshape(chunk * rows, width)
        state = merge(state, scores(q, k), v)
    return state


def response_body(chunk, kept, place_ref, kv_ref, qe_ref, qm_ref, ke_ref, km_ref, ve_ref, vm_ref, commit_ref, *refs):
    out_refs, scratch_ref = refs[:-1], refs[-1]
    lows = len(out_refs)
    steps, blocks, per, _ = out_refs[0].shape
    low, bit = place_ref[0], place_ref[1]
    span_rows = lows * per
    count = blocks * span_rows
    side = bit if kept else 1 - bit

    def mine(ref):
        parts = [
            ref[pl.ds(pl.multiple_of((2 * block + side) * span_rows, span_rows), span_rows), :]
            for block in range(blocks)
        ]
        return jnp.concatenate(parts, 0) if blocks > 1 else parts[0]

    by_mask, by_embed, revealed = mine(qm_ref), mine(qe_ref), mine(commit_ref)
    both = over_prompt(None, jnp.concatenate([by_mask, by_embed], 0), kv_ref, chunk)
    mask_value = jnp.broadcast_to(vm_ref[0:1], ve_ref.shape)
    for step in range(steps):
        shown = revealed <= step
        one = revealed[:, 0:1] <= step
        shown_key = commit_ref[...] <= step
        q = jnp.where(shown, by_embed, by_mask)
        k = jnp.where(shown_key, ke_ref[...], km_ref[...])
        v = jnp.where(shown_key, ve_ref[...], mask_value)
        state = (
            jnp.where(one, both[0][count:], both[0][:count]),
            jnp.where(one, both[1][count:], both[1][:count]),
            jnp.where(shown, both[2][count:], both[2][:count]),
        )
        _, total, acc = merge(state, scores(q, k), v)
        scratch_ref[step] = acc * (1.0 / total)
    for step in range(steps):
        for block in range(blocks):
            for k in range(lows):
                at = block * span_rows + (low ^ k) * per
                out_refs[k][step, block] = scratch_ref[step, pl.ds(pl.multiple_of(at, per), per), :].astype(BF16)


def prompt_body(chunk, q_ref, kv_ref, km_ref, vm_ref, *refs):
    sources, rows, width = q_ref.shape
    q = q_ref[...].reshape(sources * rows, width)
    s = scores(q, km_ref[...])
    top = jnp.max(s, axis=-1, keepdims=True)
    total = jnp.sum(jnp.exp2(s - top), axis=-1, keepdims=True)
    state = over_prompt((top, total, total * vm_ref[0:1].astype(F32)), q, kv_ref, chunk)
    refs[-1][...] = (state[2] / state[1]).astype(BF16).reshape(sources, rows, width)


def output_body(lows, split, place_ref, *refs):
    x_refs, refs = refs[:lows], refs[lows:]
    outs = refs[-STEPS:]
    steps, blocks, per, width = x_refs[0].shape
    far = lows // 2 if split else lows
    columns = outs[0].shape[2]
    here = pl.ds(pl.multiple_of(pl.program_id(0) * columns, columns), columns)
    w = jnp.concatenate([ref[:, here] for ref in refs[:-STEPS]], 0)
    xs = []
    for k, x_ref in enumerate(x_refs):
        x = x_ref[...].reshape(steps * blocks * per, width)
        if k >= far:
            swapped = jnp.concatenate([x[:, width // 2 :], x[:, : width // 2]], 1)
            x = jnp.where(place_ref[2] == 0, x, swapped)
        xs.append(x)
    total = jnp.dot(jnp.concatenate(xs, 1), w, preferred_element_type=F32)
    for step, out_ref in enumerate(outs):
        for block in range(blocks):
            at = (step * blocks + block) * per
            out_ref[block] = total[at : at + per].astype(out_ref.dtype)


def halve_body(place_ref, keep_ref, got_ref, send_ref, kept_ref):
    bit = place_ref[0]
    for pair in range(send_ref.shape[0]):
        first = keep_ref[2 * pair] + got_ref[2 * pair].astype(F32)
        second = keep_ref[2 * pair + 1] + got_ref[2 * pair + 1].astype(F32)
        kept_ref[pair] = jnp.where(bit == 0, first, second)
        send_ref[pair] = jnp.where(bit == 0, second, first).astype(BF16)


def finish_body(step, place_ref, embed_ref, mask_ref, gain_ref, commit_ref, keep_ref, got_ref, *refs):
    residual_ref, normed_ref = refs[-2:]
    shown = commit_ref[:, 0:1] <= step
    rows = jnp.where(shown, embed_ref[...].astype(F32), mask_ref[...].astype(F32))
    hidden = rows + (keep_ref[0] + got_ref[0].astype(F32))
    residual_ref[0] = hidden.astype(BF16)
    scale = lax.rsqrt(jnp.mean(hidden * hidden, axis=-1, keepdims=True) + NORM_EPS)
    normed_ref[0] = (hidden * scale * gain_ref[...].astype(F32)).astype(BF16)


def unpack_body(in_ref, out_ref):
    width = in_ref.shape[2]
    for source in range(in_ref.shape[0]):
        out_ref[:, source * width : (source + 1) * width] = in_ref[source]


def per_device(
    prompt_query,
    prompt_key,
    prompt_value,
    response_embed,
    mask_embed,
    commit_step,
    block_index,
    attention_gain,
    residual_gain,
    query_weight,
    key_weight,
    value_weight,
    output_weight,
):
    rows, head_cols = prompt_query.shape
    resp, model = response_embed.shape
    n = lax.axis_size("seq")
    me = lax.axis_index("seq")
    width = query_weight.shape[1]
    heads = width // HD
    prompt_len = rows * n
    lows = min(4, n)
    highs = n // lows
    per = resp // n

    def swap(x, bit):
        return lax.ppermute(x, "seq", [(i, i ^ bit) for i in range(n)])

    dests = max(1, n // 4)
    cos_p, sin_p = tables(me * rows + jnp.arange(rows, dtype=jnp.int32))
    kv_send = call(
        pack_kv_body,
        (n // dests,),
        [
            pl.BlockSpec((rows, dests * width), lambda j: (0, j)),
            pl.BlockSpec((rows, dests * width), lambda j: (0, j)),
            whole((rows, HD)),
            whole((rows, HD)),
        ],
        pl.BlockSpec((dests, 2, rows, width), lambda j: (j, 0, 0, 0)),
        jax.ShapeDtypeStruct((n, 2, rows, width), BF16),
        flops=6 * rows * head_cols,
        moved=8 * rows * head_cols,
    )(prompt_key, prompt_value, cos_p, sin_p)
    kv = lax.all_to_all(kv_send, "seq", 0, 0, tiled=True)
    q_send = call(
        pack_q_body,
        (n // dests,),
        [
            pl.BlockSpec((rows, dests * width), lambda j: (0, j)),
            whole((rows, HD)),
            whole((rows, HD)),
        ],
        pl.BlockSpec((dests, rows, width), lambda j: (j, 0, 0)),
        jax.ShapeDtypeStruct((n, rows, width), BF16),
        flops=6 * rows * head_cols,
        moved=4 * rows * head_cols,
    )(prompt_query, cos_p, sin_p)
    q_heads = lax.all_to_all(q_send, "seq", 0, 0, tiled=True)

    groups = lax.axis_size("groups")
    group = lax.axis_index("groups")
    split = lows == 4 and groups % 2 == 0
    weights = [output_weight, swap(output_weight, 1)]
    if split:
        half_rows = lax.dynamic_slice_in_dim(output_weight, (group & 1) * (width // 2), width // 2, 0)
        fetched = swap(half_rows, 2)
        given = lax.ppermute(fetched, "groups", [(i, i ^ 1) for i in range(groups)])
        last = swap(fetched, 1)
        weights += [fetched, given, last, swap(given, 1)]
    elif lows == 4:
        far = swap(output_weight, 2)
        weights += [far, swap(far, 1)]

    cos_r, sin_r = tables(prompt_len + block_index[0] * resp + jnp.arange(resp, dtype=jnp.int32))
    commit = jnp.broadcast_to(commit_step[:, None], (resp, HD))
    block = min(resp, 128)
    row_block = pl.BlockSpec((block, width), lambda i: (i, 0))
    wide = jax.ShapeDtypeStruct((resp, width), BF16)
    qe, qm, ke, km, ve, vm = call(
        project_body,
        (resp // block,),
        [
            pl.BlockSpec((block, model), lambda i: (i, 0)),
            whole((1, model)),
            whole((1, model)),
            whole((model, width)),
            whole((model, width)),
            whole((model, width)),
            pl.BlockSpec((block, HD), lambda i: (i, 0)),
            pl.BlockSpec((block, HD), lambda i: (i, 0)),
        ],
        [row_block] * 5 + [whole((16, width))],
        [wide] * 5 + [jax.ShapeDtypeStruct((16, width), BF16)],
        scratch=[pltpu.VMEM((16, width), F32)] * 2,
        flops=6 * resp * model * width,
        moved=2 * resp * model + 6 * model * width,
    )(
        response_embed, mask_embed[None, :], attention_gain[None, :],
        query_weight, key_weight, value_weight, cos_r, sin_r,
    )

    chunk = max(1, min(n, 256 // rows))
    kv_block = pl.BlockSpec((n, 2, rows, HD), lambda h, *_: (0, 0, 0, h))
    key_block = pl.BlockSpec((resp, HD), lambda h, *_: (0, h))
    vm_block = pl.BlockSpec((16, HD), lambda h, *_: (0, h))
    low = me & (lows - 1)
    high = me >> (lows.bit_length() - 1)
    blocks = highs // 2
    place = jnp.stack([low, high & 1, group & 1]).astype(jnp.int32)
    columns = min(model, 1024)
    projected = {}
    for kept in (False, True):
        context = pl.pallas_call(
            functools.partial(response_body, chunk, kept),
            grid_spec=pltpu.PrefetchScalarGridSpec(
                num_scalar_prefetch=1,
                grid=(heads,),
                in_specs=[kv_block] + [key_block] * 5 + [vm_block, whole((resp, HD))],
                out_specs=[pl.BlockSpec((STEPS, blocks, per, HD), lambda h, *_: (0, 0, 0, h))] * lows,
                scratch_shapes=[pltpu.VMEM((STEPS, resp // 2, HD), F32)],
            ),
            out_shape=[jax.ShapeDtypeStruct((STEPS, blocks, per, width), BF16)] * lows,
            name="response_attention",
            compiler_params=GRANT,
            cost_estimate=pl.CostEstimate(
                flops=2 * resp * width * (2 * prompt_len + STEPS * resp),
                bytes_accessed=4 * prompt_len * width,
                transcendentals=heads * resp * (2 * prompt_len + STEPS * resp) // 2,
            ),
        )(place, kv, qe, qm, ke, km, ve, vm, commit)
        plane_context = [context[0]]
        for k in range(1, lows):
            plane_context.append(swap(context[k], k))
        projected[kept] = pl.pallas_call(
            functools.partial(output_body, lows, split),
            grid_spec=pltpu.PrefetchScalarGridSpec(
                num_scalar_prefetch=1,
                grid=(model // columns,),
                in_specs=[whole((STEPS, blocks, per, width))] * lows
                + [pl.BlockSpec(memory_space=pltpu.VMEM)] * len(weights),
                out_specs=[pl.BlockSpec((blocks, per, columns), lambda j, *_: (0, 0, j))] * STEPS,
            ),
            out_shape=[jax.ShapeDtypeStruct((blocks, per, model), F32 if kept else BF16)] * STEPS,
            name="output_projection",
            compiler_params=GRANT,
            cost_estimate=pl.CostEstimate(
                flops=STEPS * resp * model * width, bytes_accessed=2 * lows * width * model, transcendentals=0
            ),
        )(place, *plane_context, *weights)
    sends, keeps = projected[False], projected[True]

    level = 0
    while True:
        gots = []
        for step in range(STEPS):
            gots.append(swap(sends[step], lows << level))
        count = keeps[0].shape[0]
        if count == 1:
            break
        level += 1
        bit = ((high >> level) & 1).astype(jnp.int32).reshape(1)
        sends, kept = [], []
        for step in range(STEPS):
            columns = model
            get = pl.BlockSpec((count, per, columns), lambda j, *_: (0, 0, j))
            put = pl.BlockSpec((count // 2, per, columns), lambda j, *_: (0, 0, j))
            one, two = pl.pallas_call(
                halve_body,
                grid_spec=pltpu.PrefetchScalarGridSpec(
                    num_scalar_prefetch=1,
                    grid=(model // columns,),
                    in_specs=[get, get],
                    out_specs=[put, put],
                ),
                out_shape=[
                    jax.ShapeDtypeStruct((count // 2, per, model), BF16),
                    jax.ShapeDtypeStruct((count // 2, per, model), F32),
                ],
                name="halve",
                compiler_params=GRANT,
                cost_estimate=pl.CostEstimate(
                    flops=count * per * model, bytes_accessed=9 * count * per * model, transcendentals=0
                ),
            )(bit, keeps[step], gots[step])
            sends.append(one)
            kept.append(two)
        keeps = kept

    blocks_of_q = max(1, min(n, 1024 // rows))
    prompt_context = None
    for head in range(heads):
        of_head = functools.partial(lambda head, *_: (0, head), head)
        of_kv = functools.partial(lambda head, *_: (0, 0, 0, head), head)
        for turn in range(n // blocks_of_q):
            of_block = functools.partial(lambda head, turn, *_: (turn, 0, head), head, turn)
            earlier = [] if prompt_context is None else [prompt_context]
            prompt_context = pl.pallas_call(
                functools.partial(prompt_body, chunk),
                grid=(1,),
                in_specs=[
                    pl.BlockSpec((blocks_of_q, rows, HD), of_block),
                    pl.BlockSpec((n, 2, rows, HD), of_kv),
                    pl.BlockSpec((resp, HD), of_head),
                    pl.BlockSpec((16, HD), of_head),
                ]
                + [pl.BlockSpec(memory_space=pl.ANY)] * len(earlier),
                out_specs=pl.BlockSpec((blocks_of_q, rows, HD), of_block),
                out_shape=jax.ShapeDtypeStruct((n, rows, width), BF16),
                name="prompt_attention",
                compiler_params=GRANT,
                input_output_aliases={4: 0} if earlier else {},
                cost_estimate=pl.CostEstimate(
                    flops=4 * blocks_of_q * rows * HD * (prompt_len + resp),
                    bytes_accessed=4 * prompt_len * HD + 4 * blocks_of_q * rows * HD,
                    transcendentals=blocks_of_q * rows * (prompt_len + resp),
                ),
            )(q_heads, kv, km, vm, *earlier)
    back = lax.all_to_all(prompt_context, "seq", 0, 0, tiled=True)

    results = []
    for step in range(STEPS):
        at_row = lambda i, at: (at[0], 0)
        at_step = functools.partial(lambda step, i, at: (step, 0, 0), step)
        one_row = pl.BlockSpec((1, model), lambda i, at: (0, 0))
        one_sum = pl.BlockSpec((1, per, model), lambda i, at: (0, 0, 0))
        results = pl.pallas_call(
            functools.partial(finish_body, step),
            grid_spec=pltpu.PrefetchScalarGridSpec(
                num_scalar_prefetch=1,
                grid=(1,),
                in_specs=[
                    pl.BlockSpec((per, model), at_row), one_row, one_row,
                    pl.BlockSpec((per, HD), at_row), one_sum, one_sum,
                ]
                + [pl.BlockSpec(memory_space=pl.ANY)] * len(results),
                out_specs=[pl.BlockSpec((1, per, model), at_step)] * 2,
            ),
            out_shape=[jax.ShapeDtypeStruct((STEPS, per, model), BF16)] * 2,
            name="finish",
            compiler_params=GRANT,
            input_output_aliases={7: 0, 8: 1} if results else {},
            cost_estimate=pl.CostEstimate(flops=8 * per * model, bytes_accessed=12 * per * model, transcendentals=0),
        )(
            me.astype(jnp.int32).reshape(1), response_embed, mask_embed[None, :], residual_gain[None, :],
            commit, keeps[step], gots[step], *results,
        )
    residual, normed_rows = results
    columns = max(1, n // 4)
    prompt_out = call(
        unpack_body,
        (n // columns,),
        [pl.BlockSpec((columns, rows, width), lambda j: (j, 0, 0))],
        pl.BlockSpec((rows, columns * width), lambda j: (0, j)),
        jax.ShapeDtypeStruct((rows, head_cols), BF16),
        moved=4 * rows * head_cols,
    )(back)
    return prompt_out, residual, normed_rows


def solution(mesh):
    return jax.shard_map(
        per_device,
        mesh=mesh,
        in_specs=(
            P(("groups", "seq"), None),
            P(("groups", "seq"), None),
            P(("groups", "seq"), None),
            P("groups", None),
            P(),
            P("groups"),
            P("groups"),
            P(),
            P(),
            P(None, "seq"),
            P(None, "seq"),
            P(None, "seq"),
            P("seq", None),
        ),
        out_specs=(
            P(("groups", "seq"), None),
            P(None, ("groups", "seq"), None),
            P(None, ("groups", "seq"), None),
        ),
        check_vma=False,
    )
```

```python
import functools
import math

import jax
import jax.numpy as jnp
from jax import lax
from jax.experimental import pallas as pl
from jax.experimental.pallas import tpu as pltpu
from jax.sharding import PartitionSpec as P


HD = 128
STEPS = 4
ROPE_BASE = 500000.0
NORM_EPS = 1e-05
SCORE_SCALE = math.log2(math.e) / math.sqrt(HD)

F32 = jnp.float32
BF16 = jnp.bfloat16


GRANT = pltpu.CompilerParams(vmem_limit_bytes=28 << 20)


def call(body, grid, in_specs, out_specs, out_shape, scratch=(), flops=0, moved=0, exps=0):
    return pl.pallas_call(
        body,
        grid=grid,
        in_specs=in_specs,
        out_specs=out_specs,
        out_shape=out_shape,
        scratch_shapes=list(scratch),
        cost_estimate=pl.CostEstimate(flops=flops, bytes_accessed=moved, transcendentals=exps),
    )


def whole(shape):
    return pl.BlockSpec(shape, lambda *_: (0,) * len(shape))


def tables(positions):
    half = HD // 2
    exponent = jnp.arange(half, dtype=F32) * (2.0 / HD)
    inv_freq = ROPE_BASE ** (-exponent)
    angles = positions.astype(F32)[:, None] * inv_freq[None, :]
    cosine, sine = jnp.cos(angles), jnp.sin(angles)
    return jnp.concatenate([cosine, cosine], 1), jnp.concatenate([-sine, sine], 1)


def rope(u, cosine, sine):
    return u * cosine + pltpu.roll(u, HD // 2, 1) * sine


def pack_kv_body(k_ref, v_ref, cos_ref, sin_ref, out_ref):
    cosine, sine = cos_ref[...], sin_ref[...]
    width = out_ref.shape[3]
    for dest in range(out_ref.shape[0]):
        for lane in range(0, width, HD):
            column = dest * width + lane
            out_ref[dest, 0, :, lane : lane + HD] = rope(
                k_ref[:, column : column + HD].astype(F32), cosine, sine
            ).astype(BF16)
        out_ref[dest, 1] = v_ref[:, dest * width : (dest + 1) * width]


def pack_q_body(q_ref, cos_ref, sin_ref, out_ref):
    cosine, sine = cos_ref[...] * SCORE_SCALE, sin_ref[...] * SCORE_SCALE
    width = out_ref.shape[2]
    for dest in range(out_ref.shape[0]):
        for lane in range(0, width, HD):
            column = dest * width + lane
            out_ref[dest, :, lane : lane + HD] = rope(
                q_ref[:, column : column + HD].astype(F32), cosine, sine
            ).astype(BF16)


def normed(rows, gain):
    rows = rows.astype(F32)
    return (
        rows * lax.rsqrt(jnp.mean(rows * rows, axis=-1, keepdims=True) + NORM_EPS) * gain.astype(F32)
    ).astype(BF16)


def project_body(
    embed_ref, mask_ref, gain_ref, wq_ref, wk_ref, wv_ref, cos_ref, sin_ref,
    qe_ref, qm_ref, ke_ref, km_ref, ve_ref, vm_ref, mq, mk,
):
    gain = gain_ref[...]

    @pl.when(pl.program_id(0) == 0)
    def _():
        mask_row = normed(jnp.broadcast_to(mask_ref[...], (16, mask_ref.shape[1])), gain)
        mq[...] = jnp.dot(mask_row, wq_ref[...], preferred_element_type=F32)
        mk[...] = jnp.dot(mask_row, wk_ref[...], preferred_element_type=F32)
        vm_ref[...] = jnp.dot(mask_row, wv_ref[...], preferred_element_type=F32).astype(BF16)

    rows = normed(embed_ref[...], gain)
    count = rows.shape[0]
    q = jnp.dot(rows, wq_ref[...], preferred_element_type=F32)
    k = jnp.dot(rows, wk_ref[...], preferred_element_type=F32)
    ve_ref[...] = jnp.dot(rows, wv_ref[...], preferred_element_type=F32).astype(BF16)
    cosine, sine = cos_ref[...], sin_ref[...]
    for lane in range(0, q.shape[1], HD):
        at = slice(lane, lane + HD)
        qe_ref[:, at] = (rope(q[:, at], cosine, sine) * SCORE_SCALE).astype(BF16)
        ke_ref[:, at] = rope(k[:, at], cosine, sine).astype(BF16)
        one_q = jnp.broadcast_to(mq[0:1, at], (count, HD))
        one_k = jnp.broadcast_to(mk[0:1, at], (count, HD))
        qm_ref[:, at] = (rope(one_q, cosine, sine) * SCORE_SCALE).astype(BF16)
        km_ref[:, at] = rope(one_k, cosine, sine).astype(BF16)


def scores(q, k):
    return lax.dot_general(q, k, (((1,), (1,)), ((), ())), preferred_element_type=F32)


def merge(state, s, v):
    top = jnp.max(s, axis=-1, keepdims=True)
    if state is None:
        w = jnp.exp2(s - top)
        return (
            top,
            jnp.sum(w, axis=-1, keepdims=True),
            jnp.dot(w.astype(BF16), v, preferred_element_type=F32),
        )
    old, total, acc = state
    top = jnp.maximum(old, top)
    keep = jnp.exp2(old - top)
    w = jnp.exp2(s - top)
    total = total * keep + jnp.sum(w, axis=-1, keepdims=True)
    acc = acc * keep + jnp.dot(w.astype(BF16), v, preferred_element_type=F32)
    return top, total, acc


def over_prompt(state, q, kv_ref, chunk):
    sources, _, rows, width = kv_ref.shape
    for first in range(0, sources, chunk):
        k = kv_ref[first : first + chunk, 0].reshape(chunk * rows, width)
        v = kv_ref[first : first + chunk, 1].reshape(chunk * rows, width)
        state = merge(state, scores(q, k), v)
    return state


def early_body(qe_ref, qm_ref, ke_ref, km_ref, ve_ref, vm_ref, commit_ref, acc_ref, stats_ref):
    mask_value = jnp.broadcast_to(vm_ref[0:1], ve_ref.shape)
    lane = lax.broadcasted_iota(jnp.int32, stats_ref.shape, 1)
    stats = jnp.zeros(stats_ref.shape, F32)
    for step in range(acc_ref.shape[0]):
        shown = commit_ref[...] <= step
        q = jnp.where(shown, qe_ref[...], qm_ref[...])
        k = jnp.where(shown, ke_ref[...], km_ref[...])
        v = jnp.where(shown, ve_ref[...], mask_value)
        top, total, acc = merge(None, scores(q, k), v)
        acc_ref[step] = acc
        stats = jnp.where(lane == step, top, stats)
        stats = jnp.where(lane == STEPS + step, total, stats)
    stats_ref[...] = stats


def response_body(chunk, kept, place_ref, kv_ref, qe_ref, qm_ref, acc_ref, stats_ref, commit_ref, *refs):
    out_refs, scratch_ref = refs[:-1], refs[-1]
    lows = len(out_refs)
    steps, blocks, per, _ = out_refs[0].shape
    low, bit = place_ref[0], place_ref[1]
    span_rows = lows * per
    count = blocks * span_rows
    side = bit if kept else 1 - bit

    def mine(ref, *lead):
        parts = [
            ref[(*lead, pl.ds(pl.multiple_of((2 * block + side) * span_rows, span_rows), span_rows), slice(None))]
            for block in range(blocks)
        ]
        return jnp.concatenate(parts, 0) if blocks > 1 else parts[0]

    revealed, stats = mine(commit_ref), mine(stats_ref)
    both = over_prompt(None, jnp.concatenate([mine(qm_ref), mine(qe_ref)], 0), kv_ref, chunk)
    for step in range(steps):
        shown = revealed <= step
        one = revealed[:, 0:1] <= step
        top_p = jnp.where(one, both[0][count:], both[0][:count])
        total_p = jnp.where(one, both[1][count:], both[1][:count])
        acc_p = jnp.where(shown, both[2][count:], both[2][:count])
        top_r, total_r = stats[:, step : step + 1], stats[:, STEPS + step : STEPS + step + 1]
        top = jnp.maximum(top_p, top_r)
        keep_p, keep_r = jnp.exp2(top_p - top), jnp.exp2(top_r - top)
        scale = 1.0 / (total_p * keep_p + total_r * keep_r)
        scratch_ref[step] = acc_p * (keep_p * scale) + mine(acc_ref, step) * (keep_r * scale)
    for step in range(steps):
        for block in range(blocks):
            for k in range(lows):
                at = block * span_rows + (low ^ k) * per
                out_refs[k][step, block] = scratch_ref[step, pl.ds(pl.multiple_of(at, per), per), :].astype(BF16)


def prompt_body(chunk, q_ref, kv_ref, km_ref, vm_ref, *refs):
    sources, rows, width = q_ref.shape
    q = q_ref[...].reshape(sources * rows, width)
    s = scores(q, km_ref[...])
    top = jnp.max(s, axis=-1, keepdims=True)
    total = jnp.sum(jnp.exp2(s - top), axis=-1, keepdims=True)
    state = over_prompt((top, total, total * vm_ref[0:1].astype(F32)), q, kv_ref, chunk)
    refs[-1][...] = (state[2] / state[1]).astype(BF16).reshape(sources, rows, width)


def output_body(lows, split, place_ref, *refs):
    x_refs, refs = refs[:lows], refs[lows:]
    outs = refs[-STEPS:]
    steps, blocks, per, width = x_refs[0].shape
    far = lows // 2 if split else lows
    w = jnp.concatenate([ref[...] for ref in refs[:-STEPS]], 0)
    xs = []
    for k, x_ref in enumerate(x_refs):
        x = x_ref[...].reshape(steps * blocks * per, width)
        if k >= far:
            swapped = jnp.concatenate([x[:, width // 2 :], x[:, : width // 2]], 1)
            x = jnp.where(place_ref[2] == 0, x, swapped)
        xs.append(x)
    total = jnp.dot(jnp.concatenate(xs, 1), w, preferred_element_type=F32)
    for step, out_ref in enumerate(outs):
        for block in range(blocks):
            at = (step * blocks + block) * per
            out_ref[block] = total[at : at + per].astype(out_ref.dtype)


def halve_body(place_ref, keep_ref, got_ref, send_ref, kept_ref):
    bit = place_ref[0]
    for pair in range(send_ref.shape[0]):
        first = keep_ref[2 * pair] + got_ref[2 * pair].astype(F32)
        second = keep_ref[2 * pair + 1] + got_ref[2 * pair + 1].astype(F32)
        kept_ref[pair] = jnp.where(bit == 0, first, second)
        send_ref[pair] = jnp.where(bit == 0, second, first).astype(BF16)


def finish_body(step, embed_ref, mask_ref, gain_ref, commit_ref, keep_ref, got_ref, *refs):
    residual_ref, normed_ref = refs[-2:]
    shown = commit_ref[:, 0:1] <= step
    rows = jnp.where(shown, embed_ref[...].astype(F32), mask_ref[...].astype(F32))
    hidden = rows + (keep_ref[0] + got_ref[0].astype(F32))
    residual_ref[0] = hidden.astype(BF16)
    scale = lax.rsqrt(jnp.mean(hidden * hidden, axis=-1, keepdims=True) + NORM_EPS)
    normed_ref[0] = (hidden * scale * gain_ref[...].astype(F32)).astype(BF16)


def unpack_body(in_ref, out_ref):
    width = in_ref.shape[2]
    for source in range(in_ref.shape[0]):
        out_ref[:, source * width : (source + 1) * width] = in_ref[source]


def per_device(
    prompt_query,
    prompt_key,
    prompt_value,
    response_embed,
    mask_embed,
    commit_step,
    block_index,
    attention_gain,
    residual_gain,
    query_weight,
    key_weight,
    value_weight,
    output_weight,
):
    rows, head_cols = prompt_query.shape
    resp, model = response_embed.shape
    n = lax.axis_size("seq")
    me = lax.axis_index("seq")
    width = query_weight.shape[1]
    heads = width // HD
    prompt_len = rows * n
    lows = min(4, n)
    highs = n // lows
    per = resp // n

    def swap(x, bit):
        return lax.ppermute(x, "seq", [(i, i ^ bit) for i in range(n)])

    dests = max(1, n // 4)
    cos_p, sin_p = tables(me * rows + jnp.arange(rows, dtype=jnp.int32))
    kv_send = call(
        pack_kv_body,
        (n // dests,),
        [
            pl.BlockSpec((rows, dests * width), lambda j: (0, j)),
            pl.BlockSpec((rows, dests * width), lambda j: (0, j)),
            whole((rows, HD)),
            whole((rows, HD)),
        ],
        pl.BlockSpec((dests, 2, rows, width), lambda j: (j, 0, 0, 0)),
        jax.ShapeDtypeStruct((n, 2, rows, width), BF16),
        flops=6 * rows * head_cols,
        moved=8 * rows * head_cols,
    )(prompt_key, prompt_value, cos_p, sin_p)
    kv = lax.all_to_all(kv_send, "seq", 0, 0, tiled=True)
    q_send = call(
        pack_q_body,
        (n // dests,),
        [
            pl.BlockSpec((rows, dests * width), lambda j: (0, j)),
            whole((rows, HD)),
            whole((rows, HD)),
        ],
        pl.BlockSpec((dests, rows, width), lambda j: (j, 0, 0)),
        jax.ShapeDtypeStruct((n, rows, width), BF16),
        flops=6 * rows * head_cols,
        moved=4 * rows * head_cols,
    )(prompt_query, cos_p, sin_p)
    q_heads = lax.all_to_all(q_send, "seq", 0, 0, tiled=True)

    groups = lax.axis_size("groups")
    group = lax.axis_index("groups")
    split = lows == 4 and groups % 2 == 0
    weights = [output_weight, swap(output_weight, 1)]
    if split:
        half_rows = lax.dynamic_slice_in_dim(output_weight, (group & 1) * (width // 2), width // 2, 0)
        fetched = swap(half_rows, 2)
        given = lax.ppermute(fetched, "groups", [(i, i ^ 1) for i in range(groups)])
        last = swap(fetched, 1)
        weights += [fetched, given, last, swap(given, 1)]
    elif lows == 4:
        far = swap(output_weight, 2)
        weights += [far, swap(far, 1)]

    cos_r, sin_r = tables(prompt_len + block_index[0] * resp + jnp.arange(resp, dtype=jnp.int32))
    commit = jnp.broadcast_to(commit_step[:, None], (resp, HD))
    block = min(resp, 128)
    row_block = pl.BlockSpec((block, width), lambda i: (i, 0))
    wide = jax.ShapeDtypeStruct((resp, width), BF16)
    qe, qm, ke, km, ve, vm = call(
        project_body,
        (resp // block,),
        [
            pl.BlockSpec((block, model), lambda i: (i, 0)),
            whole((1, model)),
            whole((1, model)),
            whole((model, width)),
            whole((model, width)),
            whole((model, width)),
            pl.BlockSpec((block, HD), lambda i: (i, 0)),
            pl.BlockSpec((block, HD), lambda i: (i, 0)),
        ],
        [row_block] * 5 + [whole((16, width))],
        [wide] * 5 + [jax.ShapeDtypeStruct((16, width), BF16)],
        scratch=[pltpu.VMEM((16, width), F32)] * 2,
        flops=6 * resp * model * width,
        moved=2 * resp * model + 6 * model * width,
    )(
        response_embed, mask_embed[None, :], attention_gain[None, :],
        query_weight, key_weight, value_weight, cos_r, sin_r,
    )

    chunk = max(1, min(n, 256 // rows))
    kv_block = pl.BlockSpec((n, 2, rows, HD), lambda h, *_: (0, 0, 0, h))
    key_block = pl.BlockSpec((resp, HD), lambda h, *_: (0, h))
    vm_block = pl.BlockSpec((16, HD), lambda h, *_: (0, h))
    low = me & (lows - 1)
    high = me >> (lows.bit_length() - 1)
    blocks = highs // 2
    place = jnp.stack([low, high & 1, group & 1]).astype(jnp.int32)
    early_acc, early_stats = call(
        early_body,
        (heads,),
        [key_block] * 5 + [vm_block, whole((resp, HD))],
        [pl.BlockSpec((STEPS, resp, HD), lambda h: (0, 0, h)), pl.BlockSpec((resp, HD), lambda h: (0, h))],
        [jax.ShapeDtypeStruct((STEPS, resp, width), F32), jax.ShapeDtypeStruct((resp, width), F32)],
        flops=4 * STEPS * resp * resp * width,
        moved=20 * resp * width,
        exps=heads * STEPS * resp * resp,
    )(qe, qm, ke, km, ve, vm, commit)
    columns = min(model, 1024)
    projected = {}
    for kept in (False, True):
        context = pl.pallas_call(
            functools.partial(response_body, chunk, kept),
            grid_spec=pltpu.PrefetchScalarGridSpec(
                num_scalar_prefetch=1,
                grid=(heads,),
                in_specs=[
                    kv_block, key_block, key_block,
                    pl.BlockSpec((STEPS, resp, HD), lambda h, *_: (0, 0, h)), key_block, whole((resp, HD)),
                ],
                out_specs=[pl.BlockSpec((STEPS, blocks, per, HD), lambda h, *_: (0, 0, 0, h))] * lows,
                scratch_shapes=[pltpu.VMEM((STEPS, resp // 2, HD), F32)],
            ),
            out_shape=[jax.ShapeDtypeStruct((STEPS, blocks, per, width), BF16)] * lows,
            name="response_attention",
            cost_estimate=pl.CostEstimate(
                flops=4 * resp * width * prompt_len,
                bytes_accessed=4 * prompt_len * width,
                transcendentals=heads * resp * prompt_len,
            ),
        )(place, kv, qe, qm, early_acc, early_stats, commit)
        plane_context = [context[0]]
        for k in range(1, lows):
            plane_context.append(swap(context[k], k))
        projected[kept] = pl.pallas_call(
            functools.partial(output_body, lows, split),
            grid_spec=pltpu.PrefetchScalarGridSpec(
                num_scalar_prefetch=1,
                grid=(model // columns,),
                in_specs=[whole((STEPS, blocks, per, width))] * lows
                + [pl.BlockSpec((w.shape[0], columns), lambda j, *_: (0, j)) for w in weights],
                out_specs=[pl.BlockSpec((blocks, per, columns), lambda j, *_: (0, 0, j))] * STEPS,
            ),
            out_shape=[jax.ShapeDtypeStruct((blocks, per, model), F32 if kept else BF16)] * STEPS,
            name="output_projection",
            cost_estimate=pl.CostEstimate(
                flops=STEPS * resp * model * width, bytes_accessed=2 * lows * width * model, transcendentals=0
            ),
        )(place, *plane_context, *weights)
    sends, keeps = projected[False], projected[True]

    level = 0
    while True:
        gots = []
        for step in range(STEPS):
            gots.append(swap(sends[step], lows << level))
        count = keeps[0].shape[0]
        if count == 1:
            break
        level += 1
        bit = ((high >> level) & 1).astype(jnp.int32).reshape(1)
        sends, kept = [], []
        for step in range(STEPS):
            columns = model
            get = pl.BlockSpec((count, per, columns), lambda j, *_: (0, 0, j))
            put = pl.BlockSpec((count // 2, per, columns), lambda j, *_: (0, 0, j))
            one, two = pl.pallas_call(
                halve_body,
                grid_spec=pltpu.PrefetchScalarGridSpec(
                    num_scalar_prefetch=1,
                    grid=(model // columns,),
                    in_specs=[get, get],
                    out_specs=[put, put],
                ),
                out_shape=[
                    jax.ShapeDtypeStruct((count // 2, per, model), BF16),
                    jax.ShapeDtypeStruct((count // 2, per, model), F32),
                ],
                name="halve",
                cost_estimate=pl.CostEstimate(
                    flops=count * per * model, bytes_accessed=9 * count * per * model, transcendentals=0
                ),
            )(bit, keeps[step], gots[step])
            sends.append(one)
            kept.append(two)
        keeps = kept

    blocks_of_q = max(1, min(n, 1024 // rows))
    prompt_context = None
    for head in range(heads):
        of_head = functools.partial(lambda head, *_: (0, head), head)
        of_kv = functools.partial(lambda head, *_: (0, 0, 0, head), head)
        for turn in range(n // blocks_of_q):
            of_block = functools.partial(lambda head, turn, *_: (turn, 0, head), head, turn)
            earlier = [] if prompt_context is None else [prompt_context]
            prompt_context = pl.pallas_call(
                functools.partial(prompt_body, chunk),
                grid=(1,),
                in_specs=[
                    pl.BlockSpec((blocks_of_q, rows, HD), of_block),
                    pl.BlockSpec((n, 2, rows, HD), of_kv),
                    pl.BlockSpec((resp, HD), of_head),
                    pl.BlockSpec((16, HD), of_head),
                ]
                + [pl.BlockSpec(memory_space=pl.ANY)] * len(earlier),
                out_specs=pl.BlockSpec((blocks_of_q, rows, HD), of_block),
                out_shape=jax.ShapeDtypeStruct((n, rows, width), BF16),
                name="prompt_attention",
                compiler_params=GRANT,
                input_output_aliases={4: 0} if earlier else {},
                cost_estimate=pl.CostEstimate(
                    flops=4 * blocks_of_q * rows * HD * (prompt_len + resp),
                    bytes_accessed=4 * prompt_len * HD + 4 * blocks_of_q * rows * HD,
                    transcendentals=blocks_of_q * rows * (prompt_len + resp),
                ),
            )(q_heads, kv, km, vm, *earlier)
    back = lax.all_to_all(prompt_context, "seq", 0, 0, tiled=True)

    my_embed = lax.dynamic_slice_in_dim(response_embed, me * per, per, 0)
    my_commit = jnp.broadcast_to(lax.dynamic_slice_in_dim(commit_step, me * per, per, 0)[:, None], (per, HD))
    results = []
    for step in range(STEPS):
        at_step = functools.partial(lambda step, i: (step, 0, 0), step)
        results = pl.pallas_call(
            functools.partial(finish_body, step),
            grid=(1,),
            in_specs=[
                whole((per, model)), whole((1, model)), whole((1, model)), whole((per, HD)),
                whole((1, per, model)), whole((1, per, model)),
            ]
            + [pl.BlockSpec(memory_space=pl.ANY)] * len(results),
            out_specs=[pl.BlockSpec((1, per, model), at_step)] * 2,
            out_shape=[jax.ShapeDtypeStruct((STEPS, per, model), BF16)] * 2,
            name="finish",
            input_output_aliases={6: 0, 7: 1} if results else {},
            cost_estimate=pl.CostEstimate(flops=8 * per * model, bytes_accessed=12 * per * model, transcendentals=0),
        )(
            my_embed, mask_embed[None, :], residual_gain[None, :], my_commit,
            keeps[step], gots[step], *results,
        )
    residual, normed_rows = results
    columns = max(1, n // 4)
    prompt_out = call(
        unpack_body,
        (n // columns,),
        [pl.BlockSpec((columns, rows, width), lambda j: (j, 0, 0))],
        pl.BlockSpec((rows, columns * width), lambda j: (0, j)),
        jax.ShapeDtypeStruct((rows, head_cols), BF16),
        moved=4 * rows * head_cols,
    )(back)
    return prompt_out, residual, normed_rows


def solution(mesh):
    return jax.shard_map(
        per_device,
        mesh=mesh,
        in_specs=(
            P(("groups", "seq"), None),
            P(("groups", "seq"), None),
            P(("groups", "seq"), None),
            P("groups", None),
            P(),
            P("groups"),
            P("groups"),
            P(),
            P(),
            P(None, "seq"),
            P(None, "seq"),
            P(None, "seq"),
            P("seq", None),
        ),
        out_specs=(
            P(("groups", "seq"), None),
            P(None, ("groups", "seq"), None),
            P(None, ("groups", "seq"), None),
        ),
        check_vma=False,
    )
```

```python
import functools
import math

import jax
import jax.numpy as jnp
from jax import lax
from jax.experimental import pallas as pl
from jax.experimental.pallas import tpu as pltpu
from jax.sharding import PartitionSpec as P


HD = 128
STEPS = 4
ROPE_BASE = 500000.0
NORM_EPS = 1e-05
SCORE_SCALE = math.log2(math.e) / math.sqrt(HD)

F32 = jnp.float32
BF16 = jnp.bfloat16


GRANT = pltpu.CompilerParams(vmem_limit_bytes=28 << 20)


def call(body, grid, in_specs, out_specs, out_shape, scratch=(), flops=0, moved=0, exps=0):
    return pl.pallas_call(
        body,
        grid=grid,
        in_specs=in_specs,
        out_specs=out_specs,
        out_shape=out_shape,
        scratch_shapes=list(scratch),
        cost_estimate=pl.CostEstimate(flops=flops, bytes_accessed=moved, transcendentals=exps),
    )


def whole(shape):
    return pl.BlockSpec(shape, lambda *_: (0,) * len(shape))


def tables(positions):
    half = HD // 2
    exponent = jnp.arange(half, dtype=F32) * (2.0 / HD)
    inv_freq = ROPE_BASE ** (-exponent)
    angles = positions.astype(F32)[:, None] * inv_freq[None, :]
    cosine, sine = jnp.cos(angles), jnp.sin(angles)
    return jnp.concatenate([cosine, cosine], 1), jnp.concatenate([-sine, sine], 1)


def rope(u, cosine, sine):
    return u * cosine + pltpu.roll(u, HD // 2, 1) * sine


def pack_kv_body(k_ref, v_ref, cos_ref, sin_ref, out_ref):
    cosine, sine = cos_ref[...], sin_ref[...]
    width = out_ref.shape[3]
    for dest in range(out_ref.shape[0]):
        for lane in range(0, width, HD):
            column = dest * width + lane
            out_ref[dest, 0, :, lane : lane + HD] = rope(
                k_ref[:, column : column + HD].astype(F32), cosine, sine
            ).astype(BF16)
        out_ref[dest, 1] = v_ref[:, dest * width : (dest + 1) * width]


def pack_q_body(q_ref, cos_ref, sin_ref, out_ref):
    cosine, sine = cos_ref[...] * SCORE_SCALE, sin_ref[...] * SCORE_SCALE
    width = out_ref.shape[2]
    for dest in range(out_ref.shape[0]):
        for lane in range(0, width, HD):
            column = dest * width + lane
            out_ref[dest, :, lane : lane + HD] = rope(
                q_ref[:, column : column + HD].astype(F32), cosine, sine
            ).astype(BF16)


def normed(rows, gain):
    rows = rows.astype(F32)
    return (
        rows * lax.rsqrt(jnp.mean(rows * rows, axis=-1, keepdims=True) + NORM_EPS) * gain.astype(F32)
    ).astype(BF16)


def project_body(
    embed_ref, mask_ref, gain_ref, wq_ref, wk_ref, wv_ref, cos_ref, sin_ref,
    qe_ref, qm_ref, ke_ref, km_ref, ve_ref, vm_ref, mq, mk,
):
    gain = gain_ref[...]

    @pl.when(pl.program_id(0) == 0)
    def _():
        mask_row = normed(jnp.broadcast_to(mask_ref[...], (16, mask_ref.shape[1])), gain)
        mq[...] = jnp.dot(mask_row, wq_ref[...], preferred_element_type=F32)
        mk[...] = jnp.dot(mask_row, wk_ref[...], preferred_element_type=F32)
        vm_ref[...] = jnp.dot(mask_row, wv_ref[...], preferred_element_type=F32).astype(BF16)

    rows = normed(embed_ref[...], gain)
    count = rows.shape[0]
    q = jnp.dot(rows, wq_ref[...], preferred_element_type=F32)
    k = jnp.dot(rows, wk_ref[...], preferred_element_type=F32)
    ve_ref[...] = jnp.dot(rows, wv_ref[...], preferred_element_type=F32).astype(BF16)
    cosine, sine = cos_ref[...], sin_ref[...]
    for lane in range(0, q.shape[1], HD):
        at = slice(lane, lane + HD)
        qe_ref[:, at] = (rope(q[:, at], cosine, sine) * SCORE_SCALE).astype(BF16)
        ke_ref[:, at] = rope(k[:, at], cosine, sine).astype(BF16)
        one_q = jnp.broadcast_to(mq[0:1, at], (count, HD))
        one_k = jnp.broadcast_to(mk[0:1, at], (count, HD))
        qm_ref[:, at] = (rope(one_q, cosine, sine) * SCORE_SCALE).astype(BF16)
        km_ref[:, at] = rope(one_k, cosine, sine).astype(BF16)


def scores(q, k):
    return lax.dot_general(q, k, (((1,), (1,)), ((), ())), preferred_element_type=F32)


def merge(state, s, v):
    top = jnp.max(s, axis=-1, keepdims=True)
    if state is None:
        w = jnp.exp2(s - top)
        return (
            top,
            jnp.sum(w, axis=-1, keepdims=True),
            jnp.dot(w.astype(BF16), v, preferred_element_type=F32),
        )
    old, total, acc = state
    top = jnp.maximum(old, top)
    keep = jnp.exp2(old - top)
    w = jnp.exp2(s - top)
    total = total * keep + jnp.sum(w, axis=-1, keepdims=True)
    acc = acc * keep + jnp.dot(w.astype(BF16), v, preferred_element_type=F32)
    return top, total, acc


def over_prompt(state, q, kv_ref, chunk):
    sources, _, rows, width = kv_ref.shape
    for first in range(0, sources, chunk):
        k = kv_ref[first : first + chunk, 0].reshape(chunk * rows, width)
        v = kv_ref[first : first + chunk, 1].reshape(chunk * rows, width)
        state = merge(state, scores(q, k), v)
    return state


def early_body(qe_ref, qm_ref, ke_ref, km_ref, ve_ref, vm_ref, commit_ref, acc_ref, stats_ref):
    mask_value = jnp.broadcast_to(vm_ref[0:1], ve_ref.shape)
    lane = lax.broadcasted_iota(jnp.int32, stats_ref.shape, 1)
    stats = jnp.zeros(stats_ref.shape, F32)
    for step in range(acc_ref.shape[0]):
        shown = commit_ref[...] <= step
        q = jnp.where(shown, qe_ref[...], qm_ref[...])
        k = jnp.where(shown, ke_ref[...], km_ref[...])
        v = jnp.where(shown, ve_ref[...], mask_value)
        top, total, acc = merge(None, scores(q, k), v)
        acc_ref[step] = acc
        stats = jnp.where(lane == step, top, stats)
        stats = jnp.where(lane == STEPS + step, total, stats)
    stats_ref[...] = stats


def response_body(chunk, place_ref, kv_ref, qe_ref, qm_ref, acc_ref, stats_ref, commit_ref, *refs):
    out_refs, scratch_ref = refs[:-1], refs[-1]
    lows = len(out_refs)
    steps, blocks, per, _ = out_refs[0].shape
    low = place_ref[0]
    span_rows = lows * per
    count = blocks * span_rows

    def flat(value):
        return value.reshape(count, HD)

    revealed, stats = flat(commit_ref[...]), flat(stats_ref[...])
    both = over_prompt(None, jnp.concatenate([flat(qm_ref[...]), flat(qe_ref[...])], 0), kv_ref, chunk)
    for step in range(steps):
        shown = revealed <= step
        one = revealed[:, 0:1] <= step
        top_p = jnp.where(one, both[0][count:], both[0][:count])
        total_p = jnp.where(one, both[1][count:], both[1][:count])
        acc_p = jnp.where(shown, both[2][count:], both[2][:count])
        top_r, total_r = stats[:, step : step + 1], stats[:, STEPS + step : STEPS + step + 1]
        top = jnp.maximum(top_p, top_r)
        keep_p, keep_r = jnp.exp2(top_p - top), jnp.exp2(top_r - top)
        scale = 1.0 / (total_p * keep_p + total_r * keep_r)
        scratch_ref[step] = acc_p * (keep_p * scale) + flat(acc_ref[step]) * (keep_r * scale)
    for step in range(steps):
        for block in range(blocks):
            for k in range(lows):
                at = block * span_rows + (low ^ k) * per
                out_refs[k][step, block] = scratch_ref[step, pl.ds(pl.multiple_of(at, per), per), :].astype(BF16)


def prompt_body(chunk, q_ref, kv_ref, km_ref, vm_ref, *refs):
    sources, rows, width = q_ref.shape
    q = q_ref[...].reshape(sources * rows, width)
    s = scores(q, km_ref[...])
    top = jnp.max(s, axis=-1, keepdims=True)
    total = jnp.sum(jnp.exp2(s - top), axis=-1, keepdims=True)
    state = over_prompt((top, total, total * vm_ref[0:1].astype(F32)), q, kv_ref, chunk)
    refs[-1][...] = (state[2] / state[1]).astype(BF16).reshape(sources, rows, width)


def output_body(lows, split, place_ref, *refs):
    x_refs, refs = refs[:lows], refs[lows:]
    outs = refs[-STEPS:]
    steps, blocks, per, width = x_refs[0].shape
    far = lows // 2 if split else lows
    w = jnp.concatenate([ref[...] for ref in refs[:-STEPS]], 0)
    xs = []
    for k, x_ref in enumerate(x_refs):
        x = x_ref[...].reshape(steps * blocks * per, width)
        if k >= far:
            swapped = jnp.concatenate([x[:, width // 2 :], x[:, : width // 2]], 1)
            x = jnp.where(place_ref[2] == 0, x, swapped)
        xs.append(x)
    total = jnp.dot(jnp.concatenate(xs, 1), w, preferred_element_type=F32)
    for step, out_ref in enumerate(outs):
        for block in range(blocks):
            at = (step * blocks + block) * per
            out_ref[block] = total[at : at + per].astype(out_ref.dtype)


def halve_body(place_ref, keep_ref, got_ref, send_ref, kept_ref):
    bit = place_ref[0]
    for pair in range(send_ref.shape[0]):
        first = keep_ref[2 * pair] + got_ref[2 * pair].astype(F32)
        second = keep_ref[2 * pair + 1] + got_ref[2 * pair + 1].astype(F32)
        kept_ref[pair] = jnp.where(bit == 0, first, second)
        send_ref[pair] = jnp.where(bit == 0, second, first).astype(BF16)


def finish_body(step, embed_ref, mask_ref, gain_ref, commit_ref, keep_ref, got_ref, *refs):
    residual_ref, normed_ref = refs[-2:]
    shown = commit_ref[:, 0:1] <= step
    rows = jnp.where(shown, embed_ref[...].astype(F32), mask_ref[...].astype(F32))
    hidden = rows + (keep_ref[0] + got_ref[0].astype(F32))
    residual_ref[0] = hidden.astype(BF16)
    scale = lax.rsqrt(jnp.mean(hidden * hidden, axis=-1, keepdims=True) + NORM_EPS)
    normed_ref[0] = (hidden * scale * gain_ref[...].astype(F32)).astype(BF16)


def unpack_body(in_ref, out_ref):
    width = in_ref.shape[2]
    for source in range(in_ref.shape[0]):
        out_ref[:, source * width : (source + 1) * width] = in_ref[source]


def per_device(
    prompt_query,
    prompt_key,
    prompt_value,
    response_embed,
    mask_embed,
    commit_step,
    block_index,
    attention_gain,
    residual_gain,
    query_weight,
    key_weight,
    value_weight,
    output_weight,
):
    rows, head_cols = prompt_query.shape
    resp, model = response_embed.shape
    n = lax.axis_size("seq")
    me = lax.axis_index("seq")
    width = query_weight.shape[1]
    heads = width // HD
    prompt_len = rows * n
    lows = min(4, n)
    highs = n // lows
    per = resp // n

    def swap(x, bit):
        return lax.ppermute(x, "seq", [(i, i ^ bit) for i in range(n)])

    dests = max(1, n // 4)
    cos_p, sin_p = tables(me * rows + jnp.arange(rows, dtype=jnp.int32))
    kv_send = call(
        pack_kv_body,
        (n // dests,),
        [
            pl.BlockSpec((rows, dests * width), lambda j: (0, j)),
            pl.BlockSpec((rows, dests * width), lambda j: (0, j)),
            whole((rows, HD)),
            whole((rows, HD)),
        ],
        pl.BlockSpec((dests, 2, rows, width), lambda j: (j, 0, 0, 0)),
        jax.ShapeDtypeStruct((n, 2, rows, width), BF16),
        flops=6 * rows * head_cols,
        moved=8 * rows * head_cols,
    )(prompt_key, prompt_value, cos_p, sin_p)
    kv = lax.all_to_all(kv_send, "seq", 0, 0, tiled=True)
    q_send = call(
        pack_q_body,
        (n // dests,),
        [
            pl.BlockSpec((rows, dests * width), lambda j: (0, j)),
            whole((rows, HD)),
            whole((rows, HD)),
        ],
        pl.BlockSpec((dests, rows, width), lambda j: (j, 0, 0)),
        jax.ShapeDtypeStruct((n, rows, width), BF16),
        flops=6 * rows * head_cols,
        moved=4 * rows * head_cols,
    )(prompt_query, cos_p, sin_p)
    q_heads = lax.all_to_all(q_send, "seq", 0, 0, tiled=True)

    groups = lax.axis_size("groups")
    group = lax.axis_index("groups")
    split = lows == 4 and groups % 2 == 0
    weights = [output_weight, swap(output_weight, 1)]
    if split:
        half_rows = lax.dynamic_slice_in_dim(output_weight, (group & 1) * (width // 2), width // 2, 0)
        fetched = swap(half_rows, 2)
        given = lax.ppermute(fetched, "groups", [(i, i ^ 1) for i in range(groups)])
        last = swap(fetched, 1)
        weights += [fetched, given, last, swap(given, 1)]
    elif lows == 4:
        far = swap(output_weight, 2)
        weights += [far, swap(far, 1)]

    cos_r, sin_r = tables(prompt_len + block_index[0] * resp + jnp.arange(resp, dtype=jnp.int32))
    commit = jnp.broadcast_to(commit_step[:, None], (resp, HD))
    block = min(resp, 128)
    row_block = pl.BlockSpec((block, width), lambda i: (i, 0))
    wide = jax.ShapeDtypeStruct((resp, width), BF16)
    qe, qm, ke, km, ve, vm = call(
        project_body,
        (resp // block,),
        [
            pl.BlockSpec((block, model), lambda i: (i, 0)),
            whole((1, model)),
            whole((1, model)),
            whole((model, width)),
            whole((model, width)),
            whole((model, width)),
            pl.BlockSpec((block, HD), lambda i: (i, 0)),
            pl.BlockSpec((block, HD), lambda i: (i, 0)),
        ],
        [row_block] * 5 + [whole((16, width))],
        [wide] * 5 + [jax.ShapeDtypeStruct((16, width), BF16)],
        scratch=[pltpu.VMEM((16, width), F32)] * 2,
        flops=6 * resp * model * width,
        moved=2 * resp * model + 6 * model * width,
    )(
        response_embed, mask_embed[None, :], attention_gain[None, :],
        query_weight, key_weight, value_weight, cos_r, sin_r,
    )

    chunk = max(1, min(n, 256 // rows))
    kv_block = pl.BlockSpec((n, 2, rows, HD), lambda h, *_: (0, 0, 0, h))
    key_block = pl.BlockSpec((resp, HD), lambda h, *_: (0, h))
    vm_block = pl.BlockSpec((16, HD), lambda h, *_: (0, h))
    low = me & (lows - 1)
    high = me >> (lows.bit_length() - 1)
    blocks = highs // 2
    place = jnp.stack([low, high & 1, group & 1]).astype(jnp.int32)
    early_acc, early_stats = call(
        early_body,
        (heads,),
        [key_block] * 5 + [vm_block, whole((resp, HD))],
        [pl.BlockSpec((STEPS, resp, HD), lambda h: (0, 0, h)), pl.BlockSpec((resp, HD), lambda h: (0, h))],
        [jax.ShapeDtypeStruct((STEPS, resp, width), F32), jax.ShapeDtypeStruct((resp, width), F32)],
        flops=4 * STEPS * resp * resp * width,
        moved=20 * resp * width,
        exps=heads * STEPS * resp * resp,
    )(qe, qm, ke, km, ve, vm, commit)

    def paired(array, *lead):
        return array.reshape(*lead, blocks, 2, lows * per, array.shape[-1])

    columns = min(model, 1024)
    projected = {}
    for kept in (False, True):
        side = (lambda at: at[1]) if kept else (lambda at: 1 - at[1])
        half_rows_of = pl.BlockSpec((blocks, None, lows * per, HD), lambda h, at, side=side: (0, side(at), 0, h))
        context = pl.pallas_call(
            functools.partial(response_body, 2 * chunk),
            grid_spec=pltpu.PrefetchScalarGridSpec(
                num_scalar_prefetch=1,
                grid=(heads,),
                in_specs=[
                    kv_block, half_rows_of, half_rows_of,
                    pl.BlockSpec(
                        (STEPS, blocks, None, lows * per, HD), lambda h, at, side=side: (0, 0, side(at), 0, h)
                    ),
                    half_rows_of,
                    pl.BlockSpec((blocks, None, lows * per, HD), lambda h, at, side=side: (0, side(at), 0, 0)),
                ],
                out_specs=[pl.BlockSpec((STEPS, blocks, per, HD), lambda h, *_: (0, 0, 0, h))] * lows,
                scratch_shapes=[pltpu.VMEM((STEPS, resp // 2, HD), F32)],
            ),
            out_shape=[jax.ShapeDtypeStruct((STEPS, blocks, per, width), BF16)] * lows,
            name="response_attention",
            cost_estimate=pl.CostEstimate(
                flops=4 * resp * width * prompt_len,
                bytes_accessed=4 * prompt_len * width,
                transcendentals=heads * resp * prompt_len,
            ),
        )(
            place, kv, paired(qe), paired(qm), paired(early_acc, STEPS), paired(early_stats), paired(commit)
        )
        plane_context = [context[0]]
        for k in range(1, lows):
            plane_context.append(swap(context[k], k))
        projected[kept] = pl.pallas_call(
            functools.partial(output_body, lows, split),
            grid_spec=pltpu.PrefetchScalarGridSpec(
                num_scalar_prefetch=1,
                grid=(model // columns,),
                in_specs=[whole((STEPS, blocks, per, width))] * lows
                + [pl.BlockSpec((w.shape[0], columns), lambda j, *_: (0, j)) for w in weights],
                out_specs=[pl.BlockSpec((blocks, per, columns), lambda j, *_: (0, 0, j))] * STEPS,
            ),
            out_shape=[jax.ShapeDtypeStruct((blocks, per, model), F32 if kept else BF16)] * STEPS,
            name="output_projection",
            cost_estimate=pl.CostEstimate(
                flops=STEPS * resp * model * width, bytes_accessed=2 * lows * width * model, transcendentals=0
            ),
        )(place, *plane_context, *weights)
    sends, keeps = projected[False], projected[True]

    level = 0
    while True:
        gots = []
        for step in range(STEPS):
            gots.append(swap(sends[step], lows << level))
        count = keeps[0].shape[0]
        if count == 1:
            break
        level += 1
        bit = ((high >> level) & 1).astype(jnp.int32).reshape(1)
        sends, kept = [], []
        for step in range(STEPS):
            columns = model
            get = pl.BlockSpec((count, per, columns), lambda j, *_: (0, 0, j))
            put = pl.BlockSpec((count // 2, per, columns), lambda j, *_: (0, 0, j))
            one, two = pl.pallas_call(
                halve_body,
                grid_spec=pltpu.PrefetchScalarGridSpec(
                    num_scalar_prefetch=1,
                    grid=(model // columns,),
                    in_specs=[get, get],
                    out_specs=[put, put],
                ),
                out_shape=[
                    jax.ShapeDtypeStruct((count // 2, per, model), BF16),
                    jax.ShapeDtypeStruct((count // 2, per, model), F32),
                ],
                name="halve",
                cost_estimate=pl.CostEstimate(
                    flops=count * per * model, bytes_accessed=9 * count * per * model, transcendentals=0
                ),
            )(bit, keeps[step], gots[step])
            sends.append(one)
            kept.append(two)
        keeps = kept

    blocks_of_q = max(1, min(n, 1024 // rows))
    prompt_context = None
    for head in range(heads):
        of_head = functools.partial(lambda head, *_: (0, head), head)
        of_kv = functools.partial(lambda head, *_: (0, 0, 0, head), head)
        for turn in range(n // blocks_of_q):
            of_block = functools.partial(lambda head, turn, *_: (turn, 0, head), head, turn)
            earlier = [] if prompt_context is None else [prompt_context]
            prompt_context = pl.pallas_call(
                functools.partial(prompt_body, chunk),
                grid=(1,),
                in_specs=[
                    pl.BlockSpec((blocks_of_q, rows, HD), of_block),
                    pl.BlockSpec((n, 2, rows, HD), of_kv),
                    pl.BlockSpec((resp, HD), of_head),
                    pl.BlockSpec((16, HD), of_head),
                ]
                + [pl.BlockSpec(memory_space=pl.ANY)] * len(earlier),
                out_specs=pl.BlockSpec((blocks_of_q, rows, HD), of_block),
                out_shape=jax.ShapeDtypeStruct((n, rows, width), BF16),
                name="prompt_attention",
                compiler_params=GRANT,
                input_output_aliases={4: 0} if earlier else {},
                cost_estimate=pl.CostEstimate(
                    flops=4 * blocks_of_q * rows * HD * (prompt_len + resp),
                    bytes_accessed=4 * prompt_len * HD + 4 * blocks_of_q * rows * HD,
                    transcendentals=blocks_of_q * rows * (prompt_len + resp),
                ),
            )(q_heads, kv, km, vm, *earlier)
    back = lax.all_to_all(prompt_context, "seq", 0, 0, tiled=True)

    my_embed = lax.dynamic_slice_in_dim(response_embed, me * per, per, 0)
    my_commit = jnp.broadcast_to(lax.dynamic_slice_in_dim(commit_step, me * per, per, 0)[:, None], (per, HD))
    results = []
    for step in range(STEPS):
        at_step = functools.partial(lambda step, i: (step, 0, 0), step)
        results = pl.pallas_call(
            functools.partial(finish_body, step),
            grid=(1,),
            in_specs=[
                whole((per, model)), whole((1, model)), whole((1, model)), whole((per, HD)),
                whole((1, per, model)), whole((1, per, model)),
            ]
            + [pl.BlockSpec(memory_space=pl.ANY)] * len(results),
            out_specs=[pl.BlockSpec((1, per, model), at_step)] * 2,
            out_shape=[jax.ShapeDtypeStruct((STEPS, per, model), BF16)] * 2,
            name="finish",
            input_output_aliases={6: 0, 7: 1} if results else {},
            cost_estimate=pl.CostEstimate(flops=8 * per * model, bytes_accessed=12 * per * model, transcendentals=0),
        )(
            my_embed, mask_embed[None, :], residual_gain[None, :], my_commit,
            keeps[step], gots[step], *results,
        )
    residual, normed_rows = results
    columns = max(1, n // 4)
    prompt_out = call(
        unpack_body,
        (n // columns,),
        [pl.BlockSpec((columns, rows, width), lambda j: (j, 0, 0))],
        pl.BlockSpec((rows, columns * width), lambda j: (0, j)),
        jax.ShapeDtypeStruct((rows, head_cols), BF16),
        moved=4 * rows * head_cols,
    )(back)
    return prompt_out, residual, normed_rows


def solution(mesh):
    return jax.shard_map(
        per_device,
        mesh=mesh,
        in_specs=(
            P(("groups", "seq"), None),
            P(("groups", "seq"), None),
            P(("groups", "seq"), None),
            P("groups", None),
            P(),
            P("groups"),
            P("groups"),
            P(),
            P(),
            P(None, "seq"),
            P(None, "seq"),
            P(None, "seq"),
            P("seq", None),
        ),
        out_specs=(
            P(("groups", "seq"), None),
            P(None, ("groups", "seq"), None),
            P(None, ("groups", "seq"), None),
        ),
        check_vma=False,
    )
```

```python
import functools
import math

import jax
import jax.numpy as jnp
from jax import lax
from jax.experimental import pallas as pl
from jax.experimental.pallas import tpu as pltpu
from jax.sharding import PartitionSpec as P


HD = 128
STEPS = 4
ROPE_BASE = 500000.0
NORM_EPS = 1e-05
SCORE_SCALE = math.log2(math.e) / math.sqrt(HD)

F32 = jnp.float32
BF16 = jnp.bfloat16


def call(body, grid, in_specs, out_specs, out_shape, scratch=(), flops=0, moved=0, exps=0):
    return pl.pallas_call(
        body,
        grid=grid,
        in_specs=in_specs,
        out_specs=out_specs,
        out_shape=out_shape,
        scratch_shapes=list(scratch),
        cost_estimate=pl.CostEstimate(flops=flops, bytes_accessed=moved, transcendentals=exps),
    )


def whole(shape):
    return pl.BlockSpec(shape, lambda *_: (0,) * len(shape))


def tables(positions):
    half = HD // 2
    exponent = jnp.arange(half, dtype=F32) * (2.0 / HD)
    inv_freq = ROPE_BASE ** (-exponent)
    angles = positions.astype(F32)[:, None] * inv_freq[None, :]
    cosine, sine = jnp.cos(angles), jnp.sin(angles)
    return jnp.concatenate([cosine, cosine], 1), jnp.concatenate([-sine, sine], 1)


def rope(u, cosine, sine):
    return u * cosine + pltpu.roll(u, HD // 2, 1) * sine


def pack_kv_body(k_ref, v_ref, cos_ref, sin_ref, out_ref):
    cosine, sine = cos_ref[...], sin_ref[...]
    width = out_ref.shape[3]
    for dest in range(out_ref.shape[0]):
        for lane in range(0, width, HD):
            column = dest * width + lane
            out_ref[dest, 0, :, lane : lane + HD] = rope(
                k_ref[:, column : column + HD].astype(F32), cosine, sine
            ).astype(BF16)
        out_ref[dest, 1] = v_ref[:, dest * width : (dest + 1) * width]


def pack_q_body(q_ref, cos_ref, sin_ref, out_ref):
    cosine, sine = cos_ref[...] * SCORE_SCALE, sin_ref[...] * SCORE_SCALE
    width = out_ref.shape[2]
    for dest in range(out_ref.shape[0]):
        for lane in range(0, width, HD):
            column = dest * width + lane
            out_ref[dest, :, lane : lane + HD] = rope(
                q_ref[:, column : column + HD].astype(F32), cosine, sine
            ).astype(BF16)


def normed(rows, gain):
    rows = rows.astype(F32)
    return (
        rows * lax.rsqrt(jnp.mean(rows * rows, axis=-1, keepdims=True) + NORM_EPS) * gain.astype(F32)
    ).astype(BF16)


def project_body(
    embed_ref, mask_ref, gain_ref, wq_ref, wk_ref, wv_ref, cos_ref, sin_ref,
    qe_ref, qm_ref, ke_ref, km_ref, ve_ref, vm_ref, mq, mk,
):
    gain = gain_ref[...]

    @pl.when(pl.program_id(0) == 0)
    def _():
        mask_row = normed(jnp.broadcast_to(mask_ref[...], (16, mask_ref.shape[1])), gain)
        mq[...] = jnp.dot(mask_row, wq_ref[...], preferred_element_type=F32)
        mk[...] = jnp.dot(mask_row, wk_ref[...], preferred_element_type=F32)
        vm_ref[...] = jnp.dot(mask_row, wv_ref[...], preferred_element_type=F32).astype(BF16)

    rows = normed(embed_ref[...], gain)
    count = rows.shape[0]
    q = jnp.dot(rows, wq_ref[...], preferred_element_type=F32)
    k = jnp.dot(rows, wk_ref[...], preferred_element_type=F32)
    ve_ref[...] = jnp.dot(rows, wv_ref[...], preferred_element_type=F32).astype(BF16)
    cosine, sine = cos_ref[...], sin_ref[...]
    for lane in range(0, q.shape[1], HD):
        at = slice(lane, lane + HD)
        qe_ref[:, at] = (rope(q[:, at], cosine, sine) * SCORE_SCALE).astype(BF16)
        ke_ref[:, at] = rope(k[:, at], cosine, sine).astype(BF16)
        one_q = jnp.broadcast_to(mq[0:1, at], (count, HD))
        one_k = jnp.broadcast_to(mk[0:1, at], (count, HD))
        qm_ref[:, at] = (rope(one_q, cosine, sine) * SCORE_SCALE).astype(BF16)
        km_ref[:, at] = rope(one_k, cosine, sine).astype(BF16)


def scores(q, k):
    return lax.dot_general(q, k, (((1,), (1,)), ((), ())), preferred_element_type=F32)


def merge(state, s, v):
    top = jnp.max(s, axis=-1, keepdims=True)
    if state is None:
        w = jnp.exp2(s - top)
        return (
            top,
            jnp.sum(w, axis=-1, keepdims=True),
            jnp.dot(w.astype(BF16), v, preferred_element_type=F32),
        )
    old, total, acc = state
    top = jnp.maximum(old, top)
    keep = jnp.exp2(old - top)
    w = jnp.exp2(s - top)
    total = total * keep + jnp.sum(w, axis=-1, keepdims=True)
    acc = acc * keep + jnp.dot(w.astype(BF16), v, preferred_element_type=F32)
    return top, total, acc


def over_prompt(state, q, kv_ref, chunk):
    sources, _, rows, width = kv_ref.shape
    for first in range(0, sources, chunk):
        k = kv_ref[first : first + chunk, 0].reshape(chunk * rows, width)
        v = kv_ref[first : first + chunk, 1].reshape(chunk * rows, width)
        state = merge(state, scores(q, k), v)
    return state


def early_body(qe_ref, qm_ref, ke_ref, km_ref, ve_ref, vm_ref, commit_ref, acc_ref, stats_ref):
    mask_value = jnp.broadcast_to(vm_ref[0:1], ve_ref.shape)
    lane = lax.broadcasted_iota(jnp.int32, stats_ref.shape, 1)
    stats = jnp.zeros(stats_ref.shape, F32)
    for step in range(acc_ref.shape[0]):
        shown = commit_ref[...] <= step
        q = jnp.where(shown, qe_ref[...], qm_ref[...])
        k = jnp.where(shown, ke_ref[...], km_ref[...])
        v = jnp.where(shown, ve_ref[...], mask_value)
        top, total, acc = merge(None, scores(q, k), v)
        acc_ref[step] = acc
        stats = jnp.where(lane == step, top, stats)
        stats = jnp.where(lane == STEPS + step, total, stats)
    stats_ref[...] = stats


def response_body(chunk, place_ref, kv_ref, qe_ref, qm_ref, acc_ref, stats_ref, commit_ref, *refs):
    out_refs, scratch_ref = refs[:-1], refs[-1]
    lows = len(out_refs)
    steps, blocks, per, _ = out_refs[0].shape
    low = place_ref[0]
    span_rows = lows * per
    count = blocks * span_rows

    def flat(value):
        return value.reshape(count, HD)

    revealed, stats = flat(commit_ref[...]), flat(stats_ref[...])
    both = over_prompt(None, jnp.concatenate([flat(qm_ref[...]), flat(qe_ref[...])], 0), kv_ref, chunk)
    for step in range(steps):
        shown = revealed <= step
        one = revealed[:, 0:1] <= step
        top_p = jnp.where(one, both[0][count:], both[0][:count])
        total_p = jnp.where(one, both[1][count:], both[1][:count])
        acc_p = jnp.where(shown, both[2][count:], both[2][:count])
        top_r, total_r = stats[:, step : step + 1], stats[:, STEPS + step : STEPS + step + 1]
        top = jnp.maximum(top_p, top_r)
        keep_p, keep_r = jnp.exp2(top_p - top), jnp.exp2(top_r - top)
        scale = 1.0 / (total_p * keep_p + total_r * keep_r)
        scratch_ref[step] = acc_p * (keep_p * scale) + flat(acc_ref[step]) * (keep_r * scale)
    for step in range(steps):
        for block in range(blocks):
            for k in range(lows):
                at = block * span_rows + (low ^ k) * per
                out_refs[k][step, block] = scratch_ref[step, pl.ds(pl.multiple_of(at, per), per), :].astype(BF16)


def prompt_body(chunk, q_ref, kv_ref, km_ref, vm_ref, *refs):
    sources, rows, width = q_ref.shape
    q = q_ref[...].reshape(sources * rows, width)
    s = scores(q, km_ref[...])
    top = jnp.max(s, axis=-1, keepdims=True)
    total = jnp.sum(jnp.exp2(s - top), axis=-1, keepdims=True)
    state = over_prompt((top, total, total * vm_ref[0:1].astype(F32)), q, kv_ref, chunk)
    refs[-1][...] = (state[2] / state[1]).astype(BF16).reshape(sources, rows, width)


def output_body(lows, split, place_ref, *refs):
    x_refs, refs = refs[:lows], refs[lows:]
    outs = refs[-STEPS:]
    steps, blocks, per, width = x_refs[0].shape
    far = lows // 2 if split else lows
    w = jnp.concatenate([ref[...] for ref in refs[:-STEPS]], 0)
    xs = []
    for k, x_ref in enumerate(x_refs):
        x = x_ref[...].reshape(steps * blocks * per, width)
        if k >= far:
            swapped = jnp.concatenate([x[:, width // 2 :], x[:, : width // 2]], 1)
            x = jnp.where(place_ref[2] == 0, x, swapped)
        xs.append(x)
    total = jnp.dot(jnp.concatenate(xs, 1), w, preferred_element_type=F32)
    for step, out_ref in enumerate(outs):
        for block in range(blocks):
            at = (step * blocks + block) * per
            out_ref[block] = total[at : at + per].astype(out_ref.dtype)


def halve_body(place_ref, keep_ref, got_ref, send_ref, kept_ref):
    bit = place_ref[0]
    for pair in range(send_ref.shape[0]):
        first = keep_ref[2 * pair].astype(F32) + got_ref[2 * pair].astype(F32)
        second = keep_ref[2 * pair + 1].astype(F32) + got_ref[2 * pair + 1].astype(F32)
        kept_ref[pair] = jnp.where(bit == 0, first, second)
        send_ref[pair] = jnp.where(bit == 0, second, first).astype(BF16)


def finish_body(step, embed_ref, mask_ref, gain_ref, commit_ref, keep_ref, got_ref, *refs):
    residual_ref, normed_ref = refs[-2:]
    shown = commit_ref[:, 0:1] <= step
    rows = jnp.where(shown, embed_ref[...].astype(F32), mask_ref[...].astype(F32))
    hidden = rows + (keep_ref[0] + got_ref[0].astype(F32))
    residual_ref[0] = hidden.astype(BF16)
    scale = lax.rsqrt(jnp.mean(hidden * hidden, axis=-1, keepdims=True) + NORM_EPS)
    normed_ref[0] = (hidden * scale * gain_ref[...].astype(F32)).astype(BF16)


def unpack_body(in_ref, out_ref):
    width = in_ref.shape[2]
    for source in range(in_ref.shape[0]):
        out_ref[:, source * width : (source + 1) * width] = in_ref[source]


def per_device(
    prompt_query,
    prompt_key,
    prompt_value,
    response_embed,
    mask_embed,
    commit_step,
    block_index,
    attention_gain,
    residual_gain,
    query_weight,
    key_weight,
    value_weight,
    output_weight,
):
    rows, head_cols = prompt_query.shape
    resp, model = response_embed.shape
    n = lax.axis_size("seq")
    me = lax.axis_index("seq")
    width = query_weight.shape[1]
    heads = width // HD
    prompt_len = rows * n
    lows = min(4, n)
    highs = n // lows
    per = resp // n

    def swap(x, bit):
        return lax.ppermute(x, "seq", [(i, i ^ bit) for i in range(n)])

    dests = max(1, n // 4)
    cos_p, sin_p = tables(me * rows + jnp.arange(rows, dtype=jnp.int32))
    kv_send = call(
        pack_kv_body,
        (n // dests,),
        [
            pl.BlockSpec((rows, dests * width), lambda j: (0, j)),
            pl.BlockSpec((rows, dests * width), lambda j: (0, j)),
            whole((rows, HD)),
            whole((rows, HD)),
        ],
        pl.BlockSpec((dests, 2, rows, width), lambda j: (j, 0, 0, 0)),
        jax.ShapeDtypeStruct((n, 2, rows, width), BF16),
        flops=6 * rows * head_cols,
        moved=8 * rows * head_cols,
    )(prompt_key, prompt_value, cos_p, sin_p)
    kv = lax.all_to_all(kv_send, "seq", 0, 0, tiled=True)
    q_send = call(
        pack_q_body,
        (n // dests,),
        [
            pl.BlockSpec((rows, dests * width), lambda j: (0, j)),
            whole((rows, HD)),
            whole((rows, HD)),
        ],
        pl.BlockSpec((dests, rows, width), lambda j: (j, 0, 0)),
        jax.ShapeDtypeStruct((n, rows, width), BF16),
        flops=6 * rows * head_cols,
        moved=4 * rows * head_cols,
    )(prompt_query, cos_p, sin_p)
    q_heads = lax.all_to_all(q_send, "seq", 0, 0, tiled=True)

    groups = lax.axis_size("groups")
    group = lax.axis_index("groups")
    split = lows == 4 and groups % 2 == 0
    weights = [output_weight, swap(output_weight, 1)]
    if split:
        half_rows = lax.dynamic_slice_in_dim(output_weight, (group & 1) * (width // 2), width // 2, 0)
        fetched = swap(half_rows, 2)
        given = lax.ppermute(fetched, "groups", [(i, i ^ 1) for i in range(groups)])
        last = swap(fetched, 1)
        weights += [fetched, given, last, swap(given, 1)]
    elif lows == 4:
        far = swap(output_weight, 2)
        weights += [far, swap(far, 1)]

    cos_r, sin_r = tables(prompt_len + block_index[0] * resp + jnp.arange(resp, dtype=jnp.int32))
    commit = jnp.broadcast_to(commit_step[:, None], (resp, HD))
    commit = lax.optimization_barrier(commit)
    block = min(resp, 128)
    row_block = pl.BlockSpec((block, width), lambda i: (i, 0))
    wide = jax.ShapeDtypeStruct((resp, width), BF16)
    qe, qm, ke, km, ve, vm = call(
        project_body,
        (resp // block,),
        [
            pl.BlockSpec((block, model), lambda i: (i, 0)),
            whole((1, model)),
            whole((1, model)),
            whole((model, width)),
            whole((model, width)),
            whole((model, width)),
            pl.BlockSpec((block, HD), lambda i: (i, 0)),
            pl.BlockSpec((block, HD), lambda i: (i, 0)),
        ],
        [row_block] * 5 + [whole((16, width))],
        [wide] * 5 + [jax.ShapeDtypeStruct((16, width), BF16)],
        scratch=[pltpu.VMEM((16, width), F32)] * 2,
        flops=6 * resp * model * width,
        moved=2 * resp * model + 6 * model * width,
    )(
        response_embed, mask_embed[None, :], attention_gain[None, :],
        query_weight, key_weight, value_weight, cos_r, sin_r,
    )

    chunk = max(1, min(n, 256 // rows))
    kv_block = pl.BlockSpec((n, 2, rows, HD), lambda h, *_: (0, 0, 0, h))
    key_block = pl.BlockSpec((resp, HD), lambda h, *_: (0, h))
    vm_block = pl.BlockSpec((16, HD), lambda h, *_: (0, h))
    low = me & (lows - 1)
    high = me >> (lows.bit_length() - 1)
    blocks = highs // 2
    place = jnp.stack([low, high & 1, group & 1]).astype(jnp.int32)
    early_acc, early_stats = call(
        early_body,
        (heads,),
        [key_block] * 5 + [vm_block, whole((resp, HD))],
        [pl.BlockSpec((STEPS, resp, HD), lambda h: (0, 0, h)), pl.BlockSpec((resp, HD), lambda h: (0, h))],
        [jax.ShapeDtypeStruct((STEPS, resp, width), F32), jax.ShapeDtypeStruct((resp, width), F32)],
        flops=4 * STEPS * resp * resp * width,
        moved=20 * resp * width,
        exps=heads * STEPS * resp * resp,
    )(qe, qm, ke, km, ve, vm, commit)

    def paired(array, *lead):
        return array.reshape(*lead, blocks, 2, lows * per, array.shape[-1])

    columns = min(model, 1024)
    projected = {}
    for kept in (False, True):
        side = (lambda at: at[1]) if kept else (lambda at: 1 - at[1])
        half_rows_of = pl.BlockSpec((blocks, None, lows * per, HD), lambda h, at, side=side: (0, side(at), 0, h))
        context = pl.pallas_call(
            functools.partial(response_body, 2 * chunk),
            grid_spec=pltpu.PrefetchScalarGridSpec(
                num_scalar_prefetch=1,
                grid=(heads,),
                in_specs=[
                    kv_block, half_rows_of, half_rows_of,
                    pl.BlockSpec(
                        (STEPS, blocks, None, lows * per, HD), lambda h, at, side=side: (0, 0, side(at), 0, h)
                    ),
                    half_rows_of,
                    pl.BlockSpec((blocks, None, lows * per, HD), lambda h, at, side=side: (0, side(at), 0, 0)),
                ],
                out_specs=[pl.BlockSpec((STEPS, blocks, per, HD), lambda h, *_: (0, 0, 0, h))] * lows,
                scratch_shapes=[pltpu.VMEM((STEPS, resp // 2, HD), F32)],
            ),
            out_shape=[jax.ShapeDtypeStruct((STEPS, blocks, per, width), BF16)] * lows,
            name="response_attention",
            cost_estimate=pl.CostEstimate(
                flops=4 * resp * width * prompt_len,
                bytes_accessed=4 * prompt_len * width,
                transcendentals=heads * resp * prompt_len,
            ),
        )(
            place, kv, paired(qe), paired(qm), paired(early_acc, STEPS), paired(early_stats), paired(commit)
        )
        plane_context = [context[0]]
        for k in range(1, lows):
            plane_context.append(swap(context[k], k))
        projected[kept] = pl.pallas_call(
            functools.partial(output_body, lows, split),
            grid_spec=pltpu.PrefetchScalarGridSpec(
                num_scalar_prefetch=1,
                grid=(model // columns,),
                in_specs=[whole((STEPS, blocks, per, width))] * lows
                + [pl.BlockSpec((w.shape[0], columns), lambda j, *_: (0, j)) for w in weights],
                out_specs=[pl.BlockSpec((blocks, per, columns), lambda j, *_: (0, 0, j))] * STEPS,
            ),
            out_shape=[jax.ShapeDtypeStruct((blocks, per, model), BF16)] * STEPS,
            name="output_projection",
            cost_estimate=pl.CostEstimate(
                flops=STEPS * resp * model * width, bytes_accessed=2 * lows * width * model, transcendentals=0
            ),
        )(place, *plane_context, *weights)
    sends, keeps = projected[False], projected[True]

    level = 0
    while True:
        gots = []
        for step in range(STEPS):
            gots.append(swap(sends[step], lows << level))
        count = keeps[0].shape[0]
        if count == 1:
            break
        level += 1
        bit = ((high >> level) & 1).astype(jnp.int32).reshape(1)
        sends, kept = [], []
        for step in range(STEPS):
            columns = model
            get = pl.BlockSpec((count, per, columns), lambda j, *_: (0, 0, j))
            put = pl.BlockSpec((count // 2, per, columns), lambda j, *_: (0, 0, j))
            one, two = pl.pallas_call(
                halve_body,
                grid_spec=pltpu.PrefetchScalarGridSpec(
                    num_scalar_prefetch=1,
                    grid=(model // columns,),
                    in_specs=[get, get],
                    out_specs=[put, put],
                ),
                out_shape=[
                    jax.ShapeDtypeStruct((count // 2, per, model), BF16),
                    jax.ShapeDtypeStruct((count // 2, per, model), F32),
                ],
                name="halve",
                cost_estimate=pl.CostEstimate(
                    flops=count * per * model, bytes_accessed=9 * count * per * model, transcendentals=0
                ),
            )(bit, keeps[step], gots[step])
            sends.append(one)
            kept.append(two)
        keeps = kept

    blocks_of_q = max(1, min(n, 1024 // rows))
    prompt_context = None
    for head in range(heads):
        of_head = functools.partial(lambda head, *_: (0, head), head)
        of_kv = functools.partial(lambda head, *_: (0, 0, 0, head), head)
        turns = n // blocks_of_q
        for turn in range(turns if head == 0 else 1):
            count = 1 if head == 0 else turns
            of_block = functools.partial(lambda head, turn, i: (turn + i, 0, head), head, turn)
            earlier = [] if prompt_context is None else [prompt_context]
            prompt_context = pl.pallas_call(
                functools.partial(prompt_body, chunk),
                grid=(count,),
                in_specs=[
                    pl.BlockSpec((blocks_of_q, rows, HD), of_block),
                    pl.BlockSpec((n, 2, rows, HD), of_kv),
                    pl.BlockSpec((resp, HD), of_head),
                    pl.BlockSpec((16, HD), of_head),
                ]
                + [pl.BlockSpec(memory_space=pl.ANY)] * len(earlier),
                out_specs=pl.BlockSpec((blocks_of_q, rows, HD), of_block),
                out_shape=jax.ShapeDtypeStruct((n, rows, width), BF16),
                name="prompt_attention",
                input_output_aliases={4: 0} if earlier else {},
                cost_estimate=pl.CostEstimate(
                    flops=4 * count * blocks_of_q * rows * HD * (prompt_len + resp),
                    bytes_accessed=4 * prompt_len * HD + 4 * count * blocks_of_q * rows * HD,
                    transcendentals=count * blocks_of_q * rows * (prompt_len + resp),
                ),
            )(q_heads, kv, km, vm, *earlier)
    back = lax.all_to_all(prompt_context, "seq", 0, 0, tiled=True)

    my_embed = lax.dynamic_slice_in_dim(response_embed, me * per, per, 0)
    my_commit = jnp.broadcast_to(lax.dynamic_slice_in_dim(commit_step, me * per, per, 0)[:, None], (per, HD))
    results = []
    for step in range(STEPS):
        at_step = functools.partial(lambda step, i: (step, 0, 0), step)
        results = pl.pallas_call(
            functools.partial(finish_body, step),
            grid=(1,),
            in_specs=[
                whole((per, model)), whole((1, model)), whole((1, model)), whole((per, HD)),
                whole((1, per, model)), whole((1, per, model)),
            ]
            + [pl.BlockSpec(memory_space=pl.ANY)] * len(results),
            out_specs=[pl.BlockSpec((1, per, model), at_step)] * 2,
            out_shape=[jax.ShapeDtypeStruct((STEPS, per, model), BF16)] * 2,
            name="finish",
            input_output_aliases={6: 0, 7: 1} if results else {},
            cost_estimate=pl.CostEstimate(flops=8 * per * model, bytes_accessed=12 * per * model, transcendentals=0),
        )(
            my_embed, mask_embed[None, :], residual_gain[None, :], my_commit,
            keeps[step], gots[step], *results,
        )
    residual, normed_rows = results
    columns = max(1, n // 4)
    prompt_out = call(
        unpack_body,
        (n // columns,),
        [pl.BlockSpec((columns, rows, width), lambda j: (j, 0, 0))],
        pl.BlockSpec((rows, columns * width), lambda j: (0, j)),
        jax.ShapeDtypeStruct((rows, head_cols), BF16),
        moved=4 * rows * head_cols,
    )(back)
    return prompt_out, residual, normed_rows


def solution(mesh):
    return jax.shard_map(
        per_device,
        mesh=mesh,
        in_specs=(
            P(("groups", "seq"), None),
            P(("groups", "seq"), None),
            P(("groups", "seq"), None),
            P("groups", None),
            P(),
            P("groups"),
            P("groups"),
            P(),
            P(),
            P(None, "seq"),
            P(None, "seq"),
            P(None, "seq"),
            P("seq", None),
        ),
        out_specs=(
            P(("groups", "seq"), None),
            P(None, ("groups", "seq"), None),
            P(None, ("groups", "seq"), None),
        ),
        check_vma=False,
    )
```

```python
import functools
import math

import jax
import jax.numpy as jnp
from jax import lax
from jax.experimental import pallas as pl
from jax.experimental.pallas import tpu as pltpu
from jax.sharding import PartitionSpec as P


HD = 128
STEPS = 4
ROPE_BASE = 500000.0
NORM_EPS = 1e-05
SCORE_SCALE = math.log2(math.e) / math.sqrt(HD)

F32 = jnp.float32
BF16 = jnp.bfloat16


def call(body, grid, in_specs, out_specs, out_shape, scratch=(), flops=0, moved=0, exps=0):
    return pl.pallas_call(
        body,
        grid=grid,
        in_specs=in_specs,
        out_specs=out_specs,
        out_shape=out_shape,
        scratch_shapes=list(scratch),
        cost_estimate=pl.CostEstimate(flops=flops, bytes_accessed=moved, transcendentals=exps),
    )


def whole(shape):
    return pl.BlockSpec(shape, lambda *_: (0,) * len(shape))


def tables(positions):
    half = HD // 2
    exponent = jnp.arange(half, dtype=F32) * (2.0 / HD)
    inv_freq = ROPE_BASE ** (-exponent)
    angles = positions.astype(F32)[:, None] * inv_freq[None, :]
    cosine, sine = jnp.cos(angles), jnp.sin(angles)
    return jnp.concatenate([cosine, cosine], 1), jnp.concatenate([-sine, sine], 1)


def rope(u, cosine, sine):
    return u * cosine + pltpu.roll(u, HD // 2, 1) * sine


def pack_kv_body(k_ref, v_ref, cos_ref, sin_ref, out_ref):
    cosine, sine = cos_ref[...], sin_ref[...]
    width = out_ref.shape[3]
    for dest in range(out_ref.shape[0]):
        for lane in range(0, width, HD):
            column = dest * width + lane
            out_ref[dest, 0, :, lane : lane + HD] = rope(
                k_ref[:, column : column + HD].astype(F32), cosine, sine
            ).astype(BF16)
        out_ref[dest, 1] = v_ref[:, dest * width : (dest + 1) * width]


def pack_q_body(q_ref, cos_ref, sin_ref, out_ref):
    cosine, sine = cos_ref[...] * SCORE_SCALE, sin_ref[...] * SCORE_SCALE
    width = out_ref.shape[2]
    for dest in range(out_ref.shape[0]):
        for lane in range(0, width, HD):
            column = dest * width + lane
            out_ref[dest, :, lane : lane + HD] = rope(
                q_ref[:, column : column + HD].astype(F32), cosine, sine
            ).astype(BF16)


def normed(rows, gain):
    rows = rows.astype(F32)
    return (
        rows * lax.rsqrt(jnp.mean(rows * rows, axis=-1, keepdims=True) + NORM_EPS) * gain.astype(F32)
    ).astype(BF16)


def project_body(
    embed_ref, mask_ref, gain_ref, wq_ref, wk_ref, wv_ref, cos_ref, sin_ref,
    qe_ref, qm_ref, ke_ref, km_ref, ve_ref, vm_ref, mq, mk,
):
    gain = gain_ref[...]

    @pl.when(pl.program_id(0) == 0)
    def _():
        mask_row = normed(jnp.broadcast_to(mask_ref[...], (16, mask_ref.shape[1])), gain)
        mq[...] = jnp.dot(mask_row, wq_ref[...], preferred_element_type=F32)
        mk[...] = jnp.dot(mask_row, wk_ref[...], preferred_element_type=F32)
        vm_ref[...] = jnp.dot(mask_row, wv_ref[...], preferred_element_type=F32).astype(BF16)

    rows = normed(embed_ref[...], gain)
    count = rows.shape[0]
    q = jnp.dot(rows, wq_ref[...], preferred_element_type=F32)
    k = jnp.dot(rows, wk_ref[...], preferred_element_type=F32)
    ve_ref[...] = jnp.dot(rows, wv_ref[...], preferred_element_type=F32).astype(BF16)
    cosine, sine = cos_ref[...], sin_ref[...]
    for lane in range(0, q.shape[1], HD):
        at = slice(lane, lane + HD)
        qe_ref[:, at] = (rope(q[:, at], cosine, sine) * SCORE_SCALE).astype(BF16)
        ke_ref[:, at] = rope(k[:, at], cosine, sine).astype(BF16)
        one_q = jnp.broadcast_to(mq[0:1, at], (count, HD))
        one_k = jnp.broadcast_to(mk[0:1, at], (count, HD))
        qm_ref[:, at] = (rope(one_q, cosine, sine) * SCORE_SCALE).astype(BF16)
        km_ref[:, at] = rope(one_k, cosine, sine).astype(BF16)


def scores(q, k):
    return lax.dot_general(q, k, (((1,), (1,)), ((), ())), preferred_element_type=F32)


def merge(state, s, v):
    top = jnp.max(s, axis=-1, keepdims=True)
    if state is None:
        w = jnp.exp2(s - top)
        return (
            top,
            jnp.sum(w, axis=-1, keepdims=True),
            jnp.dot(w.astype(BF16), v, preferred_element_type=F32),
        )
    old, total, acc = state
    top = jnp.maximum(old, top)
    keep = jnp.exp2(old - top)
    w = jnp.exp2(s - top)
    total = total * keep + jnp.sum(w, axis=-1, keepdims=True)
    acc = acc * keep + jnp.dot(w.astype(BF16), v, preferred_element_type=F32)
    return top, total, acc


def over_prompt(state, q, kv_ref, chunk):
    sources, _, rows, width = kv_ref.shape
    for first in range(0, sources, chunk):
        k = kv_ref[first : first + chunk, 0].reshape(chunk * rows, width)
        v = kv_ref[first : first + chunk, 1].reshape(chunk * rows, width)
        state = merge(state, scores(q, k), v)
    return state


def early_body(qe_ref, qm_ref, ke_ref, km_ref, ve_ref, vm_ref, commit_ref, acc_ref, stats_ref):
    mask_value = jnp.broadcast_to(vm_ref[0:1], ve_ref.shape)
    lane = lax.broadcasted_iota(jnp.int32, stats_ref.shape, 1)
    stats = jnp.zeros(stats_ref.shape, F32)
    for step in range(acc_ref.shape[0]):
        shown = commit_ref[...] <= step
        q = jnp.where(shown, qe_ref[...], qm_ref[...])
        k = jnp.where(shown, ke_ref[...], km_ref[...])
        v = jnp.where(shown, ve_ref[...], mask_value)
        top, total, acc = merge(None, scores(q, k), v)
        acc_ref[step] = acc * (1.0 / total)
        stats = jnp.where(lane == step, top + jnp.log2(total), stats)
    stats_ref[...] = stats


def response_body(chunk, place_ref, kv_ref, qe_ref, qm_ref, acc_ref, stats_ref, commit_ref, *refs):
    out_refs, scratch_ref = refs[:-1], refs[-1]
    lows = len(out_refs)
    steps, blocks, per, _ = out_refs[0].shape
    low = place_ref[0]
    span_rows = lows * per
    count = blocks * span_rows

    def flat(value):
        return value.reshape(count, HD)

    revealed, stats = flat(commit_ref[...]), flat(stats_ref[...])
    both = over_prompt(None, jnp.concatenate([flat(qm_ref[...]), flat(qe_ref[...])], 0), kv_ref, chunk)
    log_p = both[0] + jnp.log2(both[1])
    mean_p = both[2] * (1.0 / both[1])
    for step in range(steps):
        one = revealed[:, 0:1] <= step
        from_prompt = jnp.where(revealed <= step, mean_p[count:], mean_p[:count])
        gap = jnp.where(one, log_p[count:], log_p[:count]) - stats[:, step : step + 1]
        share = 1.0 / (1.0 + jnp.exp2(gap))
        scratch_ref[step] = from_prompt + share * (flat(acc_ref[step]) - from_prompt)
    for step in range(steps):
        for block in range(blocks):
            for k in range(lows):
                at = block * span_rows + (low ^ k) * per
                out_refs[k][step, block] = scratch_ref[step, pl.ds(pl.multiple_of(at, per), per), :].astype(BF16)


def prompt_body(chunk, q_ref, kv_ref, km_ref, vm_ref, *refs):
    sources, rows, width = q_ref.shape
    q = q_ref[...].reshape(sources * rows, width)
    s = scores(q, km_ref[...])
    top = jnp.max(s, axis=-1, keepdims=True)
    total = jnp.sum(jnp.exp2(s - top), axis=-1, keepdims=True)
    state = over_prompt((top, total, total * vm_ref[0:1].astype(F32)), q, kv_ref, chunk)
    refs[-1][...] = (state[2] / state[1]).astype(BF16).reshape(sources, rows, width)


def output_body(lows, split, place_ref, *refs):
    x_refs, refs = refs[:lows], refs[lows:]
    outs = refs[-STEPS:]
    steps, blocks, per, width = x_refs[0].shape
    far = lows // 2 if split else lows
    w = jnp.concatenate([ref[...] for ref in refs[:-STEPS]], 0)
    xs = []
    for k, x_ref in enumerate(x_refs):
        x = x_ref[...].reshape(steps * blocks * per, width)
        if k >= far:
            swapped = jnp.concatenate([x[:, width // 2 :], x[:, : width // 2]], 1)
            x = jnp.where(place_ref[2] == 0, x, swapped)
        xs.append(x)
    total = jnp.dot(jnp.concatenate(xs, 1), w, preferred_element_type=F32)
    for step, out_ref in enumerate(outs):
        for block in range(blocks):
            at = (step * blocks + block) * per
            out_ref[block] = total[at : at + per].astype(out_ref.dtype)


def halve_body(place_ref, keep_ref, got_ref, send_ref, kept_ref):
    bit = place_ref[0]
    for pair in range(send_ref.shape[0]):
        first = keep_ref[2 * pair].astype(F32) + got_ref[2 * pair].astype(F32)
        second = keep_ref[2 * pair + 1].astype(F32) + got_ref[2 * pair + 1].astype(F32)
        kept_ref[pair] = jnp.where(bit == 0, first, second)
        send_ref[pair] = jnp.where(bit == 0, second, first).astype(BF16)


def finish_body(step, embed_ref, mask_ref, gain_ref, commit_ref, keep_ref, got_ref, *refs):
    residual_ref, normed_ref = refs[-2:]
    shown = commit_ref[:, 0:1] <= step
    rows = jnp.where(shown, embed_ref[...].astype(F32), mask_ref[...].astype(F32))
    hidden = rows + (keep_ref[0] + got_ref[0].astype(F32))
    residual_ref[0] = hidden.astype(BF16)
    scale = lax.rsqrt(jnp.mean(hidden * hidden, axis=-1, keepdims=True) + NORM_EPS)
    normed_ref[0] = (hidden * scale * gain_ref[...].astype(F32)).astype(BF16)


def unpack_body(in_ref, out_ref):
    width = in_ref.shape[2]
    for source in range(in_ref.shape[0]):
        out_ref[:, source * width : (source + 1) * width] = in_ref[source]


def per_device(
    prompt_query,
    prompt_key,
    prompt_value,
    response_embed,
    mask_embed,
    commit_step,
    block_index,
    attention_gain,
    residual_gain,
    query_weight,
    key_weight,
    value_weight,
    output_weight,
):
    rows, head_cols = prompt_query.shape
    resp, model = response_embed.shape
    n = lax.axis_size("seq")
    me = lax.axis_index("seq")
    width = query_weight.shape[1]
    heads = width // HD
    prompt_len = rows * n
    lows = min(4, n)
    highs = n // lows
    per = resp // n

    def swap(x, bit):
        return lax.ppermute(x, "seq", [(i, i ^ bit) for i in range(n)])

    dests = max(1, n // 4)
    cos_p, sin_p = tables(me * rows + jnp.arange(rows, dtype=jnp.int32))
    kv_send = call(
        pack_kv_body,
        (n // dests,),
        [
            pl.BlockSpec((rows, dests * width), lambda j: (0, j)),
            pl.BlockSpec((rows, dests * width), lambda j: (0, j)),
            whole((rows, HD)),
            whole((rows, HD)),
        ],
        pl.BlockSpec((dests, 2, rows, width), lambda j: (j, 0, 0, 0)),
        jax.ShapeDtypeStruct((n, 2, rows, width), BF16),
        flops=6 * rows * head_cols,
        moved=8 * rows * head_cols,
    )(prompt_key, prompt_value, cos_p, sin_p)
    kv = lax.all_to_all(kv_send, "seq", 0, 0, tiled=True)
    q_send = call(
        pack_q_body,
        (n // dests,),
        [
            pl.BlockSpec((rows, dests * width), lambda j: (0, j)),
            whole((rows, HD)),
            whole((rows, HD)),
        ],
        pl.BlockSpec((dests, rows, width), lambda j: (j, 0, 0)),
        jax.ShapeDtypeStruct((n, rows, width), BF16),
        flops=6 * rows * head_cols,
        moved=4 * rows * head_cols,
    )(prompt_query, cos_p, sin_p)
    q_heads = lax.all_to_all(q_send, "seq", 0, 0, tiled=True)

    groups = lax.axis_size("groups")
    group = lax.axis_index("groups")
    split = lows == 4 and groups % 2 == 0
    weights = [output_weight, swap(output_weight, 1)]
    if split:
        half_rows = lax.dynamic_slice_in_dim(output_weight, (group & 1) * (width // 2), width // 2, 0)
        fetched = swap(half_rows, 2)
        given = lax.ppermute(fetched, "groups", [(i, i ^ 1) for i in range(groups)])
        last = swap(fetched, 1)
        weights += [fetched, given, last, swap(given, 1)]
    elif lows == 4:
        far = swap(output_weight, 2)
        weights += [far, swap(far, 1)]

    cos_r, sin_r = tables(prompt_len + block_index[0] * resp + jnp.arange(resp, dtype=jnp.int32))
    commit = jnp.broadcast_to(commit_step[:, None], (resp, HD))
    commit = lax.optimization_barrier(commit)
    block = min(resp, 128)
    row_block = pl.BlockSpec((block, width), lambda i: (i, 0))
    wide = jax.ShapeDtypeStruct((resp, width), BF16)
    qe, qm, ke, km, ve, vm = call(
        project_body,
        (resp // block,),
        [
            pl.BlockSpec((block, model), lambda i: (i, 0)),
            whole((1, model)),
            whole((1, model)),
            whole((model, width)),
            whole((model, width)),
            whole((model, width)),
            pl.BlockSpec((block, HD), lambda i: (i, 0)),
            pl.BlockSpec((block, HD), lambda i: (i, 0)),
        ],
        [row_block] * 5 + [whole((16, width))],
        [wide] * 5 + [jax.ShapeDtypeStruct((16, width), BF16)],
        scratch=[pltpu.VMEM((16, width), F32)] * 2,
        flops=6 * resp * model * width,
        moved=2 * resp * model + 6 * model * width,
    )(
        response_embed, mask_embed[None, :], attention_gain[None, :],
        query_weight, key_weight, value_weight, cos_r, sin_r,
    )

    chunk = max(1, min(n, 256 // rows))
    kv_block = pl.BlockSpec((n, 2, rows, HD), lambda h, *_: (0, 0, 0, h))
    key_block = pl.BlockSpec((resp, HD), lambda h, *_: (0, h))
    vm_block = pl.BlockSpec((16, HD), lambda h, *_: (0, h))
    low = me & (lows - 1)
    high = me >> (lows.bit_length() - 1)
    blocks = highs // 2
    place = jnp.stack([low, high & 1, group & 1]).astype(jnp.int32)
    early_acc, early_stats = call(
        early_body,
        (heads,),
        [key_block] * 5 + [vm_block, whole((resp, HD))],
        [pl.BlockSpec((STEPS, resp, HD), lambda h: (0, 0, h)), pl.BlockSpec((resp, HD), lambda h: (0, h))],
        [jax.ShapeDtypeStruct((STEPS, resp, width), F32), jax.ShapeDtypeStruct((resp, width), F32)],
        flops=4 * STEPS * resp * resp * width,
        moved=20 * resp * width,
        exps=heads * STEPS * resp * resp,
    )(qe, qm, ke, km, ve, vm, commit)

    def paired(array, *lead):
        return array.reshape(*lead, blocks, 2, lows * per, array.shape[-1])

    columns = min(model, 1024)
    projected = {}
    for kept in (False, True):
        side = (lambda at: at[1]) if kept else (lambda at: 1 - at[1])
        half_rows_of = pl.BlockSpec((blocks, None, lows * per, HD), lambda h, at, side=side: (0, side(at), 0, h))
        context = pl.pallas_call(
            functools.partial(response_body, 2 * chunk),
            grid_spec=pltpu.PrefetchScalarGridSpec(
                num_scalar_prefetch=1,
                grid=(heads,),
                in_specs=[
                    kv_block, half_rows_of, half_rows_of,
                    pl.BlockSpec(
                        (STEPS, blocks, None, lows * per, HD), lambda h, at, side=side: (0, 0, side(at), 0, h)
                    ),
                    half_rows_of,
                    pl.BlockSpec((blocks, None, lows * per, HD), lambda h, at, side=side: (0, side(at), 0, 0)),
                ],
                out_specs=[pl.BlockSpec((STEPS, blocks, per, HD), lambda h, *_: (0, 0, 0, h))] * lows,
                scratch_shapes=[pltpu.VMEM((STEPS, resp // 2, HD), F32)],
            ),
            out_shape=[jax.ShapeDtypeStruct((STEPS, blocks, per, width), BF16)] * lows,
            name="response_attention",
            cost_estimate=pl.CostEstimate(
                flops=4 * resp * width * prompt_len,
                bytes_accessed=4 * prompt_len * width,
                transcendentals=heads * resp * prompt_len,
            ),
        )(
            place, kv, paired(qe), paired(qm), paired(early_acc, STEPS), paired(early_stats), paired(commit)
        )
        plane_context = [context[0]]
        for k in range(1, lows):
            plane_context.append(swap(context[k], k))
        projected[kept] = pl.pallas_call(
            functools.partial(output_body, lows, split),
            grid_spec=pltpu.PrefetchScalarGridSpec(
                num_scalar_prefetch=1,
                grid=(model // columns,),
                in_specs=[whole((STEPS, blocks, per, width))] * lows
                + [pl.BlockSpec((w.shape[0], columns), lambda j, *_: (0, j)) for w in weights],
                out_specs=[pl.BlockSpec((blocks, per, columns), lambda j, *_: (0, 0, j))] * STEPS,
            ),
            out_shape=[jax.ShapeDtypeStruct((blocks, per, model), BF16)] * STEPS,
            name="output_projection",
            cost_estimate=pl.CostEstimate(
                flops=STEPS * resp * model * width, bytes_accessed=2 * lows * width * model, transcendentals=0
            ),
        )(place, *plane_context, *weights)
    sends, keeps = projected[False], projected[True]

    level = 0
    while True:
        gots = []
        for step in range(STEPS):
            gots.append(swap(sends[step], lows << level))
        count = keeps[0].shape[0]
        if count == 1:
            break
        level += 1
        bit = ((high >> level) & 1).astype(jnp.int32).reshape(1)
        sends, kept = [], []
        for step in range(STEPS):
            columns = model
            get = pl.BlockSpec((count, per, columns), lambda j, *_: (0, 0, j))
            put = pl.BlockSpec((count // 2, per, columns), lambda j, *_: (0, 0, j))
            one, two = pl.pallas_call(
                halve_body,
                grid_spec=pltpu.PrefetchScalarGridSpec(
                    num_scalar_prefetch=1,
                    grid=(model // columns,),
                    in_specs=[get, get],
                    out_specs=[put, put],
                ),
                out_shape=[
                    jax.ShapeDtypeStruct((count // 2, per, model), BF16),
                    jax.ShapeDtypeStruct((count // 2, per, model), F32),
                ],
                name="halve",
                cost_estimate=pl.CostEstimate(
                    flops=count * per * model, bytes_accessed=9 * count * per * model, transcendentals=0
                ),
            )(bit, keeps[step], gots[step])
            sends.append(one)
            kept.append(two)
        keeps = kept

    blocks_of_q = max(1, min(n, 1024 // rows))
    prompt_context = None
    for head in range(heads):
        of_head = functools.partial(lambda head, *_: (0, head), head)
        of_kv = functools.partial(lambda head, *_: (0, 0, 0, head), head)
        turns = n // blocks_of_q
        for turn in range(turns if head == 0 else 1):
            count = 1 if head == 0 else turns
            of_block = functools.partial(lambda head, turn, i: (turn + i, 0, head), head, turn)
            earlier = [] if prompt_context is None else [prompt_context]
            prompt_context = pl.pallas_call(
                functools.partial(prompt_body, chunk),
                grid=(count,),
                in_specs=[
                    pl.BlockSpec((blocks_of_q, rows, HD), of_block),
                    pl.BlockSpec((n, 2, rows, HD), of_kv),
                    pl.BlockSpec((resp, HD), of_head),
                    pl.BlockSpec((16, HD), of_head),
                ]
                + [pl.BlockSpec(memory_space=pl.ANY)] * len(earlier),
                out_specs=pl.BlockSpec((blocks_of_q, rows, HD), of_block),
                out_shape=jax.ShapeDtypeStruct((n, rows, width), BF16),
                name="prompt_attention",
                input_output_aliases={4: 0} if earlier else {},
                cost_estimate=pl.CostEstimate(
                    flops=4 * count * blocks_of_q * rows * HD * (prompt_len + resp),
                    bytes_accessed=4 * prompt_len * HD + 4 * count * blocks_of_q * rows * HD,
                    transcendentals=count * blocks_of_q * rows * (prompt_len + resp),
                ),
            )(q_heads, kv, km, vm, *earlier)
    back = lax.all_to_all(prompt_context, "seq", 0, 0, tiled=True)

    my_embed = lax.dynamic_slice_in_dim(response_embed, me * per, per, 0)
    my_commit = jnp.broadcast_to(lax.dynamic_slice_in_dim(commit_step, me * per, per, 0)[:, None], (per, HD))
    results = []
    for step in range(STEPS):
        at_step = functools.partial(lambda step, i: (step, 0, 0), step)
        results = pl.pallas_call(
            functools.partial(finish_body, step),
            grid=(1,),
            in_specs=[
                whole((per, model)), whole((1, model)), whole((1, model)), whole((per, HD)),
                whole((1, per, model)), whole((1, per, model)),
            ]
            + [pl.BlockSpec(memory_space=pl.ANY)] * len(results),
            out_specs=[pl.BlockSpec((1, per, model), at_step)] * 2,
            out_shape=[jax.ShapeDtypeStruct((STEPS, per, model), BF16)] * 2,
            name="finish",
            input_output_aliases={6: 0, 7: 1} if results else {},
            cost_estimate=pl.CostEstimate(flops=8 * per * model, bytes_accessed=12 * per * model, transcendentals=0),
        )(
            my_embed, mask_embed[None, :], residual_gain[None, :], my_commit,
            keeps[step], gots[step], *results,
        )
    residual, normed_rows = results
    columns = max(1, n // 4)
    prompt_out = call(
        unpack_body,
        (n // columns,),
        [pl.BlockSpec((columns, rows, width), lambda j: (j, 0, 0))],
        pl.BlockSpec((rows, columns * width), lambda j: (0, j)),
        jax.ShapeDtypeStruct((rows, head_cols), BF16),
        moved=4 * rows * head_cols,
    )(back)
    return prompt_out, residual, normed_rows


def solution(mesh):
    return jax.shard_map(
        per_device,
        mesh=mesh,
        in_specs=(
            P(("groups", "seq"), None),
            P(("groups", "seq"), None),
            P(("groups", "seq"), None),
            P("groups", None),
            P(),
            P("groups"),
            P("groups"),
            P(),
            P(),
            P(None, "seq"),
            P(None, "seq"),
            P(None, "seq"),
            P("seq", None),
        ),
        out_specs=(
            P(("groups", "seq"), None),
            P(None, ("groups", "seq"), None),
            P(None, ("groups", "seq"), None),
        ),
        check_vma=False,
    )
```
